32 devices in a mesh: dp: 8 (over z, y), phase: 2 (over core), mp: 2 (over x).
Axes of the slice: x: 2, y: 2, z: 4, core: 2. Of those that a mesh axis runs over, the one named last changes fastest.
Arguments:
- sec_acts: bfloat16 [2, 8, 512, 4096], P('phase', 'dp', None, 'mp'), may hold values from -40 to 40
- gain: bfloat16 [4096], P('mp'), may hold values from 0.5 to 1.5
- w_kv: bfloat16 [4096, 4096], P(('dp', 'phase'), 'mp'), may hold values from -0.09375 to 0.09375
- src_len: int32 [8], P('dp'), may hold values from 1 to 512, 2560 in all
- tgt_len: int32 [8], P('dp'), may hold values from 1 to 512, 3072 in all
Outputs:
- sec_grads: bfloat16 [2, 8, 512, 4096], P('phase', 'dp', None, 'mp')
- d_wkv: float32 [4096, 4096], P(('dp', 'phase'), 'mp')
- d_gain: float32 [4096], P('mp')
The draws below stay inside these ranges and needn't reach their ends.
Inputs may be any that keep to these rules, and one draw needn't show every extreme that they name: Source positions 0 to src_len - 1 of a pair are real, the rest padding; some pair has exactly 512. Target positions 0 to tgt_len - 1 of a pair carry loss, the rest padding; some pair has exactly 512.
All inputs are finite; a program needn't handle non-finite values. No bound on the sum of `src_len` or of `tgt_len` on one device may be relied on, other than what follows from the above.
Results may differ from the reference program's by a relative error of at most 0.022.
Values may be sent and summed in bfloat16 or wider, within the bound.
No kernel may reach another device: no remote copies, remote signals or barrier semaphores. Data moves between devices by JAX's collectives and lax.ppermute only.
A program may use at most 128 MiB of HBM per device.

```python
import math
import jax
import jax.numpy as jnp
import numpy as np
from jax import lax

D = 4096
HEADS = 32
HEAD = 64
LEN = 512
PAIR_DEV = 1
PAIRS = 8
N_DP = 8
N_MP = 2


def draw_sec_acts(key, part):
    key_base = jax.random.fold_in(key, 0)
    key_cols = jax.random.fold_in(key, 2)
    shape = (2, PAIRS, LEN, D)
    section = jnp.arange(2).reshape(2, 1, 1, 1)
    place = jnp.arange(D, dtype=jnp.float32) / (D - 1)
    rough = jnp.exp(jax.random.uniform(key_cols, (D,), jnp.float32, minval=0.0, maxval=math.log(2.0)))
    rise = jnp.exp(math.log(6.0) * place) * rough / 2.0
    base = jnp.clip(jax.random.normal(key_base, shape, jnp.float32), -6.0, 6.0)
    return (base * jnp.where(section == 0, rise, 1.0)).astype(jnp.bfloat16)


def steps_of(stream_key, extent, cuts, smallest, top_value):
    loudness = 1.0
    for axis_at, shards_of in cuts:
        draws = jax.random.uniform(jax.random.fold_in(jax.random.fold_in(stream_key, 6), axis_at), (shards_of,), jnp.float32, smallest / len(cuts), top_value / len(cuts))
        loudness = loudness * jnp.repeat(jnp.exp(draws), extent[axis_at] // shards_of).reshape((-1,) + (1,) * (len(extent) - 1 - axis_at))
    return loudness


def split_up(amount, total, reach, lean):
    weights = [(1 << 20) // math.isqrt(grade ** lean) + 1 for grade in range(2, amount + 1)]
    surplus, given = total - reach - (amount - 1), [1] * (amount - 1)
    while surplus > 0:
        candidates = [i for i in range(amount - 1) if given[i] < reach]
        mass, budget = sum([weights[i] for i in candidates]), surplus
        for i in candidates:
            more = min(reach - given[i], max(1, budget * weights[i] // mass), surplus)
            given[i] = given[i] + more
            surplus = surplus - more
    return np.array([reach] + given)


def ragged(key, amount, total, bound, slope):
    if amount == 2:
        one = jax.random.randint(key, (), max(1, total - bound), min(bound, total - 1) + 1)
        return jnp.stack([one, total - one])
    tallies = jnp.asarray(split_up(amount, total, bound, slope), jnp.int32)
    pairs = (amount - 1) // 2
    source_of, sink = tallies[1:1 + 2 * pairs:2], tallies[2:2 + 2 * pairs:2]
    margin = jnp.minimum(source_of - 1, bound - sink)
    passed = jax.random.randint(jax.random.fold_in(key, 1), (pairs,), 0, 1 << 20) % (margin + 1)
    tallies = tallies.at[1:1 + 2 * pairs:2].set(source_of - passed).at[2:2 + 2 * pairs:2].set(sink + passed)
    return tallies[jax.random.permutation(jax.random.fold_in(key, 2), amount)]


def normal_values(rng, extent, spread, limit, cuts=(), held_as=jnp.bfloat16):
    entries = jax.random.normal(rng, extent, jnp.float32) * spread
    if len(cuts) > 0:
        entries = steps_of(rng, extent, cuts, -0.22, 0.18) * entries
    return jnp.clip(entries, min=-limit, max=limit).astype(held_as)


def setup_inputs(seed: int = 0) -> dict:
    splits = jax.random.split(jax.random.key(seed), 6)
    sec_acts = draw_sec_acts(jax.random.fold_in(splits[5], 71), 0)
    gain = jnp.clip(1.0 + 0.1 * jax.random.normal(splits[1], (D,), jnp.float32), 0.5, 1.5).astype(jnp.bfloat16)
    w_kv = normal_values(splits[2], (D, D), D ** -0.5, 0.09375, ((0, 16), (1, 2)))
    src_len = ragged(splits[3], PAIRS, PAIRS * LEN * 5 // 8, LEN, 2).astype(jnp.int32)
    tgt_len = ragged(splits[4], PAIRS, PAIRS * LEN * 3 // 4, LEN, 2).astype(jnp.int32)
    return {"sec_acts": sec_acts, "gain": gain, "w_kv": w_kv, "src_len": src_len, "tgt_len": tgt_len}


norm_epsilon = 1e-06

def attend_back(queries, grad_out, key_heads, values, key_mask):
    f32 = jnp.float32
    factor = 1.0 / HEAD ** 0.5
    scores = factor * jnp.einsum('pihd,pjhd->phij', queries.astype(f32), key_heads.astype(f32))
    scores = jnp.where(key_mask[:, None, None, :], scores, -1e+30)
    row_top = lax.optimization_barrier(jnp.max(scores, axis=-1, keepdims=True))
    weights = jnp.exp(scores - row_top)
    probability = weights / lax.optimization_barrier(jnp.sum(weights, axis=-1, keepdims=True))
    prob_low = probability.astype(jnp.bfloat16)
    attended = jnp.einsum('phij,pjhd->pihd', prob_low.astype(f32), values.astype(f32))
    grad_prob = jnp.einsum('pihd,pjhd->phij', grad_out.astype(f32), values.astype(f32))
    row_delta = jnp.einsum('pihd,pihd->phi', grad_out.astype(f32), attended)
    grad_score = (factor * probability * (grad_prob - row_delta[..., None])).astype(jnp.bfloat16)
    grad_query = jnp.einsum('phij,pjhd->pihd', grad_score.astype(f32), key_heads.astype(f32)).astype(jnp.bfloat16)
    grad_key = jnp.einsum('phij,pihd->pjhd', grad_score.astype(f32), queries.astype(f32)).astype(jnp.bfloat16)
    grad_value = jnp.einsum('phij,pihd->pjhd', prob_low.astype(f32), grad_out.astype(f32)).astype(jnp.bfloat16)
    return (grad_query, grad_key, grad_value)

def reference(sec_acts, gain, w_kv, src_len, tgt_len):
    f32 = jnp.float32
    bf16 = jnp.bfloat16
    hidden = sec_acts[0].astype(f32)
    inv_rms = lax.rsqrt(lax.optimization_barrier(jnp.sum(hidden * hidden, axis=-1, keepdims=True)) / D + norm_epsilon)
    normed = hidden * inv_rms
    gain_wide = gain.astype(f32)
    encoded = (normed * gain_wide).astype(bf16)
    dec_split = sec_acts[1].reshape(PAIRS, LEN, HEADS, 2, HEAD)
    positions = jnp.arange(LEN, dtype=jnp.int32)
    query_mask = positions[None, :] < tgt_len[:, None]
    key_mask = positions[None, :] < src_len[:, None]
    queries = dec_split[:, :, :, 0]
    grad_out = jnp.where(query_mask[:, :, None, None], dec_split[:, :, :, 1], jnp.zeros((), bf16))

    def one_pair(items):
        enc_pair, query_pair, grad_pair, mask_pair = items
        key_value = jnp.dot(enc_pair, w_kv, preferred_element_type=f32).astype(bf16)
        key_value = key_value.reshape(1, LEN, HEADS, 2, HEAD)
        grad_query, grad_key, grad_value = attend_back(query_pair[None], grad_pair[None], key_value[:, :, :, 0], key_value[:, :, :, 1], mask_pair[None])
        return (grad_query[0], grad_key[0], grad_value[0])
    grad_query, grad_key, grad_value = lax.map(one_pair, (encoded, queries, grad_out, key_mask))
    dec_grads = jnp.stack([grad_query, grad_key], axis=3).reshape(PAIRS, LEN, D)
    grad_kv = jnp.stack([grad_key, grad_value], axis=3).reshape(PAIRS * LEN, D)
    pair_scale = 1.0 / PAIRS
    enc_groups = encoded.reshape(N_DP, PAIR_DEV * LEN, D)
    grad_groups = grad_kv.reshape(N_DP, PAIR_DEV * LEN, D)

    def add_group(running, items):
        enc_group, grad_group = items
        term = (pair_scale * lax.dot_general(enc_group, grad_group, (((0,), (0,)), ((), ())), preferred_element_type=f32)).astype(bf16)
        return (running + term.astype(f32), None)
    d_wkv, unused = lax.scan(add_group, jnp.zeros((D, D), f32), (enc_groups, grad_groups))
    shard_width = D // N_MP
    grad_parts = grad_kv.reshape(PAIRS * LEN, N_MP, shard_width).transpose(1, 0, 2)
    weight_parts = w_kv.reshape(D, N_MP, shard_width).transpose(1, 0, 2)

    def add_heads(running, items):
        grad_part, weight_part = items
        term = lax.dot_general(grad_part, weight_part, (((1,), (1,)), ((), ())), preferred_element_type=f32).astype(bf16)
        return (running + term.astype(f32), None)
    grad_enc, unused_heads = lax.scan(add_heads, jnp.zeros((PAIRS * LEN, D), f32), (grad_parts, weight_parts))
    grad_enc = grad_enc.reshape(PAIRS, LEN, D)
    grad_normed = grad_enc * gain_wide
    d_gain = pair_scale * lax.optimization_barrier(jnp.sum(grad_enc * normed, axis=(0, 1)))
    sec_grads = jnp.stack([grad_normed.astype(bf16), dec_grads])
    return (sec_grads, d_wkv, d_gain)
```

```python
import jax
import jax.numpy as jnp
from jax import lax
from jax.experimental import pallas as pl
from jax.experimental.pallas import tpu as pltpu
from jax.sharding import Mesh, PartitionSpec as P

D = 4096
HEAD = 64
EPS = 1e-06
F32 = jnp.float32
BF16 = jnp.bfloat16

PLANE = ("y", "phase")
SWAP = [(0, 1), (1, 0)]


def attend_kernel(len_ref, qg_ref, kv_ref, dec_ref, gkv_ref):
    length = qg_ref.shape[0]
    qg = qg_ref[...]
    kv = kv_ref[...]
    low_lane = lax.broadcasted_iota(jnp.int32, qg.shape, 1) < HEAD
    factor = jnp.asarray(1.0 / HEAD**0.5, BF16)
    zero = jnp.zeros((), BF16)
    scaled = qg * factor
    queries = jnp.where(low_lane, scaled, zero)
    grads = jnp.where(low_lane, zero, scaled)
    keys = lax.broadcasted_iota(jnp.int32, (1, length), 1)
    bias = jnp.where(keys < len_ref[0], 0.0, -1e30).astype(F32)
    nt = (((1,), (1,)), ((), ()))
    nn = (((1,), (0,)), ((), ()))
    scores = lax.dot_general(queries, kv, nt, preferred_element_type=F32) + bias
    grad_prob = lax.dot_general(grads, kv, nt, preferred_element_type=F32)
    weights = jnp.exp(scores - jnp.max(scores, axis=-1, keepdims=True))
    probs = weights * (1.0 / jnp.sum(weights, axis=-1, keepdims=True))
    prob_low = probs.astype(BF16)
    attended = lax.dot_general(prob_low, kv, nn, preferred_element_type=F32)
    row_delta = jnp.sum(grads.astype(F32) * attended, axis=-1, keepdims=True)
    grad_score = (probs * (grad_prob - row_delta)).astype(BF16)
    grad_query = lax.dot_general(grad_score, kv, nn, preferred_element_type=F32)
    qg_t = qg.T
    key_t = lax.dot_general(qg_t[:HEAD], grad_score, nn, preferred_element_type=F32)
    value_t = lax.dot_general(qg_t[HEAD:], prob_low, nn, preferred_element_type=F32)
    gkv = jnp.concatenate([key_t, value_t], axis=0).T
    gkv_ref[...] = gkv.astype(BF16)
    rolled = pltpu.roll(gkv, HEAD, 1)
    dec_ref[...] = jnp.where(low_lane, grad_query, rolled).astype(BF16)


def attend(key_count, qg, kv):
    length, width = qg.shape
    block = pl.BlockSpec((length, 2 * HEAD), lambda h, n: (0, h))
    return pl.pallas_call(
        attend_kernel,
        grid_spec=pltpu.PrefetchScalarGridSpec(
            num_scalar_prefetch=1,
            grid=(width // (2 * HEAD),),
            in_specs=[block, block],
            out_specs=[block, block],
        ),
        out_shape=[jax.ShapeDtypeStruct((length, width), BF16)] * 2,
        compiler_params=pltpu.CompilerParams(vmem_limit_bytes=32 << 20),
        name="attend",
    )(key_count, qg, kv)


def cut(array, axis, index, size):
    return lax.dynamic_slice_in_dim(array, index * size, size, axis)


def ordered(first, own, other, axis):
    return jnp.where(
        first, jnp.concatenate([own, other], axis), jnp.concatenate([other, own], axis)
    )


def matmul(a, b, dims):
    return lax.dot_general(a, b, ((dims[:1], dims[1:]), ((), ())), preferred_element_type=F32)


def on_device(sec_acts, gain, w_kv, src_len, tgt_len):
    groups = lax.axis_size("z")
    shards = lax.axis_size("mp")
    y, core, x = lax.axis_index("y"), lax.axis_index("phase"), lax.axis_index("mp")
    straight = y == core
    packed = sec_acts[0, 0]
    length, width = packed.shape
    rows = w_kv.shape[0]
    half = width // 2
    pair_scale = 1.0 / (2 * groups)

    def across(value, turn, plane):
        moves = [
            (i * shards + s, i * shards + (s + turn) % shards) for i in plane for s in range(shards)
        ]
        return lax.ppermute(value, ("y", "phase", "mp"), moves)

    sent = lax.ppermute(cut(w_kv, 1, 1 - y, half), "y", SWAP)
    w_block = ordered(y == 0, cut(w_kv, 1, y, half), sent, 0)
    w_own = lax.all_gather(w_block, "z", axis=0, tiled=True)
    w_other = lax.ppermute(w_own, "phase", SWAP)

    here = lax.ppermute(packed, PLANE, [(0, 0), (2, 3)])
    there = lax.ppermute(packed, PLANE, [(0, 2), (2, 1)])
    raw = [jnp.where(straight, here, there)]
    gains = [gain]
    for turn in range(1, shards):
        raw.append(
            jnp.where(straight, across(here, turn, (0, 3)), across(there, turn, (1, 2)))
        )
        gains.append(lax.ppermute(gain, "mp", [(s, (s + turn) % shards) for s in range(shards)]))

    def natural(parts):
        if shards == 2:
            return [jnp.where(x == i, parts[0], parts[1]) for i in range(2)]
        stacked = jnp.stack(parts)
        return [
            lax.dynamic_index_in_dim(stacked, (x - i) % shards, 0, keepdims=False)
            for i in range(shards)
        ]

    hidden = jnp.concatenate(natural(raw), axis=1).astype(F32)
    gain_all = jnp.concatenate(natural(gains)).astype(F32)
    inv_rms = lax.rsqrt(jnp.sum(hidden * hidden, axis=-1, keepdims=True) / D + EPS)
    encoded = (hidden * inv_rms * gain_all).astype(BF16)
    by_core = encoded.reshape(length, 2 * groups, 2, rows)
    enc_0 = by_core[:, :, 0].reshape(length, -1)
    enc_1 = by_core[:, :, 1].reshape(length, -1)
    enc_own = jnp.where(core == 0, enc_0, enc_1)
    enc_other = jnp.where(core == 0, enc_1, enc_0)

    position = lax.broadcasted_iota(jnp.int32, (length, width), 0)
    is_grad = lax.broadcasted_iota(jnp.int32, (length, width), 1) % (2 * HEAD) >= HEAD
    masked = jnp.where(is_grad & (position >= tgt_len[0]), jnp.zeros((), BF16), packed)
    qg_here = lax.ppermute(cut(masked, 1, y, half), PLANE, [(1, 0), (3, 3)])
    qg_there = lax.ppermute(cut(masked, 1, 1 - y, half), PLANE, [(1, 2), (3, 1)])
    qg = jnp.where(straight, qg_here, qg_there)
    key_count = jnp.where(straight, src_len, lax.ppermute(src_len, "y", SWAP))

    kv = (matmul(enc_own, w_own, (1, 0)) + matmul(enc_other, w_other, (1, 0))).astype(BF16)
    dec, gkv = attend(key_count, qg, kv)

    dw_other = (pair_scale * matmul(enc_other, gkv, (0, 0))).astype(BF16)
    dw_own = pair_scale * matmul(enc_own, gkv, (0, 0))
    dw_chip = (dw_own + lax.ppermute(dw_other, "phase", SWAP).astype(F32)).astype(BF16)
    dw = lax.psum_scatter(dw_chip, "z", scatter_dimension=0, tiled=True)
    dw_sent = lax.ppermute(cut(dw, 0, 1 - y, rows), "y", SWAP)
    d_wkv = ordered(y == 0, cut(dw, 0, y, rows), dw_sent, 1).astype(F32)

    de_own = matmul(gkv, w_own, (1, 1)).astype(BF16)
    de_other = matmul(gkv, w_other, (1, 1)).astype(BF16)

    def features(shard):
        return jnp.concatenate(
            [cut(de_own, 1, shard, half), cut(de_other, 1, shard, half)], axis=1
        )

    total = features(x).astype(F32)
    for turn in range(1, shards):
        moved = lax.ppermute(
            features((x + turn) % shards), "mp", [(s, (s + turn) % shards) for s in range(shards)]
        )
        total = total + moved.astype(F32)
    total = total + lax.ppermute(total.astype(BF16), PLANE, [(2, 0), (1, 3)]).astype(F32)
    split = total.reshape(length, 2, -1, rows)
    first = jnp.where(core == 0, split[:, 0], split[:, 1])
    second = jnp.where(core == 0, split[:, 1], split[:, 0])
    grad_enc = jnp.stack([first, second], axis=2).reshape(length, width)
    grad_normed = (grad_enc * gain.astype(F32)).astype(BF16)
    enc_grads = lax.ppermute(grad_normed, PLANE, [(0, 0), (3, 2)])
    normed = raw[0].astype(F32) * inv_rms
    gain_term = pair_scale * jnp.sum(grad_enc * normed, axis=0)
    gain_term = jnp.where(straight, gain_term, 0.0)
    d_gain = lax.psum(gain_term, ("z", "y", "phase"))

    dec_here = lax.ppermute(dec, PLANE, [(0, 1), (3, 3)])
    dec_there = lax.ppermute(dec, PLANE, [(2, 1), (1, 3)])
    dec_grads = ordered(y == 0, dec_here, dec_there, 1)
    sec_grads = jnp.where(core == 0, enc_grads, dec_grads)[None, None]
    return (sec_grads, d_wkv, d_gain)


def solution(mesh):
    size = mesh.shape
    split = (size["dp"] // 2, 2, size["phase"], size["mp"])
    fine = Mesh(mesh.devices.reshape(split), ("z", "y", "phase", "mp"))
    pairs = ("z", "y")
    acts = P("phase", pairs, None, "mp")
    weights = P(("z", "y", "phase"), "mp")
    return jax.shard_map(
        on_device,
        mesh=fine,
        in_specs=(acts, P("mp"), weights, P(pairs), P(pairs)),
        out_specs=(acts, weights, P("mp")),
        check_vma=False,
    )
```

```python
import jax
import jax.numpy as jnp
from jax import lax
from jax.experimental import pallas as pl
from jax.experimental.pallas import tpu as pltpu
from jax.sharding import Mesh, PartitionSpec as P

D = 4096
HEAD = 64
EPS = 1e-06
CHUNKS = 2
F32 = jnp.float32
BF16 = jnp.bfloat16
NN = (((1,), (0,)), ((), ()))
NT = (((1,), (1,)), ((), ()))
TN = (((0,), (0,)), ((), ()))

PLANE = ("y", "phase")
SWAP = [(0, 1), (1, 0)]


def dot(a, b, dims=NN):
    return lax.dot_general(a, b, dims, preferred_element_type=F32)


def params(mib):
    return pltpu.CompilerParams(vmem_limit_bytes=mib << 20)


def norm_kernel(groups, rows, at, here, there, far_here, far_there, gain, own, other, natural):
    straight, x, y, core, z = at[0] == 1, at[1], at[2], at[3], at[4]
    width = here.shape[1]
    near = jnp.where(straight, here[...], there[...]).astype(F32)
    far = jnp.where(straight, far_here[...], far_there[...]).astype(F32)
    total = jnp.sum(near * near, axis=-1, keepdims=True) + jnp.sum(far * far, axis=-1, keepdims=True)
    inv_rms = lax.rsqrt(total / D + EPS)
    near_at = pl.ds(pl.multiple_of(x * width, width), width)
    far_at = pl.ds(pl.multiple_of((1 - x) * width, width), width)
    natural[:, near_at] = (near * inv_rms * gain[:, near_at]).astype(BF16)
    natural[:, far_at] = (far * inv_rms * gain[:, far_at]).astype(BF16)
    for slot in range(groups):
        group = lax.rem(z + slot, groups)
        for k in range(2):
            row = 2 * group + (y if k == 0 else 1 - y)
            put = slice((2 * slot + k) * rows, (2 * slot + k + 1) * rows)
            for out, half in ((own, core), (other, 1 - core)):
                got = pl.multiple_of((2 * row + half) * rows, rows)
                out[:, put] = natural[:, pl.ds(got, rows)]


def norm(at, here, there, far_here, far_there, gain, groups, rows):
    length, width = here.shape
    step = 128

    def pick(want):
        return pl.BlockSpec((step, width), lambda i, s: (jnp.where(s[0] == want, i, 0), 0))

    out = pl.BlockSpec((step, D // 2), lambda i, s: (i, 0))
    return pl.pallas_call(
        lambda *refs: norm_kernel(groups, rows, *refs),
        grid_spec=pltpu.PrefetchScalarGridSpec(
            num_scalar_prefetch=1,
            grid=(length // step,),
            in_specs=[pick(1), pick(0), pick(1), pick(0), pl.BlockSpec((1, D), lambda i, s: (0, 0))],
            out_specs=[out, out],
            scratch_shapes=[pltpu.VMEM((step, D), BF16)],
        ),
        out_shape=[jax.ShapeDtypeStruct((length, D // 2), BF16)] * 2,
        compiler_params=params(32),
        name="norm",
    )(at, here, there, far_here, far_there, gain)


def attend_head(bias, qg, kv):
    low_lane = lax.broadcasted_iota(jnp.int32, qg.shape, 1) < HEAD
    zero = jnp.zeros((), BF16)
    scaled = qg * jnp.asarray(1.0 / HEAD**0.5, BF16)
    queries = jnp.where(low_lane, scaled, zero)
    grads = jnp.where(low_lane, zero, scaled)
    scores = dot(queries, kv, NT) + bias
    grad_prob = dot(grads, kv, NT)
    weights = jnp.exp(scores - jnp.max(scores, axis=-1, keepdims=True))
    probs = weights * (1.0 / jnp.sum(weights, axis=-1, keepdims=True))
    prob_low = probs.astype(BF16)
    attended = dot(prob_low, kv)
    row_delta = jnp.sum(grads.astype(F32) * attended, axis=-1, keepdims=True)
    grad_score = (probs * (grad_prob - row_delta)).astype(BF16)
    grad_query = dot(grad_score, kv)
    qg_t = qg.T
    key_t = dot(qg_t[:HEAD], grad_score)
    value_t = dot(qg_t[HEAD:], prob_low)
    gkv = jnp.concatenate([key_t, value_t], axis=0).T
    dec = jnp.where(low_lane, grad_query, pltpu.roll(gkv, HEAD, 1))
    return dec.astype(BF16), gkv.astype(BF16)


def attend_kernel(at, enc_own, enc_other, w_own, w_other, qg_here, qg_there, dec, gkv):
    kv = (dot(enc_own[...], w_own[...]) + dot(enc_other[...], w_other[...])).astype(BF16)
    keys = lax.broadcasted_iota(jnp.int32, (1, kv.shape[0]), 1)
    bias = jnp.where(keys < at[5], 0.0, -1e30).astype(F32)
    for head in range(kv.shape[1] // (2 * HEAD)):
        lanes = slice(head * 2 * HEAD, (head + 1) * 2 * HEAD)
        qg = jnp.where(at[0] == 1, qg_here[:, lanes], qg_there[:, lanes])
        dec[:, lanes], gkv[:, lanes] = attend_head(bias, qg, kv[:, lanes])


def attend(at, enc_own, enc_other, w_own, w_other, qg_here, qg_there, chunk):
    length = enc_own.shape[0]
    half, cols = w_own.shape
    step = min(256, cols)
    first = chunk * (cols // step)
    enc = pl.BlockSpec((length, half), lambda i, s: (0, 0))
    weight = pl.BlockSpec((half, step), lambda i, s: (0, i))
    out = pl.BlockSpec((length, step), lambda i, s: (0, i))

    def pick(want):
        return pl.BlockSpec((length, step), lambda i, s: (0, jnp.where(s[0] == want, first + i, first)))

    return pl.pallas_call(
        attend_kernel,
        grid_spec=pltpu.PrefetchScalarGridSpec(
            num_scalar_prefetch=1,
            grid=(cols // step,),
            in_specs=[enc, enc, weight, weight, pick(1), pick(0)],
            out_specs=[out, out],
        ),
        out_shape=[jax.ShapeDtypeStruct((length, cols), BF16)] * 2,
        compiler_params=params(48),
        name="attend",
    )(at, enc_own, enc_other, w_own, w_other, qg_here, qg_there)


def weight_grad_kernel(scale, at, enc_a, enc_b, gkv_a, gkv_b, weight, out, gain_term):
    grad = scale * (dot(enc_a[...], gkv_a[...], TN) + dot(enc_b[...], gkv_b[...], TN))
    out[...] = grad.astype(BF16)
    product = grad * weight[...].astype(F32)
    lanes = product[:, :128]
    for i in range(1, product.shape[1] // 128):
        lanes = lanes + product[:, i * 128 : (i + 1) * 128]
    gain_term[0] = jnp.sum(lanes.T, axis=0, keepdims=True)


def weight_grad(at, enc_a, enc_b, gkv_a, gkv_b, weight, groups, scale):
    length, half = enc_a.shape
    cols = weight.shape[1]
    step = half // groups

    def slot(i, s):
        return lax.rem(i + groups - s[4], groups)

    enc = pl.BlockSpec((length, step), lambda i, s: (0, slot(i, s)))
    gkv = pl.BlockSpec((length, cols), lambda i, s: (0, 0))
    return pl.pallas_call(
        lambda *refs: weight_grad_kernel(scale, *refs),
        grid_spec=pltpu.PrefetchScalarGridSpec(
            num_scalar_prefetch=1,
            grid=(groups,),
            in_specs=[enc, enc, gkv, gkv, pl.BlockSpec((step, cols), lambda i, s: (slot(i, s), 0))],
            out_specs=[
                pl.BlockSpec((step, cols), lambda i, s: (i, 0)),
                pl.BlockSpec((1, 1, step), lambda i, s: (i, 0, 0)),
            ],
        ),
        out_shape=[
            jax.ShapeDtypeStruct((half, cols), BF16),
            jax.ShapeDtypeStruct((groups, 1, step), F32),
        ],
        compiler_params=params(32),
        name="weight_grad",
    )(at, enc_a, enc_b, gkv_a, gkv_b, weight)


def enc_grad_kernel(at, gkv_0, gkv_1, own_0, own_1, other_0, other_1, out):
    rows = own_0.shape[0]
    own = dot(gkv_0[...], own_0[...], NT) + dot(gkv_1[...], own_1[...], NT)
    other = dot(gkv_0[...], other_0[...], NT) + dot(gkv_1[...], other_1[...], NT)
    first = at[3] == 0
    out[:, :rows] = jnp.where(first, own, other).astype(BF16)
    out[:, rows:] = jnp.where(first, other, own).astype(BF16)


def enc_grad(at, gkvs, owns, others, groups, rows, shard):
    length, cols = gkvs[0].shape
    per_shard = groups // 2

    def block(i, s):
        target = lax.rem(s[1] + shard, 2)
        group = target * per_shard + i // 2
        slot = lax.rem(group + groups - s[4], groups)
        return (2 * slot + lax.rem(i + s[2], 2), 0)

    gkv = pl.BlockSpec((length, cols), lambda i, s: (0, 0))
    weight = pl.BlockSpec((rows, cols), block)
    return pl.pallas_call(
        enc_grad_kernel,
        grid_spec=pltpu.PrefetchScalarGridSpec(
            num_scalar_prefetch=1,
            grid=(groups,),
            in_specs=[gkv, gkv, weight, weight, weight, weight],
            out_specs=pl.BlockSpec((length, 2 * rows), lambda i, s: (0, i)),
        ),
        out_shape=jax.ShapeDtypeStruct((length, D // 2), BF16),
        compiler_params=params(32),
        name="enc_grad",
    )(at, *gkvs, *owns, *others)


def cut(array, axis, index, size):
    return lax.dynamic_slice_in_dim(array, index * size, size, axis)


def ordered(first, own, other, axis):
    return jnp.where(
        first, jnp.concatenate([own, other], axis), jnp.concatenate([other, own], axis)
    )


def on_device(sec_acts, gain, w_kv, src_len, tgt_len):
    groups = lax.axis_size("z")
    shards = lax.axis_size("mp")
    z, y = lax.axis_index("z"), lax.axis_index("y")
    core, x = lax.axis_index("phase"), lax.axis_index("mp")
    straight = y == core
    packed = sec_acts[0, 0]
    length, width = packed.shape
    rows = w_kv.shape[0]
    half = width // 2
    cols = half // CHUNKS
    pair_scale = 1.0 / (2 * groups)
    tiled = shards == 2 and rows % 128 == 0

    def turned(count, by):
        return [(i, (i + by) % count) for i in range(count)]

    def across(value, turn, moves):
        return lax.ppermute(
            value,
            ("y", "phase", "mp"),
            [(a * shards + s, b * shards + (s + turn) % shards) for a, b in moves for s in range(shards)],
        )

    def chunk_of(side, k):
        return lax.dynamic_slice_in_dim(w_kv, side * half + k * cols, cols, 1)

    def slots(block):
        return [lax.ppermute(block, "z", turned(groups, -s)) for s in range(1, groups)]

    mine = [chunk_of(y, k) for k in range(CHUNKS)]
    swapped = [lax.ppermute(chunk_of(1 - y, k), "y", SWAP) for k in range(CHUNKS)]

    here = lax.ppermute(packed, PLANE, [(0, 0), (2, 3)])
    there = lax.ppermute(packed, PLANE, [(0, 2), (2, 1)])
    far_here = [across(here, turn, [(0, 0), (3, 3)]) for turn in range(1, shards)]
    far_there = [across(there, turn, [(1, 1), (2, 2)]) for turn in range(1, shards)]
    gains = [gain] + [lax.ppermute(gain, "mp", turned(shards, t)) for t in range(1, shards)]

    near_slots, far_slots = slots(mine[0]), slots(swapped[0])
    w_own = [
        jnp.concatenate(
            [p for pair in zip([mine[0]] + near_slots, [swapped[0]] + far_slots) for p in pair], 0
        )
    ]
    for k in range(1, CHUNKS):
        block = jnp.concatenate([mine[k], swapped[k]], 0)
        w_own.append(jnp.concatenate([block] + slots(block), 0))
    w_other = [lax.ppermute(w, "phase", SWAP) for w in w_own]

    position = lax.broadcasted_iota(jnp.int32, (length, width), 0)
    is_grad = lax.broadcasted_iota(jnp.int32, (length, width), 1) % (2 * HEAD) >= HEAD
    masked = jnp.where(is_grad & (position >= tgt_len[0]), jnp.zeros((), BF16), packed)
    qg_here = lax.ppermute(cut(masked, 1, y, half), PLANE, [(1, 0), (3, 3)])
    qg_there = lax.ppermute(cut(masked, 1, 1 - y, half), PLANE, [(1, 2), (3, 1)])
    key_count = jnp.where(straight, src_len, lax.ppermute(src_len, "y", SWAP))
    at = jnp.concatenate(
        [jnp.stack([straight.astype(jnp.int32), x, y, core, z]).astype(jnp.int32), key_count]
    )

    def natural(parts, axis):
        if shards == 2:
            return ordered(x == 0, parts[0], parts[1], axis)
        stacked = jnp.stack(parts)
        return jnp.concatenate(
            [
                lax.dynamic_index_in_dim(stacked, (x - i) % shards, 0, keepdims=False)
                for i in range(shards)
            ],
            axis,
        )

    block_group = (z + jnp.arange(groups)) % groups
    block_pair = 2 * block_group[:, None] + jnp.stack([y, 1 - y])[None, :]
    block_order = (2 * block_pair[None] + jnp.stack([core, 1 - core])[:, None, None]).reshape(-1)
    gain_all = natural(gains, 0).astype(F32)

    if tiled:
        enc_own, enc_other = norm(
            at, here, there, far_here[0], far_there[0], gain_all[None], groups, rows
        )
    else:
        raw = [jnp.where(straight, a, b) for a, b in zip([here] + far_here, [there] + far_there)]
        hidden = natural(raw, 1).astype(F32)
        inv_rms = lax.rsqrt(jnp.sum(hidden * hidden, axis=-1, keepdims=True) / D + EPS)
        encoded = (hidden * inv_rms * gain_all).astype(BF16)
        encoded = encoded.reshape(length, -1, rows)[:, block_order].reshape(length, 2, -1)
        enc_own, enc_other = encoded[:, 0], encoded[:, 1]
    enc_mate = lax.ppermute(enc_other, "phase", SWAP)

    decs, gkvs, weight_sums, gain_terms = [], [], [], []
    for k in range(CHUNKS):
        dec, gkv = attend(at, enc_own, enc_other, w_own[k], w_other[k], qg_here, qg_there, k)
        gkvs.append(gkv)
        decs.append(
            (
                lax.ppermute(dec, PLANE, [(0, 1), (3, 3)]),
                lax.ppermute(dec, PLANE, [(2, 1), (1, 3)]),
            )
        )
        gkv_mate = lax.ppermute(gkv, "phase", SWAP)
        if tiled:
            grad, term = weight_grad(
                at, enc_own, enc_mate, gkv, gkv_mate, w_own[k], groups, pair_scale
            )
            term = term.reshape(groups, 2, rows)
        else:
            grad = pair_scale * (dot(enc_own, gkv, TN) + dot(enc_mate, gkv_mate, TN))
            term = jnp.sum(grad * w_own[k].astype(F32), axis=1).reshape(groups, 2, rows)
            term = jnp.roll(term, z, 0)
            grad = jnp.roll(grad.astype(BF16).reshape(groups, -1, cols), z, 0).reshape(-1, cols)
        gain_terms.append(term)
        weight_sums.append(lax.psum_scatter(grad, "z", scatter_dimension=0, tiled=True))

    if tiled:
        terms = [enc_grad(at, gkvs, w_own, w_other, groups, rows, s) for s in (1, 0)][::-1]
    else:
        gkv_all = jnp.concatenate(gkvs, 1)
        full = dot(gkv_all, jnp.concatenate([jnp.concatenate(w, 0) for w in zip(w_own, w_other)], 1), NT)
        back = jnp.zeros_like(block_order).at[block_order].set(jnp.arange(block_order.shape[0]))
        full = full.astype(BF16).reshape(length, -1, rows)[:, back].reshape(length, D)
        terms = [cut(full, 1, (x + s) % shards, width) for s in range(shards)]
    grad_enc = terms[0].astype(F32)
    for turn in range(1, shards):
        grad_enc = grad_enc + across(terms[turn], turn, [(0, 0), (3, 3)]).astype(F32)
    for turn in range(shards):
        grad_enc = grad_enc + across(terms[turn], turn, [(2, 0), (1, 3)]).astype(F32)
    grad_normed = (grad_enc * gain.astype(F32)).astype(BF16)
    enc_grads = lax.ppermute(grad_normed, PLANE, [(0, 0), (3, 2)])

    term = sum(gain_terms)
    term = jnp.where(y == 0, term, term[:, ::-1])
    by_core = jnp.stack([jnp.where(core == 0, term, 0.0), jnp.where(core == 1, term, 0.0)], axis=2)
    gain_sums = lax.psum(by_core.reshape(D), ("z", "y", "phase", "mp"))
    d_gain = cut(gain_sums, 0, x, width) / gain.astype(F32)

    kept = jnp.concatenate([w[:rows] for w in weight_sums], 1)
    got = jnp.concatenate([lax.ppermute(w[rows:], "y", SWAP) for w in weight_sums], 1)
    d_wkv = ordered(y == 0, kept, got, 1).astype(F32)

    dec_here = jnp.concatenate([d[0] for d in decs], 1)
    dec_there = jnp.concatenate([d[1] for d in decs], 1)
    dec_grads = ordered(y == 0, dec_here, dec_there, 1)
    sec_grads = jnp.where(core == 0, enc_grads, dec_grads)[None, None]
    return (sec_grads, d_wkv, d_gain)


def solution(mesh):
    size = mesh.shape
    split = (size["dp"] // 2, 2, size["phase"], size["mp"])
    fine = Mesh(mesh.devices.reshape(split), ("z", "y", "phase", "mp"))
    pairs = ("z", "y")
    acts = P("phase", pairs, None, "mp")
    weights = P(("z", "y", "phase"), "mp")
    return jax.shard_map(
        on_device,
        mesh=fine,
        in_specs=(acts, P("mp"), weights, P(pairs), P(pairs)),
        out_specs=(acts, weights, P("mp")),
        check_vma=False,
    )
```

```python
import jax
import jax.numpy as jnp
from jax import lax
from jax.experimental import pallas as pl
from jax.experimental.pallas import tpu as pltpu
from jax.sharding import Mesh, PartitionSpec as P

D = 4096
HEAD = 64
EPS = 1e-06
CHUNKS = 2
F32 = jnp.float32
BF16 = jnp.bfloat16
NN = (((1,), (0,)), ((), ()))
NT = (((1,), (1,)), ((), ()))
TN = (((0,), (0,)), ((), ()))

PLANE = ("y", "phase")
SWAP = [(0, 1), (1, 0)]


def dot(a, b, dims=NN):
    return lax.dot_general(a, b, dims, preferred_element_type=F32)


def cost(flops, mib, exps=0):
    return pl.CostEstimate(flops=flops, bytes_accessed=mib << 20, transcendentals=exps)


def params(mib):
    return pltpu.CompilerParams(vmem_limit_bytes=mib << 20)


def chosen(kind, local, here, there):
    return jnp.where(kind == 0, local, jnp.where(kind == 1, here, there))


def norm_kernel(groups, rows, at, *refs):
    nears, fars, (gain, own, other, natural) = refs[:3], refs[3:6], refs[6:]
    x, y, core, z = at[1], at[2], at[3], at[4]
    width = nears[0].shape[1]
    near = chosen(at[0], *[r[...] for r in nears]).astype(F32)
    far = chosen(at[0], *[r[...] for r in fars]).astype(F32)
    total = jnp.sum(near * near, axis=-1, keepdims=True) + jnp.sum(far * far, axis=-1, keepdims=True)
    inv_rms = lax.rsqrt(total / D + EPS)
    near_at = pl.ds(pl.multiple_of(x * width, width), width)
    far_at = pl.ds(pl.multiple_of((1 - x) * width, width), width)
    natural[:, near_at] = (near * inv_rms * gain[:, near_at]).astype(BF16)
    natural[:, far_at] = (far * inv_rms * gain[:, far_at]).astype(BF16)
    for slot in range(groups):
        group = lax.rem(z + slot, groups)
        for k in range(2):
            row = 2 * group + (y if k == 0 else 1 - y)
            put = slice((2 * slot + k) * rows, (2 * slot + k + 1) * rows)
            for out, half in ((own, core), (other, 1 - core)):
                got = pl.multiple_of((2 * row + half) * rows, rows)
                out[:, put] = natural[:, pl.ds(got, rows)]


def norm(at, nears, fars, gain, groups, rows):
    length, width = nears[0].shape
    step = 128

    def pick(want):
        return pl.BlockSpec((step, width), lambda i, s: (jnp.where(s[0] == want, i, 0), 0))

    out = pl.BlockSpec((step, D // 2), lambda i, s: (i, 0))
    return pl.pallas_call(
        lambda *refs: norm_kernel(groups, rows, *refs),
        grid_spec=pltpu.PrefetchScalarGridSpec(
            num_scalar_prefetch=1,
            grid=(length // step,),
            in_specs=[pick(i % 3) for i in range(6)] + [pl.BlockSpec((1, D), lambda i, s: (0, 0))],
            out_specs=[out, out],
            scratch_shapes=[pltpu.VMEM((step, D), BF16)],
        ),
        out_shape=[jax.ShapeDtypeStruct((length, D // 2), BF16)] * 2,
        compiler_params=params(32),
        cost_estimate=cost(8 * length * D, 8),
        name="norm",
    )(at, *nears, *fars, gain)


def attend_head(bias, qg, kv):
    low_lane = lax.broadcasted_iota(jnp.int32, qg.shape, 1) < HEAD
    zero = jnp.zeros((), BF16)
    scaled = qg * jnp.asarray(1.0 / HEAD**0.5, BF16)
    queries = jnp.where(low_lane, scaled, zero)
    grads = jnp.where(low_lane, zero, scaled)
    scores = dot(queries, kv, NT) + bias
    grad_prob = dot(grads, kv, NT)
    weights = jnp.exp(scores - jnp.max(scores, axis=-1, keepdims=True))
    probs = weights * (1.0 / jnp.sum(weights, axis=-1, keepdims=True))
    prob_low = probs.astype(BF16)
    attended = dot(prob_low, kv)
    row_delta = jnp.sum(grads.astype(F32) * attended, axis=-1, keepdims=True)
    grad_score = (probs * (grad_prob - row_delta)).astype(BF16)
    grad_query = dot(grad_score, kv)
    qg_t = qg.T
    key_t = dot(qg_t[:HEAD], grad_score)
    value_t = dot(qg_t[HEAD:], prob_low)
    gkv = jnp.concatenate([key_t, value_t], axis=0).T
    dec = jnp.where(low_lane, grad_query, pltpu.roll(gkv, HEAD, 1))
    return dec.astype(BF16), gkv.astype(BF16)


def attend_kernel(at, enc_own, enc_other, w_own, w_other, *refs):
    qgs, (dec, gkv) = refs[:3], refs[3:]
    kv = (dot(enc_own[...], w_own[...]) + dot(enc_other[...], w_other[...])).astype(BF16)
    keys = lax.broadcasted_iota(jnp.int32, (1, kv.shape[0]), 1)
    bias = jnp.where(keys < at[5], 0.0, -1e30).astype(F32)
    for head in range(kv.shape[1] // (2 * HEAD)):
        lanes = slice(head * 2 * HEAD, (head + 1) * 2 * HEAD)
        qg = chosen(at[6], *[r[:, lanes] for r in qgs])
        dec[:, lanes], gkv[:, lanes] = attend_head(bias, qg, kv[:, lanes])


def attend(at, enc_own, enc_other, w_own, w_other, qgs, chunk):
    length = enc_own.shape[0]
    half, cols = w_own.shape
    step = min(256, cols)
    first = chunk * (cols // step)
    enc = pl.BlockSpec((length, half), lambda i, s: (0, 0))
    weight = pl.BlockSpec((half, step), lambda i, s: (0, i))
    out = pl.BlockSpec((length, step), lambda i, s: (0, i))

    def pick(want):
        return pl.BlockSpec((length, step), lambda i, s: (0, jnp.where(s[6] == want, first + i, first)))

    return pl.pallas_call(
        attend_kernel,
        grid_spec=pltpu.PrefetchScalarGridSpec(
            num_scalar_prefetch=1,
            grid=(cols // step,),
            in_specs=[enc, enc, weight, weight, pick(0), pick(1), pick(2)],
            out_specs=[out, out],
        ),
        out_shape=[jax.ShapeDtypeStruct((length, cols), BF16)] * 2,
        compiler_params=params(48),
        cost_estimate=cost(
            length * cols * (4 * half + 14 * length), 8, length * length * cols // (2 * HEAD)
        ),
        name="attend",
    )(at, enc_own, enc_other, w_own, w_other, *qgs)


def weight_grad_kernel(scale, at, enc_a, enc_b, gkv_a, gkv_b, weight, out, gain_term):
    grad = scale * (dot(enc_a[...], gkv_a[...], TN) + dot(enc_b[...], gkv_b[...], TN))
    out[...] = grad.astype(BF16)
    product = grad * weight[...].astype(F32)
    lanes = product[:, :128]
    for i in range(1, product.shape[1] // 128):
        lanes = lanes + product[:, i * 128 : (i + 1) * 128]
    gain_term[0] = jnp.sum(lanes.T, axis=0, keepdims=True)


def weight_grad(at, enc_a, enc_b, gkv_a, gkv_b, weight, groups, scale):
    length, half = enc_a.shape
    cols = weight.shape[1]
    step = half // groups

    def slot(i, s):
        return lax.rem(i + groups - s[4], groups)

    enc = pl.BlockSpec((length, step), lambda i, s: (0, slot(i, s)))
    gkv = pl.BlockSpec((length, cols), lambda i, s: (0, 0))
    return pl.pallas_call(
        lambda *refs: weight_grad_kernel(scale, *refs),
        grid_spec=pltpu.PrefetchScalarGridSpec(
            num_scalar_prefetch=1,
            grid=(groups,),
            in_specs=[enc, enc, gkv, gkv, pl.BlockSpec((step, cols), lambda i, s: (slot(i, s), 0))],
            out_specs=[
                pl.BlockSpec((step, cols), lambda i, s: (i, 0)),
                pl.BlockSpec((1, 1, step), lambda i, s: (i, 0, 0)),
            ],
        ),
        out_shape=[
            jax.ShapeDtypeStruct((half, cols), BF16),
            jax.ShapeDtypeStruct((groups, 1, step), F32),
        ],
        compiler_params=params(32),
        cost_estimate=cost(4 * length * half * cols, 8),
        name="weight_grad",
    )(at, enc_a, enc_b, gkv_a, gkv_b, weight)


def enc_grad_kernel(at, gkv_0, gkv_1, own_0, own_1, other_0, other_1, out):
    rows = own_0.shape[0]
    own = dot(gkv_0[...], own_0[...], NT) + dot(gkv_1[...], own_1[...], NT)
    other = dot(gkv_0[...], other_0[...], NT) + dot(gkv_1[...], other_1[...], NT)
    first = at[3] == 0
    out[:, :rows] = jnp.where(first, own, other).astype(BF16)
    out[:, rows:] = jnp.where(first, other, own).astype(BF16)


def enc_grad(at, gkvs, owns, others, groups, rows, shard):
    length, cols = gkvs[0].shape
    per_shard = groups // 2

    def block(i, s):
        target = lax.rem(s[1] + shard, 2)
        group = target * per_shard + i // 2
        slot = lax.rem(group + groups - s[4], groups)
        return (2 * slot + lax.rem(i + s[2], 2), 0)

    gkv = pl.BlockSpec((length, cols), lambda i, s: (0, 0))
    weight = pl.BlockSpec((rows, cols), block)
    return pl.pallas_call(
        enc_grad_kernel,
        grid_spec=pltpu.PrefetchScalarGridSpec(
            num_scalar_prefetch=1,
            grid=(groups,),
            in_specs=[gkv, gkv, weight, weight, weight, weight],
            out_specs=pl.BlockSpec((length, 2 * rows), lambda i, s: (0, i)),
        ),
        out_shape=jax.ShapeDtypeStruct((length, D // 2), BF16),
        compiler_params=params(32),
        cost_estimate=cost(4 * length * D * cols, 8),
        name="enc_grad",
    )(at, *gkvs, *owns, *others)


def cut(array, axis, index, size):
    return lax.dynamic_slice_in_dim(array, index * size, size, axis)


def ordered(first, own, other, axis):
    return jnp.where(
        first, jnp.concatenate([own, other], axis), jnp.concatenate([other, own], axis)
    )


def after(value, *others):
    return lax.optimization_barrier((value,) + others)[0]


def on_device(sec_acts, gain, w_kv, src_len, tgt_len):
    groups = lax.axis_size("z")
    shards = lax.axis_size("mp")
    z, y = lax.axis_index("z"), lax.axis_index("y")
    core, x = lax.axis_index("phase"), lax.axis_index("mp")
    straight = y == core
    packed = sec_acts[0, 0]
    length, width = packed.shape
    rows = w_kv.shape[0]
    half = width // 2
    cols = half // CHUNKS
    pair_scale = 1.0 / (2 * groups)
    tiled = shards == 2 and rows % 128 == 0

    def turned(count, by):
        return [(i, (i + by) % count) for i in range(count)]

    def across(value, turn, moves):
        return lax.ppermute(
            value,
            ("y", "phase", "mp"),
            [(a * shards + s, b * shards + (s + turn) % shards) for a, b in moves for s in range(shards)],
        )

    def chunk_of(side, k):
        return lax.dynamic_slice_in_dim(w_kv, side * half + k * cols, cols, 1)

    def slots(block):
        return [lax.ppermute(block, "z", turned(groups, -s)) for s in range(1, groups)]

    mine = [chunk_of(y, k) for k in range(CHUNKS)]
    swapped = []
    for k in range(CHUNKS):
        sent = chunk_of(1 - y, k)
        swapped.append(lax.ppermute(after(sent, *swapped), "y", SWAP))

    there = lax.ppermute(packed, PLANE, [(0, 2), (2, 1)])
    here = lax.ppermute(packed, PLANE, [(2, 3)])
    nears = [packed, here, there]
    fars = []
    for turn in range(1, shards):
        fars.append(
            [
                across(packed, turn, [(0, 0)]),
                across(here, turn, [(3, 3)]),
                across(there, turn, [(1, 1), (2, 2)]),
            ]
        )
    gains = [gain] + [lax.ppermute(gain, "mp", turned(shards, t)) for t in range(1, shards)]

    near_slots, far_slots = slots(mine[0]), slots(swapped[0])
    w_own = [
        jnp.concatenate(
            [p for pair in zip([mine[0]] + near_slots, [swapped[0]] + far_slots) for p in pair], 0
        )
    ]
    slot_0, later = {}, {}
    for k in range(1, CHUNKS):
        block = after(jnp.concatenate([mine[k], swapped[k]], 0), near_slots[0])
        slot_0[k], later[k] = block, slots(block)
    w_other = [lax.ppermute(w_own[0], "phase", SWAP)]

    position = lax.broadcasted_iota(jnp.int32, (length, width), 0)
    is_grad = lax.broadcasted_iota(jnp.int32, (length, width), 1) % (2 * HEAD) >= HEAD
    masked = jnp.where(is_grad & (position >= tgt_len[0]), jnp.zeros((), BF16), packed)
    qg_near, qg_far = cut(masked, 1, y, half), cut(masked, 1, 1 - y, half)
    qg_near, qg_far = lax.optimization_barrier((qg_near, qg_far, swapped[0]))[:2]
    qgs = [
        qg_near,
        lax.ppermute(qg_near, PLANE, [(1, 0)]),
        lax.ppermute(qg_far, PLANE, [(1, 2), (3, 1)]),
    ]
    key_count = jnp.where(straight, src_len, lax.ppermute(src_len, "y", SWAP))
    enc_kind = jnp.where(straight, y, 2)
    qg_kind = jnp.where(straight, 1 - y, 2)
    at = jnp.concatenate(
        [jnp.stack([enc_kind, x, y, core, z]).astype(jnp.int32), key_count, qg_kind[None]]
    )

    def natural(parts, axis):
        if shards == 2:
            return ordered(x == 0, parts[0], parts[1], axis)
        stacked = jnp.stack(parts)
        return jnp.concatenate(
            [
                lax.dynamic_index_in_dim(stacked, (x - i) % shards, 0, keepdims=False)
                for i in range(shards)
            ],
            axis,
        )

    block_group = (z + jnp.arange(groups)) % groups
    block_pair = 2 * block_group[:, None] + jnp.stack([y, 1 - y])[None, :]
    block_order = (2 * block_pair[None] + jnp.stack([core, 1 - core])[:, None, None]).reshape(-1)
    gain_all = natural(gains, 0).astype(F32)

    if tiled:
        gain_row = after(gain_all[None], *swapped)
        enc_own, enc_other = norm(at, nears, fars[0], gain_row, groups, rows)
    else:
        raw = [chosen(enc_kind, *parts) for parts in [nears] + fars]
        hidden = natural(raw, 1).astype(F32)
        inv_rms = lax.rsqrt(jnp.sum(hidden * hidden, axis=-1, keepdims=True) / D + EPS)
        encoded = (hidden * inv_rms * gain_all).astype(BF16)
        encoded = encoded.reshape(length, -1, rows)[:, block_order].reshape(length, 2, -1)
        enc_own, enc_other = encoded[:, 0], encoded[:, 1]
    enc_mate = lax.ppermute(enc_other, "phase", SWAP)

    decs, gkvs, weight_sums, gain_terms = [], [], [], []
    for k in range(CHUNKS):
        if k > 0:
            slot_0[k] = after(slot_0[k], grad)
            w_own.append(jnp.concatenate([slot_0[k]] + [after(p, grad) for p in later[k]], 0))
            w_other.append(lax.ppermute(w_own[k], "phase", SWAP))
        dec, gkv = attend(at, enc_own, enc_other, w_own[k], w_other[k], qgs, k)
        gkvs.append(gkv)
        decs.append(
            (
                jnp.where(y == 0, lax.ppermute(dec, PLANE, [(0, 1)]), dec),
                lax.ppermute(dec, PLANE, [(2, 1), (1, 3)]),
            )
        )
        gkv_mate = lax.ppermute(gkv, "phase", SWAP)
        if tiled:
            grad, term = weight_grad(
                at, enc_own, enc_mate, gkv, gkv_mate, w_own[k], groups, pair_scale
            )
            term = term.reshape(groups, 2, rows)
        else:
            grad = pair_scale * (dot(enc_own, gkv, TN) + dot(enc_mate, gkv_mate, TN))
            term = jnp.sum(grad * w_own[k].astype(F32), axis=1).reshape(groups, 2, rows)
            term = jnp.roll(term, z, 0)
            grad = jnp.roll(grad.astype(BF16).reshape(groups, -1, cols), z, 0).reshape(-1, cols)
        gain_terms.append(term)
        weight_sums.append(lax.psum_scatter(grad, "z", scatter_dimension=0, tiled=True))

    if tiled:
        terms = [enc_grad(at, gkvs, w_own, w_other, groups, rows, s) for s in (1, 0)][::-1]
    else:
        gkv_all = jnp.concatenate(gkvs, 1)
        full = dot(gkv_all, jnp.concatenate([jnp.concatenate(w, 0) for w in zip(w_own, w_other)], 1), NT)
        back = jnp.zeros_like(block_order).at[block_order].set(jnp.arange(block_order.shape[0]))
        full = full.astype(BF16).reshape(length, -1, rows)[:, back].reshape(length, D)
        terms = [cut(full, 1, (x + s) % shards, width) for s in range(shards)]
    moved = [across(terms[turn], turn, [(0, 0), (3, 3)]) for turn in range(1, shards)]
    moved += [across(terms[turn], turn, [(2, 0), (1, 3)]) for turn in range(shards)]

    term = sum(gain_terms)
    term = jnp.where(y == 0, term, term[:, ::-1])
    by_core = jnp.stack([jnp.where(core == 0, term, 0.0), jnp.where(core == 1, term, 0.0)], axis=2)
    gain_sums = lax.psum(by_core.reshape(D), ("z", "y", "phase", "mp"))
    d_gain = cut(gain_sums, 0, x, width) / gain.astype(F32)

    kept = jnp.concatenate([w[:rows] for w in weight_sums], 1)
    got = [lax.ppermute(w[rows:], "y", SWAP) for w in weight_sums]
    terms[0] = after(terms[0], gain_sums, got[0])
    grad_enc = terms[0].astype(F32)
    for part in moved:
        grad_enc = grad_enc + part.astype(F32)
    grad_normed = (grad_enc * gain.astype(F32)).astype(BF16)
    enc_grads = jnp.where(y == 0, grad_normed, lax.ppermute(grad_normed, PLANE, [(3, 2)]))
    got = jnp.concatenate(got, 1)
    d_wkv = ordered(y == 0, kept, got, 1).astype(F32)

    dec_here = jnp.concatenate([d[0] for d in decs], 1)
    dec_there = jnp.concatenate([d[1] for d in decs], 1)
    dec_grads = ordered(y == 0, dec_here, dec_there, 1)
    sec_grads = jnp.where(core == 0, enc_grads, dec_grads)[None, None]
    return (sec_grads, d_wkv, d_gain)


def solution(mesh):
    size = mesh.shape
    split = (size["dp"] // 2, 2, size["phase"], size["mp"])
    fine = Mesh(mesh.devices.reshape(split), ("z", "y", "phase", "mp"))
    pairs = ("z", "y")
    acts = P("phase", pairs, None, "mp")
    weights = P(("z", "y", "phase"), "mp")
    return jax.shard_map(
        on_device,
        mesh=fine,
        in_specs=(acts, P("mp"), weights, P(pairs), P(pairs)),
        out_specs=(acts, weights, P("mp")),
        check_vma=False,
    )
```

```python
import jax
import jax.numpy as jnp
from jax import lax
from jax.experimental import pallas as pl
from jax.experimental.pallas import tpu as pltpu
from jax.sharding import Mesh, PartitionSpec as P

D = 4096
HEAD = 64
EPS = 1e-06
CHUNKS = 2
DIRECT = ()
F32 = jnp.float32
BF16 = jnp.bfloat16
NN = (((1,), (0,)), ((), ()))
NT = (((1,), (1,)), ((), ()))
TN = (((0,), (0,)), ((), ()))

PLANE = ("y", "phase")
SWAP = [(0, 1), (1, 0)]


def dot(a, b, dims=NN):
    return lax.dot_general(a, b, dims, preferred_element_type=F32)


def cost(flops, mib, exps=0):
    return pl.CostEstimate(flops=flops, bytes_accessed=mib << 20, transcendentals=exps)


def params(mib):
    return pltpu.CompilerParams(vmem_limit_bytes=mib << 20)


def norm_kernel(groups, rows, at, *refs):
    nears, fars, (gain, own, other, inv_out, natural) = refs[:2], refs[2:4], refs[4:]
    x, y, core = at[1], at[2], at[3]
    width = nears[0].shape[1]
    near = jnp.where(at[0] == 1, *[r[...] for r in nears]).astype(F32)
    far = jnp.where(at[0] == 1, *[r[...] for r in fars]).astype(F32)
    total = jnp.sum(near * near, axis=-1, keepdims=True) + jnp.sum(far * far, axis=-1, keepdims=True)
    inv_rms = lax.rsqrt(total / D + EPS)
    inv_out[...] = jnp.broadcast_to(inv_rms, inv_out.shape)
    near_at = pl.ds(pl.multiple_of(x * width, width), width)
    far_at = pl.ds(pl.multiple_of((1 - x) * width, width), width)
    natural[:, near_at] = (near * inv_rms * gain[:, near_at]).astype(BF16)
    natural[:, far_at] = (far * inv_rms * gain[:, far_at]).astype(BF16)
    for group in range(groups):
        for k in range(2):
            row = 2 * group + (y if k == 0 else 1 - y)
            put = slice((2 * group + k) * rows, (2 * group + k + 1) * rows)
            for out, half in ((own, core), (other, 1 - core)):
                got = pl.multiple_of((2 * row + half) * rows, rows)
                out[:, put] = natural[:, pl.ds(got, rows)]


def norm(at, nears, fars, gain, groups, rows):
    length, width = nears[0].shape
    step = 128

    def pick(want):
        return pl.BlockSpec((step, width), lambda i, s: (jnp.where(s[0] == want, i, 0), 0))

    out = pl.BlockSpec((step, D // 2), lambda i, s: (i, 0))
    return pl.pallas_call(
        lambda *refs: norm_kernel(groups, rows, *refs),
        grid_spec=pltpu.PrefetchScalarGridSpec(
            num_scalar_prefetch=1,
            grid=(length // step,),
            in_specs=[pick(1), pick(0), pick(1), pick(0)] + [pl.BlockSpec((1, D), lambda i, s: (0, 0))],
            out_specs=[out, out, pl.BlockSpec((step, 128), lambda i, s: (i, 0))],
            scratch_shapes=[pltpu.VMEM((step, D), BF16)],
        ),
        out_shape=[jax.ShapeDtypeStruct((length, D // 2), BF16)] * 2
        + [jax.ShapeDtypeStruct((length, 128), F32)],
        compiler_params=params(32),
        cost_estimate=cost(8 * length * D, 8),
        name="norm",
    )(at, *nears, *fars, gain)


def attend_head(bias, qg, kv):
    low_lane = lax.broadcasted_iota(jnp.int32, qg.shape, 1) < HEAD
    zero = jnp.zeros((), BF16)
    scaled = qg * jnp.asarray(1.0 / HEAD**0.5, BF16)
    queries = jnp.where(low_lane, scaled, zero)
    grads = jnp.where(low_lane, zero, scaled)
    scores = dot(queries, kv, NT) + bias
    grad_prob = dot(grads, kv, NT)
    weights = jnp.exp(scores - jnp.max(scores, axis=-1, keepdims=True))
    probs = weights * (1.0 / jnp.sum(weights, axis=-1, keepdims=True))
    prob_low = probs.astype(BF16)
    attended = dot(prob_low, kv)
    row_delta = jnp.sum(grads.astype(F32) * attended, axis=-1, keepdims=True)
    grad_score = (probs * (grad_prob - row_delta)).astype(BF16)
    grad_query = dot(grad_score, kv)
    qg_t = qg.T
    key_t = dot(qg_t[:HEAD], grad_score)
    value_t = dot(qg_t[HEAD:], prob_low)
    gkv = jnp.concatenate([key_t, value_t], axis=0).T
    dec = jnp.where(low_lane, grad_query, pltpu.roll(gkv, HEAD, 1))
    return dec.astype(BF16), gkv.astype(BF16)


def attend_kernel(at, enc_own, enc_other, w_own, w_other, *refs):
    qgs, (dec, gkv) = refs[:2], refs[2:]
    kv = (dot(enc_own[...], w_own[...]) + dot(enc_other[...], w_other[...])).astype(BF16)
    keys = lax.broadcasted_iota(jnp.int32, (1, kv.shape[0]), 1)
    bias = jnp.where(keys < at[4], 0.0, -1e30).astype(F32)
    for head in range(kv.shape[1] // (2 * HEAD)):
        lanes = slice(head * 2 * HEAD, (head + 1) * 2 * HEAD)
        qg = jnp.where(at[0] == 1, *[r[:, lanes] for r in qgs])
        dec[:, lanes], gkv[:, lanes] = attend_head(bias, qg, kv[:, lanes])


def attend(at, enc_own, enc_other, w_own, w_other, qgs, chunk):
    length = enc_own.shape[0]
    half, cols = w_own.shape
    step = min(256, cols)
    first = chunk * (cols // step)
    enc = pl.BlockSpec((length, half), lambda i, s: (0, 0))
    weight = pl.BlockSpec((half, step), lambda i, s: (0, i))
    out = pl.BlockSpec((length, step), lambda i, s: (0, i))

    def pick(want):
        return pl.BlockSpec((length, step), lambda i, s: (0, jnp.where(s[0] == want, first + i, first)))

    return pl.pallas_call(
        attend_kernel,
        grid_spec=pltpu.PrefetchScalarGridSpec(
            num_scalar_prefetch=1,
            grid=(cols // step,),
            in_specs=[enc, enc, weight, weight, pick(1), pick(0)],
            out_specs=[out, out],
        ),
        out_shape=[jax.ShapeDtypeStruct((length, cols), BF16)] * 2,
        compiler_params=params(48),
        cost_estimate=cost(
            length * cols * (4 * half + 14 * length), 8, length * length * cols // (2 * HEAD)
        ),
        name="attend",
    )(at, enc_own, enc_other, w_own, w_other, *qgs)


def weight_grad_kernel(scale, at, enc_a, enc_b, gkv_a, gkv_b, out):
    grad = scale * (dot(enc_a[...], gkv_a[...], TN) + dot(enc_b[...], gkv_b[...], TN))
    out[...] = grad.astype(BF16)


def weight_grad(at, enc_a, enc_b, gkv_a, gkv_b, groups, scale):
    length, half = enc_a.shape
    cols = gkv_a.shape[1]
    step = half // groups
    enc = pl.BlockSpec((length, step), lambda i, s: (0, i))
    gkv = pl.BlockSpec((length, cols), lambda i, s: (0, 0))
    return pl.pallas_call(
        lambda *refs: weight_grad_kernel(scale, *refs),
        grid_spec=pltpu.PrefetchScalarGridSpec(
            num_scalar_prefetch=1,
            grid=(groups,),
            in_specs=[enc, enc, gkv, gkv],
            out_specs=pl.BlockSpec((step, cols), lambda i, s: (i, 0)),
        ),
        out_shape=jax.ShapeDtypeStruct((half, cols), BF16),
        cost_estimate=cost(4 * length * half * cols // 64, 0),
        compiler_params=params(32),
        name="weight_grad",
    )(at, enc_a, enc_b, gkv_a, gkv_b)


def collect_kernel(scale, at, *refs):
    terms, (raw, inv, gain, out, gain_term) = refs[:4], refs[4:]
    total = terms[0][...].astype(F32)
    for term in terms[1:]:
        total = total + term[...].astype(F32)
    out[...] = (total * gain[...]).astype(BF16)
    product = total * (raw[...].astype(F32) * inv[:, :1])
    gain_term[0] = scale * jnp.sum(product, axis=0, keepdims=True)


def collect(at, terms, raw, inv_rms, gain, scale):
    length, width = raw.shape
    step = 128
    block = pl.BlockSpec((step, width), lambda i, s: (i, 0))
    return pl.pallas_call(
        lambda *refs: collect_kernel(scale, *refs),
        grid_spec=pltpu.PrefetchScalarGridSpec(
            num_scalar_prefetch=1,
            grid=(length // step,),
            in_specs=[block] * 5
            + [
                pl.BlockSpec((step, 128), lambda i, s: (i, 0)),
                pl.BlockSpec((1, width), lambda i, s: (0, 0)),
            ],
            out_specs=[block, pl.BlockSpec((1, 1, width), lambda i, s: (i, 0, 0))],
        ),
        out_shape=[
            jax.ShapeDtypeStruct((length, width), BF16),
            jax.ShapeDtypeStruct((length // step, 1, width), F32),
        ],
        cost_estimate=cost(8 * length * width, 12),
        compiler_params=params(32),
        name="collect",
    )(at, *terms, raw, inv_rms, gain)


def enc_grad_kernel(at, gkv_0, gkv_1, own_0, own_1, other_0, other_1, out):
    rows = own_0.shape[0]
    own = dot(gkv_0[...], own_0[...], NT) + dot(gkv_1[...], own_1[...], NT)
    other = dot(gkv_0[...], other_0[...], NT) + dot(gkv_1[...], other_1[...], NT)
    first = at[3] == 0
    out[:, :rows] = jnp.where(first, own, other).astype(BF16)
    out[:, rows:] = jnp.where(first, other, own).astype(BF16)


def enc_grad(at, gkvs, owns, others, groups, rows, shard):
    length, cols = gkvs[0].shape
    per_shard = groups // 2

    def block(i, s):
        target = lax.rem(s[1] + shard, 2)
        group = target * per_shard + i // 2
        return (2 * group + lax.rem(i + s[2], 2), 0)

    gkv = pl.BlockSpec((length, cols), lambda i, s: (0, 0))
    weight = pl.BlockSpec((rows, cols), block)
    return pl.pallas_call(
        enc_grad_kernel,
        grid_spec=pltpu.PrefetchScalarGridSpec(
            num_scalar_prefetch=1,
            grid=(groups,),
            in_specs=[gkv, gkv, weight, weight, weight, weight],
            out_specs=pl.BlockSpec((length, 2 * rows), lambda i, s: (0, i)),
        ),
        out_shape=jax.ShapeDtypeStruct((length, D // 2), BF16),
        compiler_params=params(32),
        cost_estimate=cost(4 * length * D * cols, 8),
        name="enc_grad",
    )(at, *gkvs, *owns, *others)


def cut(array, axis, index, size):
    return lax.dynamic_slice_in_dim(array, index * size, size, axis)


def ordered(first, own, other, axis):
    return jnp.where(
        first, jnp.concatenate([own, other], axis), jnp.concatenate([other, own], axis)
    )


def after(value, *others):
    return lax.optimization_barrier((value,) + others)[0]


def on_device(sec_acts, gain, w_kv, src_len, tgt_len):
    groups = lax.axis_size("z")
    shards = lax.axis_size("mp")
    z, y = lax.axis_index("z"), lax.axis_index("y")
    core, x = lax.axis_index("phase"), lax.axis_index("mp")
    straight = y == core
    packed = sec_acts[0, 0]
    length, width = packed.shape
    rows = w_kv.shape[0]
    half = width // 2
    cols = half // CHUNKS
    pair_scale = 1.0 / (2 * groups)
    tiled = shards == 2 and rows % 128 == 0

    def turned(count, by):
        return [(i, (i + by) % count) for i in range(count)]

    def across(value, turn, moves):
        return lax.ppermute(
            value,
            ("y", "phase", "mp"),
            [(a * shards + s, b * shards + (s + turn) % shards) for a, b in moves for s in range(shards)],
        )

    def chunk_of(side, k):
        return lax.dynamic_slice_in_dim(w_kv, side * half + k * cols, cols, 1)

    def slots(block):
        return [lax.ppermute(block, "z", turned(groups, -s)) for s in range(1, groups)]

    mine = [chunk_of(y, k) for k in range(CHUNKS)]
    swap = lax.ppermute(cut(w_kv, 1, 1 - y, half), "y", SWAP)
    swapped = [swap[:, k * cols : (k + 1) * cols] for k in range(CHUNKS)]

    there = lax.ppermute(after(packed, swap), PLANE, [(0, 2), (2, 1)])
    here = jnp.where(y == 0, packed, lax.ppermute(packed, PLANE, [(2, 3)]))
    nears = [here, there]
    fars = []
    for turn in range(1, shards):
        fars.append(
            [across(here, turn, [(0, 0), (3, 3)]), across(there, turn, [(1, 1), (2, 2)])]
        )
    gains = [gain] + [lax.ppermute(gain, "mp", turned(shards, t)) for t in range(1, shards)]

    blocks = [jnp.concatenate([mine[k], swapped[k]], 0) for k in range(CHUNKS)]
    w_own, w_other = [], []

    position = lax.broadcasted_iota(jnp.int32, (length, width), 0)
    is_grad = lax.broadcasted_iota(jnp.int32, (length, width), 1) % (2 * HEAD) >= HEAD
    masked = jnp.where(is_grad & (position >= tgt_len[0]), jnp.zeros((), BF16), packed)
    qg_near, qg_far = cut(masked, 1, y, half), cut(masked, 1, 1 - y, half)
    qg_near, qg_far = lax.optimization_barrier((qg_near, qg_far, there))[:2]
    qgs = [
        jnp.where(y == 1, qg_near, lax.ppermute(qg_near, PLANE, [(1, 0)])),
        lax.ppermute(qg_far, PLANE, [(1, 2), (3, 1)]),
    ]
    key_count = jnp.where(straight, src_len, lax.ppermute(src_len, "y", SWAP))
    at = jnp.concatenate(
        [jnp.stack([straight.astype(jnp.int32), x, y, core]).astype(jnp.int32), key_count]
    )

    def natural(parts, axis):
        if shards == 2:
            return ordered(x == 0, parts[0], parts[1], axis)
        stacked = jnp.stack(parts)
        return jnp.concatenate(
            [
                lax.dynamic_index_in_dim(stacked, (x - i) % shards, 0, keepdims=False)
                for i in range(shards)
            ],
            axis,
        )

    block_group = jnp.arange(groups)
    block_pair = 2 * block_group[:, None] + jnp.stack([y, 1 - y])[None, :]
    block_order = (2 * block_pair[None] + jnp.stack([core, 1 - core])[:, None, None]).reshape(-1)
    gain_all = natural(gains, 0).astype(F32)

    if tiled:
        enc_own, enc_other, inv_rms = norm(
            at, nears, fars[0], after(gain_all[None], *qgs), groups, rows
        )
    else:
        raw = [jnp.where(straight, *parts) for parts in [nears] + fars]
        hidden = natural(raw, 1).astype(F32)
        inv_rms = lax.rsqrt(jnp.sum(hidden * hidden, axis=-1, keepdims=True) / D + EPS)
        encoded = (hidden * inv_rms * gain_all).astype(BF16)
        encoded = encoded.reshape(length, -1, rows)[:, block_order].reshape(length, 2, -1)
        enc_own, enc_other = encoded[:, 0], encoded[:, 1]
    enc_mate = lax.ppermute(enc_other, "phase", SWAP)

    decs, gkvs, weight_sums = [], [], []
    for k in range(CHUNKS):
        if k in DIRECT:
            pieces = [blocks[k]] + slots(after(blocks[k], w_own[0]))
            pieces = lax.optimization_barrier((*pieces, grad))[:-1]
            gathered = jnp.zeros((groups * 2 * rows, cols), BF16)
            for turn, piece in enumerate(pieces):
                start = (z + turn) % groups * 2 * rows
                gathered = lax.dynamic_update_slice_in_dim(gathered, piece, start, 0)
            w_own.append(gathered)
        else:
            block = blocks[k] if k == 0 else after(blocks[k], there)
            w_own.append(lax.all_gather(block, "z", axis=0, tiled=True))
            if k > 0:
                w_own[k] = after(w_own[k], grad)
        w_other.append(lax.ppermute(w_own[k], "phase", SWAP))
        dec, gkv = attend(at, enc_own, enc_other, w_own[k], w_other[k], qgs, k)
        gkvs.append(gkv)
        decs.append(
            (
                jnp.where(y == 0, lax.ppermute(dec, PLANE, [(0, 1)]), dec),
                lax.ppermute(dec, PLANE, [(2, 1), (1, 3)]),
            )
        )
        parts = jnp.split(gkv, 2, axis=1)
        gkv_mate = jnp.concatenate([lax.ppermute(p, "phase", SWAP) for p in parts], 1)
        if tiled:
            grad = weight_grad(at, enc_own, enc_mate, gkv, gkv_mate, groups, pair_scale)
        else:
            grad = pair_scale * (dot(enc_own, gkv, TN) + dot(enc_mate, gkv_mate, TN))
            grad = grad.astype(BF16)
        weight_sums.append(lax.psum_scatter(grad, "z", scatter_dimension=0, tiled=True))

    if tiled:
        terms = [enc_grad(at, gkvs, w_own, w_other, groups, rows, s) for s in (1, 0)][::-1]
    else:
        gkv_all = jnp.concatenate(gkvs, 1)
        full = dot(gkv_all, jnp.concatenate([jnp.concatenate(w, 0) for w in zip(w_own, w_other)], 1), NT)
        back = jnp.zeros_like(block_order).at[block_order].set(jnp.arange(block_order.shape[0]))
        full = full.astype(BF16).reshape(length, -1, rows)[:, back].reshape(length, D)
        terms = [cut(full, 1, (x + s) % shards, width) for s in range(shards)]
    moved = [across(terms[turn], turn, [(0, 0), (3, 3)]) for turn in range(1, shards)]
    moved += [across(terms[turn], turn, [(2, 0), (1, 3)]) for turn in range(shards)]

    kept = jnp.concatenate([w[:rows] for w in weight_sums], 1)
    got = [lax.ppermute(w[rows:], "y", SWAP) for w in weight_sums]
    if tiled:
        terms[0] = after(terms[0], got[0])
        grad_normed, gain_term = collect(
            at, [terms[0]] + moved, here, inv_rms, gain.astype(F32)[None], pair_scale
        )
        gain_term = jnp.sum(gain_term, axis=(0, 1))
    else:
        grad_enc = terms[0].astype(F32)
        for part in moved:
            grad_enc = grad_enc + part.astype(F32)
        grad_normed = (grad_enc * gain.astype(F32)).astype(BF16)
        normed = raw[0].astype(F32) * inv_rms
        gain_term = pair_scale * jnp.sum(grad_enc * normed, axis=0)
    enc_grads = jnp.where(y == 0, grad_normed, lax.ppermute(grad_normed, PLANE, [(3, 2)]))

    gain_term = jnp.where(straight, gain_term, 0.0)
    gain_term = gain_term + lax.ppermute(gain_term, PLANE, [(0, 3), (3, 0), (1, 2), (2, 1)])
    turn = 1
    while turn < groups:
        gain_term = gain_term + lax.ppermute(gain_term, "z", [(i, i ^ turn) for i in range(groups)])
        turn *= 2
    d_gain = jnp.where(straight, gain_term, lax.ppermute(gain_term, "phase", SWAP))
    got = jnp.concatenate(got, 1)
    d_wkv = ordered(y == 0, kept, got, 1).astype(F32)

    dec_here = jnp.concatenate([d[0] for d in decs], 1)
    dec_there = jnp.concatenate([d[1] for d in decs], 1)
    dec_grads = ordered(y == 0, dec_here, dec_there, 1)
    sec_grads = jnp.where(core == 0, enc_grads, dec_grads)[None, None]
    return (sec_grads, d_wkv, d_gain)


def solution(mesh):
    size = mesh.shape
    split = (size["dp"] // 2, 2, size["phase"], size["mp"])
    fine = Mesh(mesh.devices.reshape(split), ("z", "y", "phase", "mp"))
    pairs = ("z", "y")
    acts = P("phase", pairs, None, "mp")
    weights = P(("z", "y", "phase"), "mp")
    return jax.shard_map(
        on_device,
        mesh=fine,
        in_specs=(acts, P("mp"), weights, P(pairs), P(pairs)),
        out_specs=(acts, weights, P("mp")),
        check_vma=False,
    )
```

```python
import jax
import jax.numpy as jnp
from jax import lax
from jax.experimental import pallas as pl
from jax.experimental.pallas import tpu as pltpu
from jax.sharding import Mesh, PartitionSpec as P

D = 4096
HEAD = 64
EPS = 1e-06
CHUNKS = 2
DIRECT = ()
F32 = jnp.float32
BF16 = jnp.bfloat16
NN = (((1,), (0,)), ((), ()))
NT = (((1,), (1,)), ((), ()))
TN = (((0,), (0,)), ((), ()))

PLANE = ("y", "phase")
SWAP = [(0, 1), (1, 0)]


def dot(a, b, dims=NN):
    return lax.dot_general(a, b, dims, preferred_element_type=F32)


def cost(flops, mib, exps=0):
    return pl.CostEstimate(flops=flops, bytes_accessed=mib << 20, transcendentals=exps)


def in_hbm(*arrays):
    return [pltpu.with_memory_space_constraint(a, pltpu.HBM) for a in arrays]


def params(mib):
    return pltpu.CompilerParams(vmem_limit_bytes=mib << 20)


def norm_kernel(groups, rows, at, *refs):
    nears, fars, (gain, own, other, inv_out, natural) = refs[:2], refs[2:4], refs[4:]
    x, y, core = at[1], at[2], at[3]
    width = nears[0].shape[1]
    near = jnp.where(at[0] == 1, *[r[...] for r in nears]).astype(F32)
    far = jnp.where(at[0] == 1, *[r[...] for r in fars]).astype(F32)
    total = jnp.sum(near * near, axis=-1, keepdims=True) + jnp.sum(far * far, axis=-1, keepdims=True)
    inv_rms = lax.rsqrt(total / D + EPS)
    inv_out[...] = jnp.broadcast_to(inv_rms, inv_out.shape)
    near_at = pl.ds(pl.multiple_of(x * width, width), width)
    far_at = pl.ds(pl.multiple_of((1 - x) * width, width), width)
    natural[:, near_at] = (near * inv_rms * gain[:, near_at]).astype(BF16)
    natural[:, far_at] = (far * inv_rms * gain[:, far_at]).astype(BF16)
    for group in range(groups):
        for k in range(2):
            row = 2 * group + (y if k == 0 else 1 - y)
            put = slice((2 * group + k) * rows, (2 * group + k + 1) * rows)
            for out, half in ((own, core), (other, 1 - core)):
                got = pl.multiple_of((2 * row + half) * rows, rows)
                out[:, put] = natural[:, pl.ds(got, rows)]


def norm(at, nears, fars, gain, groups, rows):
    length, width = nears[0].shape
    step = 128

    def pick(want):
        return pl.BlockSpec((step, width), lambda i, s: (jnp.where(s[0] == want, i, 0), 0))

    out = pl.BlockSpec((step, D // 2), lambda i, s: (i, 0))
    return pl.pallas_call(
        lambda *refs: norm_kernel(groups, rows, *refs),
        grid_spec=pltpu.PrefetchScalarGridSpec(
            num_scalar_prefetch=1,
            grid=(length // step,),
            in_specs=[pick(1), pick(0), pick(1), pick(0)] + [pl.BlockSpec((1, D), lambda i, s: (0, 0))],
            out_specs=[out, out, pl.BlockSpec((step, 128), lambda i, s: (i, 0))],
            scratch_shapes=[pltpu.VMEM((step, D), BF16)],
        ),
        out_shape=[pltpu.HBM((length, D // 2), BF16)] * 2
        + [jax.ShapeDtypeStruct((length, 128), F32)],
        compiler_params=params(32),
        cost_estimate=cost(8 * length * D, 8),
        name="norm",
    )(at, *in_hbm(*nears, *fars), gain)


def attend_head(bias, qg, kv):
    low_lane = lax.broadcasted_iota(jnp.int32, qg.shape, 1) < HEAD
    zero = jnp.zeros((), BF16)
    scaled = qg * jnp.asarray(1.0 / HEAD**0.5, BF16)
    queries = jnp.where(low_lane, scaled, zero)
    grads = jnp.where(low_lane, zero, scaled)
    scores = dot(queries, kv, NT) + bias
    grad_prob = dot(grads, kv, NT)
    weights = jnp.exp(scores - jnp.max(scores, axis=-1, keepdims=True))
    probs = weights * (1.0 / jnp.sum(weights, axis=-1, keepdims=True))
    prob_low = probs.astype(BF16)
    attended = dot(prob_low, kv)
    row_delta = jnp.sum(grads.astype(F32) * attended, axis=-1, keepdims=True)
    grad_score = (probs * (grad_prob - row_delta)).astype(BF16)
    grad_query = dot(grad_score, kv)
    qg_t = qg.T
    key_t = dot(qg_t[:HEAD], grad_score)
    value_t = dot(qg_t[HEAD:], prob_low)
    gkv = jnp.concatenate([key_t, value_t], axis=0).T
    dec = jnp.where(low_lane, grad_query, pltpu.roll(gkv, HEAD, 1))
    return dec.astype(BF16), gkv.astype(BF16)


def attend_kernel(at, enc_own, enc_other, w_own, w_other, *refs):
    qgs, (dec, gkv) = refs[:2], refs[2:]
    kv = (dot(enc_own[...], w_own[...]) + dot(enc_other[...], w_other[...])).astype(BF16)
    keys = lax.broadcasted_iota(jnp.int32, (1, kv.shape[0]), 1)
    bias = jnp.where(keys < at[4], 0.0, -1e30).astype(F32)
    for head in range(kv.shape[1] // (2 * HEAD)):
        lanes = slice(head * 2 * HEAD, (head + 1) * 2 * HEAD)
        qg = jnp.where(at[0] == 1, *[r[:, lanes] for r in qgs])
        dec[:, lanes], gkv[:, lanes] = attend_head(bias, qg, kv[:, lanes])


def attend(at, enc_own, enc_other, w_own, w_other, qgs, chunk):
    length = enc_own.shape[0]
    half, cols = w_own.shape
    step = min(256, cols)
    first = chunk * (cols // step)
    enc = pl.BlockSpec((length, half), lambda i, s: (0, 0))
    weight = pl.BlockSpec((half, step), lambda i, s: (0, i))
    out = pl.BlockSpec((length, step), lambda i, s: (0, i))

    def pick(want):
        return pl.BlockSpec((length, step), lambda i, s: (0, jnp.where(s[0] == want, first + i, first)))

    return pl.pallas_call(
        attend_kernel,
        grid_spec=pltpu.PrefetchScalarGridSpec(
            num_scalar_prefetch=1,
            grid=(cols // step,),
            in_specs=[enc, enc, weight, weight, pick(1), pick(0)],
            out_specs=[out, out],
        ),
        out_shape=[pltpu.HBM((length, cols), BF16)] * 2,
        compiler_params=params(48),
        cost_estimate=cost(
            length * cols * (4 * half + 14 * length), 8, length * length * cols // (2 * HEAD)
        ),
        name="attend",
    )(at, *in_hbm(enc_own, enc_other, w_own, w_other, *qgs))


def weight_grad_kernel(scale, at, enc_a, enc_b, gkv_a, gkv_b, out):
    grad = scale * (dot(enc_a[...], gkv_a[...], TN) + dot(enc_b[...], gkv_b[...], TN))
    out[...] = grad.astype(BF16)


def weight_grad(at, enc_a, enc_b, gkv_a, gkv_b, groups, scale):
    length, half = enc_a.shape
    cols = gkv_a.shape[1]
    step = half // groups
    enc = pl.BlockSpec((length, step), lambda i, s: (0, i))
    gkv = pl.BlockSpec((length, cols), lambda i, s: (0, 0))
    return pl.pallas_call(
        lambda *refs: weight_grad_kernel(scale, *refs),
        grid_spec=pltpu.PrefetchScalarGridSpec(
            num_scalar_prefetch=1,
            grid=(groups,),
            in_specs=[enc, enc, gkv, gkv],
            out_specs=pl.BlockSpec((step, cols), lambda i, s: (i, 0)),
        ),
        out_shape=pltpu.HBM((half, cols), BF16),
        cost_estimate=cost(4 * length * half * cols // 64, 0),
        compiler_params=params(32),
        name="weight_grad",
    )(at, *in_hbm(enc_a, enc_b, gkv_a, gkv_b))


def collect_kernel(scale, at, *refs):
    terms, (raw, inv, gain, out, gain_term) = refs[:4], refs[4:]
    total = terms[0][...].astype(F32)
    for term in terms[1:]:
        total = total + term[...].astype(F32)
    out[...] = (total * gain[...]).astype(BF16)
    product = total * (raw[...].astype(F32) * inv[:, :1])
    gain_term[0] = scale * jnp.sum(product, axis=0, keepdims=True)


def collect(at, terms, raw, inv_rms, gain, scale):
    length, width = raw.shape
    step = 128
    block = pl.BlockSpec((step, width), lambda i, s: (i, 0))
    return pl.pallas_call(
        lambda *refs: collect_kernel(scale, *refs),
        grid_spec=pltpu.PrefetchScalarGridSpec(
            num_scalar_prefetch=1,
            grid=(length // step,),
            in_specs=[block] * 5
            + [
                pl.BlockSpec((step, 128), lambda i, s: (i, 0)),
                pl.BlockSpec((1, width), lambda i, s: (0, 0)),
            ],
            out_specs=[block, pl.BlockSpec((1, 1, width), lambda i, s: (i, 0, 0))],
        ),
        out_shape=[
            jax.ShapeDtypeStruct((length, width), BF16),
            jax.ShapeDtypeStruct((length // step, 1, width), F32),
        ],
        cost_estimate=cost(8 * length * width, 12),
        compiler_params=params(32),
        name="collect",
    )(at, *in_hbm(*terms, raw), inv_rms, gain)


def enc_grad_kernel(at, gkv_0, gkv_1, own_0, own_1, other_0, other_1, out):
    rows = own_0.shape[0]
    own = dot(gkv_0[...], own_0[...], NT) + dot(gkv_1[...], own_1[...], NT)
    other = dot(gkv_0[...], other_0[...], NT) + dot(gkv_1[...], other_1[...], NT)
    first = at[3] == 0
    out[:, :rows] = jnp.where(first, own, other).astype(BF16)
    out[:, rows:] = jnp.where(first, other, own).astype(BF16)


def enc_grad(at, gkvs, owns, others, groups, rows, shard):
    length, cols = gkvs[0].shape
    per_shard = groups // 2

    def block(i, s):
        target = lax.rem(s[1] + shard, 2)
        group = target * per_shard + i // 2
        return (2 * group + lax.rem(i + s[2], 2), 0)

    gkv = pl.BlockSpec((length, cols), lambda i, s: (0, 0))
    weight = pl.BlockSpec((rows, cols), block)
    return pl.pallas_call(
        enc_grad_kernel,
        grid_spec=pltpu.PrefetchScalarGridSpec(
            num_scalar_prefetch=1,
            grid=(groups,),
            in_specs=[gkv, gkv, weight, weight, weight, weight],
            out_specs=pl.BlockSpec((length, 2 * rows), lambda i, s: (0, i)),
        ),
        out_shape=pltpu.HBM((length, D // 2), BF16),
        compiler_params=params(32),
        cost_estimate=cost(4 * length * D * cols, 8),
        name="enc_grad",
    )(at, *in_hbm(*gkvs, *owns, *others))


def cut(array, axis, index, size):
    return lax.dynamic_slice_in_dim(array, index * size, size, axis)


def ordered(first, own, other, axis):
    return jnp.where(
        first, jnp.concatenate([own, other], axis), jnp.concatenate([other, own], axis)
    )


def after(value, *others):
    return lax.optimization_barrier((value,) + others)[0]


def on_device(sec_acts, gain, w_kv, src_len, tgt_len):
    groups = lax.axis_size("z")
    shards = lax.axis_size("mp")
    z, y = lax.axis_index("z"), lax.axis_index("y")
    core, x = lax.axis_index("phase"), lax.axis_index("mp")
    straight = y == core
    packed = sec_acts[0, 0]
    length, width = packed.shape
    rows = w_kv.shape[0]
    half = width // 2
    cols = half // CHUNKS
    pair_scale = 1.0 / (2 * groups)
    tiled = shards == 2 and rows % 128 == 0

    def turned(count, by):
        return [(i, (i + by) % count) for i in range(count)]

    def across(value, turn, moves):
        return lax.ppermute(
            value,
            ("y", "phase", "mp"),
            [(a * shards + s, b * shards + (s + turn) % shards) for a, b in moves for s in range(shards)],
        )

    def chunk_of(side, k):
        return lax.dynamic_slice_in_dim(w_kv, side * half + k * cols, cols, 1)

    def slots(block):
        return [lax.ppermute(block, "z", turned(groups, -s)) for s in range(1, groups)]

    gains = [gain] + [lax.ppermute(gain, "mp", turned(shards, t)) for t in range(1, shards)]
    key_count = jnp.where(straight, src_len, lax.ppermute(src_len, "y", SWAP))

    here = jnp.where(y == 0, packed, lax.ppermute(packed, PLANE, [(2, 3)]))
    swapped = [lax.ppermute(chunk_of(1 - y, 0), "y", SWAP)]
    there = after(packed, swapped[0], key_count, here, *gains)
    there = lax.ppermute(there, PLANE, [(0, 2), (2, 1)])
    for k in range(1, CHUNKS):
        swapped.append(lax.ppermute(after(chunk_of(1 - y, k), there), "y", SWAP))
    nears = [here, there]
    fars = []
    for turn in range(1, shards):
        fars.append(
            [across(here, turn, [(0, 0), (3, 3)]), across(there, turn, [(1, 1), (2, 2)])]
        )
    blocks = [jnp.concatenate([chunk_of(y, k), swapped[k]], 0) for k in range(CHUNKS)]
    w_own, w_other = [], []

    position = lax.broadcasted_iota(jnp.int32, (length, width), 0)
    is_grad = lax.broadcasted_iota(jnp.int32, (length, width), 1) % (2 * HEAD) >= HEAD
    masked = jnp.where(is_grad & (position >= tgt_len[0]), jnp.zeros((), BF16), packed)
    qg_near, qg_far = cut(masked, 1, y, half), cut(masked, 1, 1 - y, half)
    qg_near, qg_far = lax.optimization_barrier((qg_near, qg_far, there))[:2]
    qgs = [
        jnp.where(y == 1, qg_near, lax.ppermute(qg_near, PLANE, [(1, 0)])),
        lax.ppermute(qg_far, PLANE, [(1, 2), (3, 1)]),
    ]
    at = jnp.concatenate(
        [jnp.stack([straight.astype(jnp.int32), x, y, core]).astype(jnp.int32), key_count]
    )

    def natural(parts, axis):
        if shards == 2:
            return ordered(x == 0, parts[0], parts[1], axis)
        stacked = jnp.stack(parts)
        return jnp.concatenate(
            [
                lax.dynamic_index_in_dim(stacked, (x - i) % shards, 0, keepdims=False)
                for i in range(shards)
            ],
            axis,
        )

    block_group = jnp.arange(groups)
    block_pair = 2 * block_group[:, None] + jnp.stack([y, 1 - y])[None, :]
    block_order = (2 * block_pair[None] + jnp.stack([core, 1 - core])[:, None, None]).reshape(-1)
    gain_all = natural(gains, 0).astype(F32)

    if tiled:
        enc_own, enc_other, inv_rms = norm(
            at, nears, fars[0], after(gain_all[None], *qgs, *blocks), groups, rows
        )
    else:
        raw = [jnp.where(straight, *parts) for parts in [nears] + fars]
        hidden = natural(raw, 1).astype(F32)
        inv_rms = lax.rsqrt(jnp.sum(hidden * hidden, axis=-1, keepdims=True) / D + EPS)
        encoded = (hidden * inv_rms * gain_all).astype(BF16)
        encoded = encoded.reshape(length, -1, rows)[:, block_order].reshape(length, 2, -1)
        enc_own, enc_other = encoded[:, 0], encoded[:, 1]
    enc_mate = lax.ppermute(enc_other, "phase", SWAP)

    decs, gkvs, weight_sums = [], [], []
    for k in range(CHUNKS):
        if k in DIRECT:
            pieces = [blocks[k]] + slots(after(blocks[k], w_own[0]))
            pieces = lax.optimization_barrier((*pieces, grad))[:-1]
            gathered = jnp.zeros((groups * 2 * rows, cols), BF16)
            for turn, piece in enumerate(pieces):
                start = (z + turn) % groups * 2 * rows
                gathered = lax.dynamic_update_slice_in_dim(gathered, piece, start, 0)
            w_own.append(gathered)
        else:
            block = blocks[k]
            w_own.append(lax.all_gather(block, "z", axis=0, tiled=True))
            if k > 0:
                w_own[k] = after(w_own[k], grad)
        w_other.append(lax.ppermute(w_own[k], "phase", SWAP))
        dec, gkv = attend(at, enc_own, enc_other, w_own[k], w_other[k], qgs, k)
        gkvs.append(gkv)
        decs.append(
            (
                jnp.where(y == 0, lax.ppermute(dec, PLANE, [(0, 1)]), dec),
                lax.ppermute(dec, PLANE, [(2, 1), (1, 3)]),
            )
        )
        parts = jnp.split(gkv, 2, axis=1)
        gkv_mate = jnp.concatenate([lax.ppermute(p, "phase", SWAP) for p in parts], 1)
        if tiled:
            if k == CHUNKS - 1:
                terms = [enc_grad(at, gkvs, w_own, w_other, groups, rows, s) for s in (1, 0)][::-1]
                gkv_mate = after(gkv_mate, *terms)
            grad = weight_grad(at, enc_own, enc_mate, gkv, gkv_mate, groups, pair_scale)
        else:
            grad = pair_scale * (dot(enc_own, gkv, TN) + dot(enc_mate, gkv_mate, TN))
            grad = grad.astype(BF16)
        weight_sums.append(lax.psum_scatter(grad, "z", scatter_dimension=0, tiled=True))

    if not tiled:
        gkv_all = jnp.concatenate(gkvs, 1)
        full = dot(gkv_all, jnp.concatenate([jnp.concatenate(w, 0) for w in zip(w_own, w_other)], 1), NT)
        back = jnp.zeros_like(block_order).at[block_order].set(jnp.arange(block_order.shape[0]))
        full = full.astype(BF16).reshape(length, -1, rows)[:, back].reshape(length, D)
        terms = [cut(full, 1, (x + s) % shards, width) for s in range(shards)]
    moved = [across(terms[turn], turn, [(0, 0), (3, 3)]) for turn in range(1, shards)]
    moved += [across(terms[turn], turn, [(2, 0), (1, 3)]) for turn in range(shards)]

    dec_here = jnp.concatenate([d[0] for d in decs], 1)
    dec_there = jnp.concatenate([d[1] for d in decs], 1)
    dec_grads = ordered(y == 0, dec_here, dec_there, 1)
    kept = jnp.concatenate([w[:rows] for w in weight_sums], 1)
    got = [lax.ppermute(w[rows:], "y", SWAP) for w in weight_sums]
    got = jnp.concatenate(got, 1)
    d_wkv = ordered(y == 0, kept, got, 1).astype(F32)
    if tiled:
        terms[0], d_wkv, dec_grads = lax.optimization_barrier((terms[0], d_wkv, dec_grads))
        grad_normed, gain_term = collect(
            at, [terms[0]] + moved, here, inv_rms, gain.astype(F32)[None], pair_scale
        )
        gain_term = jnp.sum(gain_term, axis=(0, 1))
    else:
        grad_enc = terms[0].astype(F32)
        for part in moved:
            grad_enc = grad_enc + part.astype(F32)
        grad_normed = (grad_enc * gain.astype(F32)).astype(BF16)
        normed = raw[0].astype(F32) * inv_rms
        gain_term = pair_scale * jnp.sum(grad_enc * normed, axis=0)
    enc_grads = jnp.where(y == 0, grad_normed, lax.ppermute(grad_normed, PLANE, [(3, 2)]))

    gain_term = jnp.where(straight, gain_term, 0.0)
    gain_term = gain_term + lax.ppermute(gain_term, PLANE, [(0, 3), (3, 0), (1, 2), (2, 1)])
    turn = 1
    while turn < groups:
        gain_term = gain_term + lax.ppermute(gain_term, "z", [(i, i ^ turn) for i in range(groups)])
        turn *= 2
    d_gain = jnp.where(straight, gain_term, lax.ppermute(gain_term, "phase", SWAP))

    sec_grads = jnp.where(core == 0, enc_grads, dec_grads)[None, None]
    return (sec_grads, d_wkv, d_gain)


def solution(mesh):
    size = mesh.shape
    split = (size["dp"] // 2, 2, size["phase"], size["mp"])
    fine = Mesh(mesh.devices.reshape(split), ("z", "y", "phase", "mp"))
    pairs = ("z", "y")
    acts = P("phase", pairs, None, "mp")
    weights = P(("z", "y", "phase"), "mp")
    return jax.shard_map(
        on_device,
        mesh=fine,
        in_specs=(acts, P("mp"), weights, P(pairs), P(pairs)),
        out_specs=(acts, weights, P("mp")),
        check_vma=False,
    )
```

```python
import jax
import jax.numpy as jnp
from jax import lax
from jax.experimental import pallas as pl
from jax.experimental.pallas import tpu as pltpu
from jax.sharding import Mesh, PartitionSpec as P

D = 4096
HEAD = 64
EPS = 1e-06
CHUNKS = 2
DIRECT = ()
F32 = jnp.float32
BF16 = jnp.bfloat16
NN = (((1,), (0,)), ((), ()))
NT = (((1,), (1,)), ((), ()))
TN = (((0,), (0,)), ((), ()))

PLANE = ("y", "phase")
SWAP = [(0, 1), (1, 0)]


def dot(a, b, dims=NN):
    return lax.dot_general(a, b, dims, preferred_element_type=F32)


def cost(flops, mib, exps=0):
    return pl.CostEstimate(flops=flops, bytes_accessed=mib << 20, transcendentals=exps)


def in_hbm(*arrays):
    return [pltpu.with_memory_space_constraint(a, pltpu.HBM) for a in arrays]


def params(mib):
    return pltpu.CompilerParams(vmem_limit_bytes=mib << 20)


def chosen(kind, *values):
    return jnp.where(kind == 0, values[0], jnp.where(kind == 1, values[1], values[2]))


def norm_kernel(groups, rows, at, *refs):
    nears, fars, (gain, own, other, inv_out, natural) = refs[:3], refs[3:6], refs[6:]
    x, y, core = at[1], at[2], at[3]
    width = nears[0].shape[1]
    near = chosen(at[0], *[r[...] for r in nears]).astype(F32)
    far = chosen(at[0], *[r[...] for r in fars]).astype(F32)
    total = jnp.sum(near * near, axis=-1, keepdims=True) + jnp.sum(far * far, axis=-1, keepdims=True)
    inv_rms = lax.rsqrt(total / D + EPS)
    inv_out[...] = jnp.broadcast_to(inv_rms, inv_out.shape)
    near_at = pl.ds(pl.multiple_of(x * width, width), width)
    far_at = pl.ds(pl.multiple_of((1 - x) * width, width), width)
    natural[:, near_at] = (near * inv_rms * gain[:, near_at]).astype(BF16)
    natural[:, far_at] = (far * inv_rms * gain[:, far_at]).astype(BF16)
    for group in range(groups):
        for k in range(2):
            row = 2 * group + (y if k == 0 else 1 - y)
            put = slice((2 * group + k) * rows, (2 * group + k + 1) * rows)
            for out, half in ((own, core), (other, 1 - core)):
                got = pl.multiple_of((2 * row + half) * rows, rows)
                out[:, put] = natural[:, pl.ds(got, rows)]


def norm(at, nears, fars, gain, groups, rows):
    length, width = nears[0].shape
    step = 128

    def pick(want):
        return pl.BlockSpec((step, width), lambda i, s: (jnp.where(s[0] == want, i, 0), 0))

    out = pl.BlockSpec((step, D // 2), lambda i, s: (i, 0))
    return pl.pallas_call(
        lambda *refs: norm_kernel(groups, rows, *refs),
        grid_spec=pltpu.PrefetchScalarGridSpec(
            num_scalar_prefetch=1,
            grid=(length // step,),
            in_specs=[pick(i % 3) for i in range(6)] + [pl.BlockSpec((1, D), lambda i, s: (0, 0))],
            out_specs=[out, out, pl.BlockSpec((step, 128), lambda i, s: (i, 0))],
            scratch_shapes=[pltpu.VMEM((step, D), BF16)],
        ),
        out_shape=[pltpu.HBM((length, D // 2), BF16)] * 2
        + [jax.ShapeDtypeStruct((length, 128), F32)],
        compiler_params=params(14),
        cost_estimate=cost(8 * length * D, 8),
        name="norm",
    )(at, *nears, *fars, gain)


def attend_head(bias, qg, kv):
    low_lane = lax.broadcasted_iota(jnp.int32, qg.shape, 1) < HEAD
    zero = jnp.zeros((), BF16)
    scaled = qg * jnp.asarray(1.0 / HEAD**0.5, BF16)
    queries = jnp.where(low_lane, scaled, zero)
    grads = jnp.where(low_lane, zero, scaled)
    scores = dot(queries, kv, NT) + bias
    grad_prob = dot(grads, kv, NT)
    weights = jnp.exp(scores - jnp.max(scores, axis=-1, keepdims=True))
    probs = weights * (1.0 / jnp.sum(weights, axis=-1, keepdims=True))
    prob_low = probs.astype(BF16)
    row_delta = jnp.sum(prob_low.astype(F32) * grad_prob, axis=-1, keepdims=True)
    grad_score = (probs * (grad_prob - row_delta)).astype(BF16)
    grad_query = dot(grad_score, kv)
    qg_t = qg.T
    key_t = dot(qg_t[:HEAD], grad_score)
    value_t = dot(qg_t[HEAD:], prob_low)
    gkv = jnp.concatenate([key_t, value_t], axis=0).T
    dec = jnp.where(low_lane, grad_query, pltpu.roll(gkv, HEAD, 1))
    return dec.astype(BF16), gkv.astype(BF16)


def attend_kernel(at, enc_own, enc_other, w_own, w_other, *refs):
    qgs, (dec, gkv) = refs[:3], refs[3:]
    kv = (dot(enc_own[...], w_own[...]) + dot(enc_other[...], w_other[...])).astype(BF16)
    keys = lax.broadcasted_iota(jnp.int32, (1, kv.shape[0]), 1)
    bias = jnp.where(keys < at[4], 0.0, -1e30).astype(F32)
    for head in range(kv.shape[1] // (2 * HEAD)):
        lanes = slice(head * 2 * HEAD, (head + 1) * 2 * HEAD)
        qg = chosen(at[5], *[r[:, lanes] for r in qgs])
        dec[:, lanes], gkv[:, lanes] = attend_head(bias, qg, kv[:, lanes])


def attend(at, enc_own, enc_other, w_own, w_other, qgs, chunk):
    length = enc_own.shape[0]
    half, cols = w_own.shape
    step = min(256, cols)
    first = chunk * (cols // step)
    enc = pl.BlockSpec((length, half), lambda i, s: (0, 0))
    weight = pl.BlockSpec((half, step), lambda i, s: (0, i))
    out = pl.BlockSpec((length, step), lambda i, s: (0, i))

    def pick(want):
        return pl.BlockSpec((length, step), lambda i, s: (0, jnp.where(s[5] == want, first + i, first)))

    return pl.pallas_call(
        attend_kernel,
        grid_spec=pltpu.PrefetchScalarGridSpec(
            num_scalar_prefetch=1,
            grid=(cols // step,),
            in_specs=[enc, enc, weight, weight, pick(0), pick(1), pick(2)],
            out_specs=[out, out],
        ),
        out_shape=[jax.ShapeDtypeStruct((length, cols), BF16)] * 2,
        compiler_params=params(26),
        cost_estimate=cost(
            length * cols * (4 * half + 14 * length), 8, length * length * cols // (2 * HEAD)
        ),
        name="attend",
    )(at, *in_hbm(enc_own, enc_other, w_own, w_other, *qgs))


def weight_grad_kernel(scale, at, enc_a, enc_b, gkv_a, gkv_b, out):
    grad = scale * (dot(enc_a[...], gkv_a[...], TN) + dot(enc_b[...], gkv_b[...], TN))
    out[...] = grad.astype(BF16)


def weight_grad(at, enc_a, enc_b, gkv_a, gkv_b, groups, scale):
    length, half = enc_a.shape
    cols = gkv_a.shape[1]
    step = half // groups
    enc = pl.BlockSpec((length, step), lambda i, s: (0, i))
    gkv = pl.BlockSpec((length, cols), lambda i, s: (0, 0))
    return pl.pallas_call(
        lambda *refs: weight_grad_kernel(scale, *refs),
        grid_spec=pltpu.PrefetchScalarGridSpec(
            num_scalar_prefetch=1,
            grid=(groups,),
            in_specs=[enc, enc, gkv, gkv],
            out_specs=pl.BlockSpec((step, cols), lambda i, s: (i, 0)),
        ),
        out_shape=pltpu.HBM((half, cols), BF16),
        cost_estimate=cost(4 * length * half * cols // 64, 0),
        compiler_params=params(12),
        name="weight_grad",
    )(at, *in_hbm(enc_a, enc_b), gkv_a, gkv_b)


def collect_kernel(scale, at, *refs):
    terms, (local, here, inv, gain, out, gain_term) = refs[:3], refs[3:]
    total = terms[0][...].astype(F32)
    for term in terms[1:]:
        total = total + term[...].astype(F32)
    out[...] = (total * gain[...]).astype(BF16)
    raw = jnp.where(at[0] == 0, local[...], here[...]).astype(F32)
    product = total * (raw * inv[:, :1])
    gain_term[0] = scale * jnp.sum(product, axis=0, keepdims=True)


def collect(at, terms, local, here, inv_rms, gain, scale):
    length, width = local.shape
    step = 128
    block = pl.BlockSpec((step, width), lambda i, s: (i, 0))

    def pick(want):
        return pl.BlockSpec((step, width), lambda i, s: (jnp.where(s[0] == want, i, 0), 0))

    return pl.pallas_call(
        lambda *refs: collect_kernel(scale, *refs),
        grid_spec=pltpu.PrefetchScalarGridSpec(
            num_scalar_prefetch=1,
            grid=(length // step,),
            in_specs=[block] * 3
            + [pick(0), pick(1)]
            + [
                pl.BlockSpec((step, 128), lambda i, s: (i, 0)),
                pl.BlockSpec((1, width), lambda i, s: (0, 0)),
            ],
            out_specs=[block, pl.BlockSpec((1, 1, width), lambda i, s: (i, 0, 0))],
        ),
        out_shape=[
            jax.ShapeDtypeStruct((length, width), BF16),
            jax.ShapeDtypeStruct((length // step, 1, width), F32),
        ],
        cost_estimate=cost(8 * length * width, 12),
        compiler_params=params(16),
        name="collect",
    )(at, *terms, local, here, inv_rms, gain)


def enc_grad_kernel(at, gkv_0, gkv_1, own_0, own_1, other_0, other_1, out):
    rows = own_0.shape[0]
    own = dot(gkv_0[...], own_0[...], NT) + dot(gkv_1[...], own_1[...], NT)
    other = dot(gkv_0[...], other_0[...], NT) + dot(gkv_1[...], other_1[...], NT)
    first = at[3] == 0
    out[:, :rows] = jnp.where(first, own, other).astype(BF16)
    out[:, rows:] = jnp.where(first, other, own).astype(BF16)


def enc_grad(at, gkvs, owns, others, groups, rows, shard):
    length, cols = gkvs[0].shape
    per_shard = groups // 2

    def block(i, s):
        target = lax.rem(s[1] + shard, 2)
        group = target * per_shard + i // 2
        return (2 * group + lax.rem(i + s[2], 2), 0)

    gkv = pl.BlockSpec((length, cols), lambda i, s: (0, 0))
    weight = pl.BlockSpec((rows, cols), block)
    return pl.pallas_call(
        enc_grad_kernel,
        grid_spec=pltpu.PrefetchScalarGridSpec(
            num_scalar_prefetch=1,
            grid=(groups,),
            in_specs=[gkv, gkv, weight, weight, weight, weight],
            out_specs=pl.BlockSpec((length, 2 * rows), lambda i, s: (0, i)),
        ),
        out_shape=pltpu.HBM((length, D // 2), BF16),
        compiler_params=params(12),
        cost_estimate=cost(4 * length * D * cols, 8),
        name="enc_grad",
    )(at, *in_hbm(*gkvs, *owns, *others))


def cut(array, axis, index, size):
    return lax.dynamic_slice_in_dim(array, index * size, size, axis)


def ordered(first, own, other, axis):
    return jnp.where(
        first, jnp.concatenate([own, other], axis), jnp.concatenate([other, own], axis)
    )


def after(value, *others):
    return lax.optimization_barrier((value,) + others)[0]


def on_device(sec_acts, gain, w_kv, src_len, tgt_len):
    groups = lax.axis_size("z")
    shards = lax.axis_size("mp")
    z, y = lax.axis_index("z"), lax.axis_index("y")
    core, x = lax.axis_index("phase"), lax.axis_index("mp")
    straight = y == core
    packed = sec_acts[0, 0]
    length, width = packed.shape
    rows = w_kv.shape[0]
    half = width // 2
    cols = half // CHUNKS
    pair_scale = 1.0 / (2 * groups)
    tiled = shards == 2 and rows % 128 == 0

    def turned(count, by):
        return [(i, (i + by) % count) for i in range(count)]

    def across(value, turn, moves):
        return lax.ppermute(
            value,
            ("y", "phase", "mp"),
            [(a * shards + s, b * shards + (s + turn) % shards) for a, b in moves for s in range(shards)],
        )

    def chunk_of(side, k):
        return lax.dynamic_slice_in_dim(w_kv, side * half + k * cols, cols, 1)

    def slots(block):
        return [lax.ppermute(block, "z", turned(groups, -s)) for s in range(1, groups)]

    swapped = [lax.ppermute(chunk_of(1 - y, 0), "y", SWAP)]
    here = lax.ppermute(packed, PLANE, [(2, 3)])
    gain_sent, len_sent = lax.optimization_barrier((gain, src_len, here))[:2]
    gains = [gain] + [lax.ppermute(gain_sent, "mp", turned(shards, t)) for t in range(1, shards)]
    key_count = jnp.where(straight, src_len, lax.ppermute(len_sent, "y", SWAP))
    there = lax.ppermute(after(packed, swapped[0], key_count, *gains), PLANE, [(0, 2), (2, 1)])
    for k in range(1, CHUNKS):
        swapped.append(lax.ppermute(after(chunk_of(1 - y, k), there), "y", SWAP))
    nears = [packed, here, there]
    fars = []
    for turn in range(1, shards):
        fars.append(
            [
                across(packed, turn, [(0, 0)]),
                across(here, turn, [(3, 3)]),
                across(there, turn, [(1, 1), (2, 2)]),
            ]
        )
    blocks = [jnp.concatenate([chunk_of(y, k), swapped[k]], 0) for k in range(CHUNKS)]
    w_own, w_other = [], []

    position = lax.broadcasted_iota(jnp.int32, (length, width), 0)
    is_grad = lax.broadcasted_iota(jnp.int32, (length, width), 1) % (2 * HEAD) >= HEAD
    masked = jnp.where(is_grad & (position >= tgt_len[0]), jnp.zeros((), BF16), packed)
    qg_near, qg_far = cut(masked, 1, y, half), cut(masked, 1, 1 - y, half)
    qg_near, qg_far = lax.optimization_barrier((qg_near, qg_far, there))[:2]
    qgs = [
        qg_near,
        lax.ppermute(qg_near, PLANE, [(1, 0)]),
        lax.ppermute(qg_far, PLANE, [(1, 2), (3, 1)]),
    ]
    enc_kind = jnp.where(straight, y, 2)
    qg_kind = jnp.where(straight, 1 - y, 2)
    at = jnp.concatenate(
        [jnp.stack([enc_kind, x, y, core]).astype(jnp.int32), key_count, qg_kind[None]]
    )

    def natural(parts, axis):
        if shards == 2:
            return ordered(x == 0, parts[0], parts[1], axis)
        stacked = jnp.stack(parts)
        return jnp.concatenate(
            [
                lax.dynamic_index_in_dim(stacked, (x - i) % shards, 0, keepdims=False)
                for i in range(shards)
            ],
            axis,
        )

    block_group = jnp.arange(groups)
    block_pair = 2 * block_group[:, None] + jnp.stack([y, 1 - y])[None, :]
    block_order = (2 * block_pair[None] + jnp.stack([core, 1 - core])[:, None, None]).reshape(-1)
    gain_all = natural(gains, 0).astype(F32)

    if tiled:
        enc_own, enc_other, inv_rms = norm(
            at, nears, fars[0], after(gain_all[None], *qgs, *blocks), groups, rows
        )
    else:
        raw = [chosen(enc_kind, *parts) for parts in [nears] + fars]
        hidden = natural(raw, 1).astype(F32)
        inv_rms = lax.rsqrt(jnp.sum(hidden * hidden, axis=-1, keepdims=True) / D + EPS)
        encoded = (hidden * inv_rms * gain_all).astype(BF16)
        encoded = encoded.reshape(length, -1, rows)[:, block_order].reshape(length, 2, -1)
        enc_own, enc_other = encoded[:, 0], encoded[:, 1]
    enc_mate = lax.ppermute(enc_other, "phase", SWAP)

    decs, gkvs, weight_sums = [], [], []
    for k in range(CHUNKS):
        if k in DIRECT:
            pieces = [blocks[k]] + slots(after(blocks[k], w_own[0]))
            pieces = lax.optimization_barrier((*pieces, grad))[:-1]
            gathered = jnp.zeros((groups * 2 * rows, cols), BF16)
            for turn, piece in enumerate(pieces):
                start = (z + turn) % groups * 2 * rows
                gathered = lax.dynamic_update_slice_in_dim(gathered, piece, start, 0)
            w_own.append(gathered)
        else:
            block = blocks[k]
            w_own.append(lax.all_gather(block, "z", axis=0, tiled=True))
            if k > 0:
                w_own[k] = after(w_own[k], grad)
        w_other.append(lax.ppermute(w_own[k], "phase", SWAP))
        dec, gkv = attend(at, enc_own, enc_other, w_own[k], w_other[k], qgs, k)
        gkvs.append(gkv)
        decs.append(
            (
                lax.ppermute(dec, PLANE, [(0, 1)]),
                dec,
                lax.ppermute(dec, PLANE, [(2, 1), (1, 3)]),
            )
        )
        if tiled and k == CHUNKS - 1:
            terms = [enc_grad(at, gkvs, w_own, w_other, groups, rows, s) for s in (1, 0)][::-1]
            gkv_sent = after(gkv, *terms)
        else:
            gkv_sent = gkv
        parts = jnp.split(gkv_sent, 2, axis=1)
        gkv_mate = jnp.concatenate([lax.ppermute(p, "phase", SWAP) for p in parts], 1)
        if tiled:
            grad = weight_grad(at, enc_own, enc_mate, gkv, gkv_mate, groups, pair_scale)
        else:
            grad = pair_scale * (dot(enc_own, gkv, TN) + dot(enc_mate, gkv_mate, TN))
            grad = grad.astype(BF16)
        weight_sums.append(lax.psum_scatter(grad, "z", scatter_dimension=0, tiled=True))

    if not tiled:
        gkv_all = jnp.concatenate(gkvs, 1)
        full = dot(gkv_all, jnp.concatenate([jnp.concatenate(w, 0) for w in zip(w_own, w_other)], 1), NT)
        back = jnp.zeros_like(block_order).at[block_order].set(jnp.arange(block_order.shape[0]))
        full = full.astype(BF16).reshape(length, -1, rows)[:, back].reshape(length, D)
        terms = [cut(full, 1, (x + s) % shards, width) for s in range(shards)]
    far_terms = terms[0].astype(F32)
    for turn in range(1, shards):
        far_terms = far_terms + across(terms[turn], turn, [(1, 1), (2, 2)]).astype(F32)
    moved = [across(terms[turn], turn, [(0, 0), (3, 3)]) for turn in range(1, shards)]
    moved.append(lax.ppermute(far_terms.astype(BF16), PLANE, [(2, 0), (1, 3)]))

    dec_here = jnp.concatenate([jnp.where(y == 0, d[0], d[1]) for d in decs], 1)
    dec_there = jnp.concatenate([d[2] for d in decs], 1)
    dec_grads = ordered(y == 0, dec_here, dec_there, 1)
    kept = jnp.concatenate([w[:rows] for w in weight_sums], 1)
    got = [lax.ppermute(w[rows:], "y", SWAP) for w in weight_sums]
    got = jnp.concatenate(got, 1)
    d_wkv = ordered(y == 0, kept, got, 1).astype(F32)
    if tiled:
        grad_normed, gain_term = collect(
            at, [terms[0]] + moved, packed, here, inv_rms, gain.astype(F32)[None], pair_scale
        )
        gain_term = jnp.sum(gain_term, axis=(0, 1))
    else:
        grad_enc = terms[0].astype(F32)
        for part in moved:
            grad_enc = grad_enc + part.astype(F32)
        grad_normed = (grad_enc * gain.astype(F32)).astype(BF16)
        normed = raw[0].astype(F32) * inv_rms
        gain_term = pair_scale * jnp.sum(grad_enc * normed, axis=0)
    enc_grads = jnp.where(y == 0, grad_normed, lax.ppermute(grad_normed, PLANE, [(3, 2)]))

    gain_term = jnp.where(straight, gain_term, 0.0)
    gain_term = gain_term + lax.ppermute(gain_term, PLANE, [(0, 3), (3, 0), (1, 2), (2, 1)])
    turn = 1
    while turn < groups:
        gain_term = gain_term + lax.ppermute(gain_term, "z", [(i, i ^ turn) for i in range(groups)])
        turn *= 2
    d_gain = jnp.where(straight, gain_term, lax.ppermute(gain_term, "phase", SWAP))

    sec_grads = jnp.where(core == 0, enc_grads, dec_grads)[None, None]
    return (sec_grads, d_wkv, d_gain)


def solution(mesh):
    size = mesh.shape
    split = (size["dp"] // 2, 2, size["phase"], size["mp"])
    fine = Mesh(mesh.devices.reshape(split), ("z", "y", "phase", "mp"))
    pairs = ("z", "y")
    acts = P("phase", pairs, None, "mp")
    weights = P(("z", "y", "phase"), "mp")
    return jax.shard_map(
        on_device,
        mesh=fine,
        in_specs=(acts, P("mp"), weights, P(pairs), P(pairs)),
        out_specs=(acts, weights, P("mp")),
        check_vma=False,
    )
```

```python
import jax
import jax.numpy as jnp
from jax import lax
from jax.experimental import pallas as pl
from jax.experimental.pallas import tpu as pltpu
from jax.sharding import Mesh, PartitionSpec as P

D = 4096
HEAD = 64
EPS = 1e-06
CHUNKS = 2
DIRECT = ()
F32 = jnp.float32
BF16 = jnp.bfloat16
NN = (((1,), (0,)), ((), ()))
NT = (((1,), (1,)), ((), ()))
TN = (((0,), (0,)), ((), ()))

PLANE = ("y", "phase")
SWAP = [(0, 1), (1, 0)]


def dot(a, b, dims=NN):
    return lax.dot_general(a, b, dims, preferred_element_type=F32)


def cost(flops, mib, exps=0):
    return pl.CostEstimate(flops=flops, bytes_accessed=mib << 20, transcendentals=exps)


def in_hbm(*arrays):
    return [pltpu.with_memory_space_constraint(a, pltpu.HBM) for a in arrays]


def params(mib):
    return pltpu.CompilerParams(vmem_limit_bytes=mib << 20)


def chosen(kind, *values):
    return jnp.where(kind == 0, values[0], jnp.where(kind == 1, values[1], values[2]))


def norm_kernel(groups, rows, at, *refs):
    nears, fars, (gain, own, other, inv_out, natural) = refs[:3], refs[3:6], refs[6:]
    x, y, core = at[1], at[2], at[3]
    width = nears[0].shape[1]
    near = chosen(at[0], *[r[...] for r in nears]).astype(F32)
    far = chosen(at[0], *[r[...] for r in fars]).astype(F32)
    total = jnp.sum(near * near, axis=-1, keepdims=True) + jnp.sum(far * far, axis=-1, keepdims=True)
    inv_rms = lax.rsqrt(total / D + EPS)
    inv_out[...] = jnp.broadcast_to(inv_rms, inv_out.shape)
    near_at = pl.ds(pl.multiple_of(x * width, width), width)
    far_at = pl.ds(pl.multiple_of((1 - x) * width, width), width)
    natural[:, near_at] = (near * inv_rms * gain[:, near_at]).astype(BF16)
    natural[:, far_at] = (far * inv_rms * gain[:, far_at]).astype(BF16)
    for group in range(groups):
        for k in range(2):
            row = 2 * group + (y if k == 0 else 1 - y)
            put = slice((2 * group + k) * rows, (2 * group + k + 1) * rows)
            for out, half in ((own, core), (other, 1 - core)):
                got = pl.multiple_of((2 * row + half) * rows, rows)
                out[:, put] = natural[:, pl.ds(got, rows)]


def norm(at, nears, fars, gain, groups, rows):
    length, width = nears[0].shape
    step = 128

    def pick(want):
        return pl.BlockSpec((step, width), lambda i, s: (jnp.where(s[0] == want, i, 0), 0))

    out = pl.BlockSpec((step, D // 2), lambda i, s: (i, 0))
    return pl.pallas_call(
        lambda *refs: norm_kernel(groups, rows, *refs),
        grid_spec=pltpu.PrefetchScalarGridSpec(
            num_scalar_prefetch=1,
            grid=(length // step,),
            in_specs=[pick(i % 3) for i in range(6)] + [pl.BlockSpec((1, D), lambda i, s: (0, 0))],
            out_specs=[out, out, pl.BlockSpec((step, 128), lambda i, s: (i, 0))],
            scratch_shapes=[pltpu.VMEM((step, D), BF16)],
        ),
        out_shape=[pltpu.HBM((length, D // 2), BF16)] * 2
        + [jax.ShapeDtypeStruct((length, 128), F32)],
        compiler_params=params(14),
        cost_estimate=cost(8 * length * D, 8),
        name="norm",
    )(at, *nears, *fars, gain)


def attend_head(bias, qg, kv):
    low_lane = lax.broadcasted_iota(jnp.int32, qg.shape, 1) < HEAD
    zero = jnp.zeros((), BF16)
    scaled = qg * jnp.asarray(1.0 / HEAD**0.5, BF16)
    queries = jnp.where(low_lane, scaled, zero)
    grads = jnp.where(low_lane, zero, scaled)
    scores = dot(queries, kv, NT) + bias
    grad_prob = dot(grads, kv, NT)
    weights = jnp.exp(scores - jnp.max(scores, axis=-1, keepdims=True))
    probs = weights * (1.0 / jnp.sum(weights, axis=-1, keepdims=True))
    prob_low = probs.astype(BF16)
    row_delta = jnp.sum(prob_low.astype(F32) * grad_prob, axis=-1, keepdims=True)
    grad_score = (probs * (grad_prob - row_delta)).astype(BF16)
    grad_query = dot(grad_score, kv)
    qg_t = qg.T
    key_t = dot(qg_t[:HEAD], grad_score)
    value_t = dot(qg_t[HEAD:], prob_low)
    gkv = jnp.concatenate([key_t, value_t], axis=0).T
    dec = jnp.where(low_lane, grad_query, pltpu.roll(gkv, HEAD, 1))
    return dec.astype(BF16), gkv.astype(BF16)


def attend_kernel(at, part, enc_other, w_other, *refs):
    qgs, (dec, gkv) = refs[:3], refs[3:]
    kv = (part[...] + dot(enc_other[...], w_other[...])).astype(BF16)
    keys = lax.broadcasted_iota(jnp.int32, (1, kv.shape[0]), 1)
    bias = jnp.where(keys < at[4], 0.0, -1e30).astype(F32)
    for head in range(kv.shape[1] // (2 * HEAD)):
        lanes = slice(head * 2 * HEAD, (head + 1) * 2 * HEAD)
        qg = chosen(at[5], *[r[:, lanes] for r in qgs])
        dec[:, lanes], gkv[:, lanes] = attend_head(bias, qg, kv[:, lanes])


def attend(at, part, enc_other, w_other, qgs, chunk):
    length = part.shape[0]
    half, cols = w_other.shape
    step = min(256, cols)
    first = chunk * (cols // step)
    enc = pl.BlockSpec((length, half), lambda i, s: (0, 0))
    weight = pl.BlockSpec((half, step), lambda i, s: (0, i))
    out = pl.BlockSpec((length, step), lambda i, s: (0, i))

    def pick(want):
        return pl.BlockSpec((length, step), lambda i, s: (0, jnp.where(s[5] == want, first + i, first)))

    return pl.pallas_call(
        attend_kernel,
        grid_spec=pltpu.PrefetchScalarGridSpec(
            num_scalar_prefetch=1,
            grid=(cols // step,),
            in_specs=[out, enc, weight, pick(0), pick(1), pick(2)],
            out_specs=[out, out],
        ),
        out_shape=[jax.ShapeDtypeStruct((length, cols), BF16)] * 2,
        compiler_params=params(26),
        cost_estimate=cost(
            length * cols * (4 * half + 14 * length), 8, length * length * cols // (2 * HEAD)
        ),
        name="attend",
    )(at, part, *in_hbm(enc_other, w_other, *qgs))


def weight_grad_kernel(scale, at, enc_a, enc_b, gkv_a, gkv_b, out):
    grad = scale * (dot(enc_a[...], gkv_a[...], TN) + dot(enc_b[...], gkv_b[...], TN))
    out[...] = grad.astype(BF16)


def weight_grad(at, enc_a, enc_b, gkv_a, gkv_b, groups, scale):
    length, half = enc_a.shape
    cols = gkv_a.shape[1]
    step = half // groups
    enc = pl.BlockSpec((length, step), lambda i, s: (0, i))
    gkv = pl.BlockSpec((length, cols), lambda i, s: (0, 0))
    return pl.pallas_call(
        lambda *refs: weight_grad_kernel(scale, *refs),
        grid_spec=pltpu.PrefetchScalarGridSpec(
            num_scalar_prefetch=1,
            grid=(groups,),
            in_specs=[enc, enc, gkv, gkv],
            out_specs=pl.BlockSpec((step, cols), lambda i, s: (i, 0)),
        ),
        out_shape=pltpu.HBM((half, cols), BF16),
        cost_estimate=cost(4 * length * half * cols // 64, 0),
        compiler_params=params(12),
        name="weight_grad",
    )(at, *in_hbm(enc_a, enc_b), gkv_a, gkv_b)


def collect_kernel(scale, at, *refs):
    terms, (local, here, inv, gain, out, gain_term) = refs[:3], refs[3:]
    total = terms[0][...].astype(F32)
    for term in terms[1:]:
        total = total + term[...].astype(F32)
    out[...] = (total * gain[...]).astype(BF16)
    raw = jnp.where(at[0] == 0, local[...], here[...]).astype(F32)
    product = total * (raw * inv[:, :1])
    gain_term[0] = scale * jnp.sum(product, axis=0, keepdims=True)


def collect(at, terms, local, here, inv_rms, gain, scale):
    length, width = local.shape
    step = 128
    block = pl.BlockSpec((step, width), lambda i, s: (i, 0))

    def pick(want):
        return pl.BlockSpec((step, width), lambda i, s: (jnp.where(s[0] == want, i, 0), 0))

    return pl.pallas_call(
        lambda *refs: collect_kernel(scale, *refs),
        grid_spec=pltpu.PrefetchScalarGridSpec(
            num_scalar_prefetch=1,
            grid=(length // step,),
            in_specs=[block] * 3
            + [pick(0), pick(1)]
            + [
                pl.BlockSpec((step, 128), lambda i, s: (i, 0)),
                pl.BlockSpec((1, width), lambda i, s: (0, 0)),
            ],
            out_specs=[block, pl.BlockSpec((1, 1, width), lambda i, s: (i, 0, 0))],
        ),
        out_shape=[
            jax.ShapeDtypeStruct((length, width), BF16),
            jax.ShapeDtypeStruct((length // step, 1, width), F32),
        ],
        cost_estimate=cost(8 * length * width, 12),
        compiler_params=params(16),
        name="collect",
    )(at, *terms, local, here, inv_rms, gain)


def enc_grad_kernel(at, gkv_0, gkv_1, own_0, own_1, other_0, other_1, out):
    rows = own_0.shape[0]
    own = dot(gkv_0[...], own_0[...], NT) + dot(gkv_1[...], own_1[...], NT)
    other = dot(gkv_0[...], other_0[...], NT) + dot(gkv_1[...], other_1[...], NT)
    first = at[3] == 0
    out[:, :rows] = jnp.where(first, own, other).astype(BF16)
    out[:, rows:] = jnp.where(first, other, own).astype(BF16)


def enc_grad(at, gkvs, owns, others, groups, rows, shard):
    length, cols = gkvs[0].shape
    per_shard = groups // 2

    def block(i, s):
        target = lax.rem(s[1] + shard, 2)
        group = target * per_shard + i // 2
        return (2 * group + lax.rem(i + s[2], 2), 0)

    gkv = pl.BlockSpec((length, cols), lambda i, s: (0, 0))
    weight = pl.BlockSpec((rows, cols), block)
    return pl.pallas_call(
        enc_grad_kernel,
        grid_spec=pltpu.PrefetchScalarGridSpec(
            num_scalar_prefetch=1,
            grid=(groups,),
            in_specs=[gkv, gkv, weight, weight, weight, weight],
            out_specs=pl.BlockSpec((length, 2 * rows), lambda i, s: (0, i)),
        ),
        out_shape=pltpu.HBM((length, D // 2), BF16),
        compiler_params=params(12),
        cost_estimate=cost(4 * length * D * cols, 8),
        name="enc_grad",
    )(at, *in_hbm(*gkvs, *owns, *others))


def cut(array, axis, index, size):
    return lax.dynamic_slice_in_dim(array, index * size, size, axis)


def ordered(first, own, other, axis):
    return jnp.where(
        first, jnp.concatenate([own, other], axis), jnp.concatenate([other, own], axis)
    )


def after(value, *others):
    return lax.optimization_barrier((value,) + others)[0]


def on_device(sec_acts, gain, w_kv, src_len, tgt_len):
    groups = lax.axis_size("z")
    shards = lax.axis_size("mp")
    z, y = lax.axis_index("z"), lax.axis_index("y")
    core, x = lax.axis_index("phase"), lax.axis_index("mp")
    straight = y == core
    packed = sec_acts[0, 0]
    length, width = packed.shape
    rows = w_kv.shape[0]
    half = width // 2
    cols = half // CHUNKS
    pair_scale = 1.0 / (2 * groups)
    tiled = shards == 2 and rows % 128 == 0

    def turned(count, by):
        return [(i, (i + by) % count) for i in range(count)]

    def across(value, turn, moves):
        return lax.ppermute(
            value,
            ("y", "phase", "mp"),
            [(a * shards + s, b * shards + (s + turn) % shards) for a, b in moves for s in range(shards)],
        )

    def chunk_of(side, k):
        return lax.dynamic_slice_in_dim(w_kv, side * half + k * cols, cols, 1)

    def slots(block):
        return [lax.ppermute(block, "z", turned(groups, -s)) for s in range(1, groups)]

    swapped = [lax.ppermute(chunk_of(1 - y, 0), "y", SWAP)]
    here = lax.ppermute(packed, PLANE, [(2, 3)])
    gain_sent, len_sent = lax.optimization_barrier((gain, src_len, here))[:2]
    gains = [gain] + [lax.ppermute(gain_sent, "mp", turned(shards, t)) for t in range(1, shards)]
    key_count = jnp.where(straight, src_len, lax.ppermute(len_sent, "y", SWAP))
    there = lax.ppermute(after(packed, swapped[0], key_count, *gains), PLANE, [(0, 2), (2, 1)])
    for k in range(1, CHUNKS):
        swapped.append(lax.ppermute(after(chunk_of(1 - y, k), there), "y", SWAP))
    nears = [packed, here, there]
    fars = []
    for turn in range(1, shards):
        fars.append(
            [
                across(packed, turn, [(0, 0)]),
                across(here, turn, [(3, 3)]),
                across(there, turn, [(1, 1), (2, 2)]),
            ]
        )
    blocks = [jnp.concatenate([chunk_of(y, k), swapped[k]], 0) for k in range(CHUNKS)]
    w_own, w_other = [], []

    position = lax.broadcasted_iota(jnp.int32, (length, width), 0)
    is_grad = lax.broadcasted_iota(jnp.int32, (length, width), 1) % (2 * HEAD) >= HEAD
    masked = jnp.where(is_grad & (position >= tgt_len[0]), jnp.zeros((), BF16), packed)
    qg_near, qg_far = cut(masked, 1, y, half), cut(masked, 1, 1 - y, half)
    qg_near, qg_far = lax.optimization_barrier((qg_near, qg_far, there))[:2]
    qgs = [
        qg_near,
        lax.ppermute(qg_near, PLANE, [(1, 0)]),
        lax.ppermute(qg_far, PLANE, [(1, 2), (3, 1)]),
    ]
    enc_kind = jnp.where(straight, y, 2)
    qg_kind = jnp.where(straight, 1 - y, 2)
    at = jnp.concatenate(
        [jnp.stack([enc_kind, x, y, core]).astype(jnp.int32), key_count, qg_kind[None]]
    )

    def natural(parts, axis):
        if shards == 2:
            return ordered(x == 0, parts[0], parts[1], axis)
        stacked = jnp.stack(parts)
        return jnp.concatenate(
            [
                lax.dynamic_index_in_dim(stacked, (x - i) % shards, 0, keepdims=False)
                for i in range(shards)
            ],
            axis,
        )

    block_group = jnp.arange(groups)
    block_pair = 2 * block_group[:, None] + jnp.stack([y, 1 - y])[None, :]
    block_order = (2 * block_pair[None] + jnp.stack([core, 1 - core])[:, None, None]).reshape(-1)
    gain_all = natural(gains, 0).astype(F32)

    if tiled:
        enc_own, enc_other, inv_rms = norm(
            at, nears, fars[0], after(gain_all[None], *qgs, *blocks), groups, rows
        )
    else:
        raw = [chosen(enc_kind, *parts) for parts in [nears] + fars]
        hidden = natural(raw, 1).astype(F32)
        inv_rms = lax.rsqrt(jnp.sum(hidden * hidden, axis=-1, keepdims=True) / D + EPS)
        encoded = (hidden * inv_rms * gain_all).astype(BF16)
        encoded = encoded.reshape(length, -1, rows)[:, block_order].reshape(length, 2, -1)
        enc_own, enc_other = encoded[:, 0], encoded[:, 1]
    enc_mate = lax.ppermute(enc_other, "phase", SWAP)

    decs, gkvs, weight_sums = [], [], []
    for k in range(CHUNKS):
        if k in DIRECT:
            pieces = [blocks[k]] + slots(after(blocks[k], w_own[0]))
            pieces = lax.optimization_barrier((*pieces, grad))[:-1]
            gathered = jnp.zeros((groups * 2 * rows, cols), BF16)
            for turn, piece in enumerate(pieces):
                start = (z + turn) % groups * 2 * rows
                gathered = lax.dynamic_update_slice_in_dim(gathered, piece, start, 0)
            w_own.append(gathered)
        else:
            block = blocks[k]
            w_own.append(lax.all_gather(block, "z", axis=0, tiled=True))
            if k > 0:
                w_own[k] = after(w_own[k], grad)
        w_other.append(lax.ppermute(w_own[k], "phase", SWAP))
        dec, gkv = attend(at, dot(enc_own, w_own[k]), enc_other, w_other[k], qgs, k)
        gkvs.append(gkv)
        decs.append(
            (
                lax.ppermute(dec, PLANE, [(0, 1)]),
                dec,
                lax.ppermute(dec, PLANE, [(2, 1), (1, 3)]),
            )
        )
        parts = jnp.split(gkv, 2, axis=1)
        gkv_mate = jnp.concatenate([lax.ppermute(p, "phase", SWAP) for p in parts], 1)
        if tiled:
            last = k == CHUNKS - 1
            if last:
                away = enc_grad(at, gkvs, w_own, w_other, groups, rows, 1)
                gkv_mate = after(gkv_mate, away)
            grad = weight_grad(at, enc_own, enc_mate, gkv, gkv_mate, groups, pair_scale)
            if last:
                kept = [after(gkvs[0], grad)] + gkvs[1:]
                terms = [enc_grad(at, kept, w_own, w_other, groups, rows, 0), away]
        else:
            grad = pair_scale * (dot(enc_own, gkv, TN) + dot(enc_mate, gkv_mate, TN))
            grad = grad.astype(BF16)
        weight_sums.append(lax.psum_scatter(grad, "z", scatter_dimension=0, tiled=True))

    if not tiled:
        gkv_all = jnp.concatenate(gkvs, 1)
        full = dot(gkv_all, jnp.concatenate([jnp.concatenate(w, 0) for w in zip(w_own, w_other)], 1), NT)
        back = jnp.zeros_like(block_order).at[block_order].set(jnp.arange(block_order.shape[0]))
        full = full.astype(BF16).reshape(length, -1, rows)[:, back].reshape(length, D)
        terms = [cut(full, 1, (x + s) % shards, width) for s in range(shards)]
    far_terms = terms[0].astype(F32)
    moved = []
    for turn in range(1, shards):
        got = across(terms[turn], turn, [(1, 1), (2, 2)])
        far_terms = far_terms + got.astype(F32)
        moved.append(across(after(terms[turn], got), turn, [(0, 0), (3, 3)]))
    moved.append(lax.ppermute(far_terms.astype(BF16), PLANE, [(2, 0), (1, 3)]))

    dec_here = jnp.concatenate([jnp.where(y == 0, d[0], d[1]) for d in decs], 1)
    dec_there = jnp.concatenate([d[2] for d in decs], 1)
    dec_grads = ordered(y == 0, dec_here, dec_there, 1)
    kept = jnp.concatenate([w[:rows] for w in weight_sums], 1)
    got = [lax.ppermute(w[rows:], "y", SWAP) for w in weight_sums]
    if tiled:
        moved[0], dec_grads, got[0] = lax.optimization_barrier((moved[0], dec_grads, got[0]))
        grad_normed, gain_term = collect(
            at, [terms[0]] + moved, packed, here, inv_rms, gain.astype(F32)[None], pair_scale
        )
        gain_term = jnp.sum(gain_term, axis=(0, 1))
    else:
        grad_enc = terms[0].astype(F32)
        for part in moved:
            grad_enc = grad_enc + part.astype(F32)
        grad_normed = (grad_enc * gain.astype(F32)).astype(BF16)
        normed = raw[0].astype(F32) * inv_rms
        gain_term = pair_scale * jnp.sum(grad_enc * normed, axis=0)
    enc_grads = jnp.where(y == 0, grad_normed, lax.ppermute(grad_normed, PLANE, [(3, 2)]))

    gain_term = jnp.where(straight, gain_term, 0.0)
    gain_term = gain_term + lax.ppermute(gain_term, PLANE, [(0, 3), (3, 0), (1, 2), (2, 1)])
    turn = 1
    while turn < groups:
        gain_term = gain_term + lax.ppermute(gain_term, "z", [(i, i ^ turn) for i in range(groups)])
        turn *= 2
    d_gain = jnp.where(straight, gain_term, lax.ppermute(gain_term, "phase", SWAP))

    got = jnp.concatenate(got, 1)
    d_wkv = ordered(y == 0, kept, got, 1).astype(F32)
    sec_grads = jnp.where(core == 0, enc_grads, dec_grads)[None, None]
    return (sec_grads, d_wkv, d_gain)


def solution(mesh):
    size = mesh.shape
    split = (size["dp"] // 2, 2, size["phase"], size["mp"])
    fine = Mesh(mesh.devices.reshape(split), ("z", "y", "phase", "mp"))
    pairs = ("z", "y")
    acts = P("phase", pairs, None, "mp")
    weights = P(("z", "y", "phase"), "mp")
    return jax.shard_map(
        on_device,
        mesh=fine,
        in_specs=(acts, P("mp"), weights, P(pairs), P(pairs)),
        out_specs=(acts, weights, P("mp")),
        check_vma=False,
    )
```

```python
import jax
import jax.numpy as jnp
from jax import lax
from jax.experimental import pallas as pl
from jax.experimental.pallas import tpu as pltpu
from jax.sharding import Mesh, PartitionSpec as P

D = 4096
HEAD = 64
EPS = 1e-06
CHUNKS = 2
DIRECT = ()
F32 = jnp.float32
BF16 = jnp.bfloat16
NN = (((1,), (0,)), ((), ()))
NT = (((1,), (1,)), ((), ()))
TN = (((0,), (0,)), ((), ()))

PLANE = ("y", "phase")
SWAP = [(0, 1), (1, 0)]


def dot(a, b, dims=NN):
    return lax.dot_general(a, b, dims, preferred_element_type=F32)


def cost(flops, mib, exps=0):
    return pl.CostEstimate(flops=flops, bytes_accessed=mib << 20, transcendentals=exps)


def in_hbm(*arrays):
    return [pltpu.with_memory_space_constraint(a, pltpu.HBM) for a in arrays]


def params(mib):
    return pltpu.CompilerParams(vmem_limit_bytes=mib << 20)


def chosen(kind, *values):
    return jnp.where(kind == 0, values[0], jnp.where(kind == 1, values[1], values[2]))


def norm_kernel(groups, rows, at, *refs):
    nears, fars, (gain, own, other, inv_out, natural) = refs[:3], refs[3:6], refs[6:]
    x, y, core = at[1], at[2], at[3]
    width = nears[0].shape[1]
    near = chosen(at[0], *[r[...] for r in nears]).astype(F32)
    far = chosen(at[0], *[r[...] for r in fars]).astype(F32)
    total = jnp.sum(near * near, axis=-1, keepdims=True) + jnp.sum(far * far, axis=-1, keepdims=True)
    inv_rms = lax.rsqrt(total / D + EPS)
    inv_out[...] = jnp.broadcast_to(inv_rms, inv_out.shape)
    near_at = pl.ds(pl.multiple_of(x * width, width), width)
    far_at = pl.ds(pl.multiple_of((1 - x) * width, width), width)
    natural[:, near_at] = (near * inv_rms * gain[:, near_at]).astype(BF16)
    natural[:, far_at] = (far * inv_rms * gain[:, far_at]).astype(BF16)
    for group in range(groups):
        for k in range(2):
            row = 2 * group + (y if k == 0 else 1 - y)
            put = slice((2 * group + k) * rows, (2 * group + k + 1) * rows)
            for out, half in ((own, core), (other, 1 - core)):
                got = pl.multiple_of((2 * row + half) * rows, rows)
                out[:, put] = natural[:, pl.ds(got, rows)]


def norm(at, nears, fars, gain, groups, rows):
    length, width = nears[0].shape
    step = 128

    def pick(want):
        return pl.BlockSpec((step, width), lambda i, s: (jnp.where(s[0] == want, i, 0), 0))

    out = pl.BlockSpec((step, D // 2), lambda i, s: (i, 0))
    return pl.pallas_call(
        lambda *refs: norm_kernel(groups, rows, *refs),
        grid_spec=pltpu.PrefetchScalarGridSpec(
            num_scalar_prefetch=1,
            grid=(length // step,),
            in_specs=[pick(i % 3) for i in range(6)] + [pl.BlockSpec((1, D), lambda i, s: (0, 0))],
            out_specs=[out, out, pl.BlockSpec((step, 128), lambda i, s: (i, 0))],
            scratch_shapes=[pltpu.VMEM((step, D), BF16)],
        ),
        out_shape=[pltpu.HBM((length, D // 2), BF16)] * 2
        + [jax.ShapeDtypeStruct((length, 128), F32)],
        compiler_params=params(14),
        cost_estimate=cost(8 * length * D, 8),
        name="norm",
    )(at, *nears, *fars, gain)


def attend_head(bias, qg, kv):
    low_lane = lax.broadcasted_iota(jnp.int32, qg.shape, 1) < HEAD
    zero = jnp.zeros((), BF16)
    scaled = qg * jnp.asarray(1.0 / HEAD**0.5, BF16)
    queries = jnp.where(low_lane, scaled, zero)
    grads = jnp.where(low_lane, zero, scaled)
    scores = dot(queries, kv, NT) + bias
    grad_prob = dot(grads, kv, NT)
    weights = jnp.exp(scores - jnp.max(scores, axis=-1, keepdims=True))
    probs = weights * (1.0 / jnp.sum(weights, axis=-1, keepdims=True))
    prob_low = probs.astype(BF16)
    row_delta = jnp.sum(prob_low.astype(F32) * grad_prob, axis=-1, keepdims=True)
    grad_score = (probs * (grad_prob - row_delta)).astype(BF16)
    grad_query = dot(grad_score, kv)
    qg_t = qg.T
    key_t = dot(qg_t[:HEAD], grad_score)
    value_t = dot(qg_t[HEAD:], prob_low)
    gkv = jnp.concatenate([key_t, value_t], axis=0).T
    dec = jnp.where(low_lane, grad_query, pltpu.roll(gkv, HEAD, 1))
    return dec.astype(BF16), gkv.astype(BF16)


def attend_kernel(at, part, enc_other, w_other, *refs):
    qgs, (dec, gkv) = refs[:3], refs[3:]
    kv = (part[...] + dot(enc_other[...], w_other[...])).astype(BF16)
    keys = lax.broadcasted_iota(jnp.int32, (1, kv.shape[0]), 1)
    bias = jnp.where(keys < at[4], 0.0, -1e30).astype(F32)
    for head in range(kv.shape[1] // (2 * HEAD)):
        lanes = slice(head * 2 * HEAD, (head + 1) * 2 * HEAD)
        qg = chosen(at[5], *[r[:, lanes] for r in qgs])
        dec[:, lanes], gkv[:, lanes] = attend_head(bias, qg, kv[:, lanes])


def attend(at, part, enc_other, w_other, qgs, chunk):
    length = part.shape[0]
    half, cols = w_other.shape
    step = min(256, cols)
    first = chunk * (cols // step)
    enc = pl.BlockSpec((length, half), lambda i, s: (0, 0))
    weight = pl.BlockSpec((half, step), lambda i, s: (0, i))
    out = pl.BlockSpec((length, step), lambda i, s: (0, i))

    def pick(want):
        return pl.BlockSpec((length, step), lambda i, s: (0, jnp.where(s[5] == want, first + i, first)))

    return pl.pallas_call(
        attend_kernel,
        grid_spec=pltpu.PrefetchScalarGridSpec(
            num_scalar_prefetch=1,
            grid=(cols // step,),
            in_specs=[out, enc, weight, pick(0), pick(1), pick(2)],
            out_specs=[out, out],
        ),
        out_shape=[jax.ShapeDtypeStruct((length, cols), BF16)] * 2,
        compiler_params=params(26),
        cost_estimate=cost(
            length * cols * (4 * half + 14 * length), 8, length * length * cols // (2 * HEAD)
        ),
        name="attend",
    )(at, part, *in_hbm(enc_other, w_other, *qgs))


def weight_grad_kernel(scale, at, enc_a, enc_b, gkv_a, gkv_b, out):
    grad = scale * (dot(enc_a[...], gkv_a[...], TN) + dot(enc_b[...], gkv_b[...], TN))
    out[...] = grad.astype(BF16)


def weight_grad(at, enc_a, enc_b, gkv_a, gkv_b, groups, scale):
    length, half = enc_a.shape
    cols = gkv_a.shape[1]
    step = half // groups
    enc = pl.BlockSpec((length, step), lambda i, s: (0, i))
    gkv = pl.BlockSpec((length, cols), lambda i, s: (0, 0))
    return pl.pallas_call(
        lambda *refs: weight_grad_kernel(scale, *refs),
        grid_spec=pltpu.PrefetchScalarGridSpec(
            num_scalar_prefetch=1,
            grid=(groups,),
            in_specs=[enc, enc, gkv, gkv],
            out_specs=pl.BlockSpec((step, cols), lambda i, s: (i, 0)),
        ),
        out_shape=pltpu.HBM((half, cols), BF16),
        cost_estimate=cost(4 * length * half * cols // 64, 0),
        compiler_params=params(12),
        name="weight_grad",
    )(at, *in_hbm(enc_a, enc_b), gkv_a, gkv_b)


def collect_kernel(scale, at, *refs):
    terms, (local, here, inv, gain, out, gain_term) = refs[:3], refs[3:]
    total = terms[0][...].astype(F32)
    for term in terms[1:]:
        total = total + term[...].astype(F32)
    out[...] = (total * gain[...]).astype(BF16)
    raw = jnp.where(at[0] == 0, local[...], here[...]).astype(F32)
    product = total * (raw * inv[:, :1])
    gain_term[0] = scale * jnp.sum(product, axis=0, keepdims=True)


def collect(at, terms, local, here, inv_rms, gain, scale):
    length, width = local.shape
    step = 128
    block = pl.BlockSpec((step, width), lambda i, s: (i, 0))

    def pick(want):
        return pl.BlockSpec((step, width), lambda i, s: (jnp.where(s[0] == want, i, 0), 0))

    return pl.pallas_call(
        lambda *refs: collect_kernel(scale, *refs),
        grid_spec=pltpu.PrefetchScalarGridSpec(
            num_scalar_prefetch=1,
            grid=(length // step,),
            in_specs=[block] * 3
            + [pick(0), pick(1)]
            + [
                pl.BlockSpec((step, 128), lambda i, s: (i, 0)),
                pl.BlockSpec((1, width), lambda i, s: (0, 0)),
            ],
            out_specs=[block, pl.BlockSpec((1, 1, width), lambda i, s: (i, 0, 0))],
        ),
        out_shape=[
            jax.ShapeDtypeStruct((length, width), BF16),
            jax.ShapeDtypeStruct((length // step, 1, width), F32),
        ],
        cost_estimate=cost(8 * length * width, 12),
        compiler_params=params(16),
        name="collect",
    )(at, *terms, local, here, inv_rms, gain)


def enc_grad_kernel(at, gkv_0, gkv_1, own_0, own_1, other_0, other_1, out):
    rows = own_0.shape[0]
    own = dot(gkv_0[...], own_0[...], NT) + dot(gkv_1[...], own_1[...], NT)
    other = dot(gkv_0[...], other_0[...], NT) + dot(gkv_1[...], other_1[...], NT)
    first = at[3] == 0
    out[:, :rows] = jnp.where(first, own, other).astype(BF16)
    out[:, rows:] = jnp.where(first, other, own).astype(BF16)


def enc_grad(at, gkvs, owns, others, groups, rows, shard):
    length, cols = gkvs[0].shape
    per_shard = groups // 2

    def block(i, s):
        target = lax.rem(s[1] + shard, 2)
        group = target * per_shard + i // 2
        return (2 * group + lax.rem(i + s[2], 2), 0)

    gkv = pl.BlockSpec((length, cols), lambda i, s: (0, 0))
    weight = pl.BlockSpec((rows, cols), block)
    return pl.pallas_call(
        enc_grad_kernel,
        grid_spec=pltpu.PrefetchScalarGridSpec(
            num_scalar_prefetch=1,
            grid=(groups,),
            in_specs=[gkv, gkv, weight, weight, weight, weight],
            out_specs=pl.BlockSpec((length, 2 * rows), lambda i, s: (0, i)),
        ),
        out_shape=pltpu.HBM((length, D // 2), BF16),
        compiler_params=params(12),
        cost_estimate=cost(4 * length * D * cols, 8),
        name="enc_grad",
    )(at, *in_hbm(*gkvs, *owns, *others))


def cut(array, axis, index, size):
    return lax.dynamic_slice_in_dim(array, index * size, size, axis)


def ordered(first, own, other, axis):
    return jnp.where(
        first, jnp.concatenate([own, other], axis), jnp.concatenate([other, own], axis)
    )


def after(value, *others):
    return lax.optimization_barrier((value,) + others)[0]


def on_device(sec_acts, gain, w_kv, src_len, tgt_len):
    groups = lax.axis_size("z")
    shards = lax.axis_size("mp")
    z, y = lax.axis_index("z"), lax.axis_index("y")
    core, x = lax.axis_index("phase"), lax.axis_index("mp")
    straight = y == core
    packed = sec_acts[0, 0]
    length, width = packed.shape
    rows = w_kv.shape[0]
    half = width // 2
    cols = half // CHUNKS
    pair_scale = 1.0 / (2 * groups)
    tiled = shards == 2 and rows % 128 == 0

    def turned(count, by):
        return [(i, (i + by) % count) for i in range(count)]

    def across(value, turn, moves):
        return lax.ppermute(
            value,
            ("y", "phase", "mp"),
            [(a * shards + s, b * shards + (s + turn) % shards) for a, b in moves for s in range(shards)],
        )

    def chunk_of(side, k):
        return lax.dynamic_slice_in_dim(w_kv, side * half + k * cols, cols, 1)

    def slots(block):
        return [lax.ppermute(block, "z", turned(groups, -s)) for s in range(1, groups)]

    swapped = [lax.ppermute(chunk_of(1 - y, 0), "y", SWAP)]
    here = lax.ppermute(packed, PLANE, [(2, 3)])
    gain_sent, len_sent = lax.optimization_barrier((gain, src_len, here))[:2]
    gains = [gain] + [lax.ppermute(gain_sent, "mp", turned(shards, t)) for t in range(1, shards)]
    key_count = jnp.where(straight, src_len, lax.ppermute(len_sent, "y", SWAP))
    there = lax.ppermute(after(packed, swapped[0], key_count, *gains), PLANE, [(0, 2), (2, 1)])
    nears = [packed, here, there]
    fars = []
    for turn in range(1, shards):
        fars.append(
            [
                across(packed, turn, [(0, 0)]),
                across(here, turn, [(3, 3)]),
                across(there, turn, [(1, 1), (2, 2)]),
            ]
        )
    for k in range(1, CHUNKS):
        swapped.append(lax.ppermute(after(chunk_of(1 - y, k), there, fars[0][1]), "y", SWAP))
    blocks = [jnp.concatenate([chunk_of(y, k), swapped[k]], 0) for k in range(CHUNKS)]
    w_own, w_other = [], []

    position = lax.broadcasted_iota(jnp.int32, (length, width), 0)
    is_grad = lax.broadcasted_iota(jnp.int32, (length, width), 1) % (2 * HEAD) >= HEAD
    masked = jnp.where(is_grad & (position >= tgt_len[0]), jnp.zeros((), BF16), packed)
    qg_near, qg_far = cut(masked, 1, y, half), cut(masked, 1, 1 - y, half)
    qg_near, qg_far = lax.optimization_barrier((qg_near, qg_far, swapped[-1]))[:2]
    qgs = [
        qg_near,
        lax.ppermute(qg_near, PLANE, [(1, 0)]),
        lax.ppermute(qg_far, PLANE, [(1, 2), (3, 1)]),
    ]
    enc_kind = jnp.where(straight, y, 2)
    qg_kind = jnp.where(straight, 1 - y, 2)
    at = jnp.concatenate(
        [jnp.stack([enc_kind, x, y, core]).astype(jnp.int32), key_count, qg_kind[None]]
    )

    def natural(parts, axis):
        if shards == 2:
            return ordered(x == 0, parts[0], parts[1], axis)
        stacked = jnp.stack(parts)
        return jnp.concatenate(
            [
                lax.dynamic_index_in_dim(stacked, (x - i) % shards, 0, keepdims=False)
                for i in range(shards)
            ],
            axis,
        )

    block_group = jnp.arange(groups)
    block_pair = 2 * block_group[:, None] + jnp.stack([y, 1 - y])[None, :]
    block_order = (2 * block_pair[None] + jnp.stack([core, 1 - core])[:, None, None]).reshape(-1)
    gain_all = natural(gains, 0).astype(F32)

    if tiled:
        enc_own, enc_other, inv_rms = norm(
            at, nears, fars[0], after(gain_all[None], *qgs, *blocks), groups, rows
        )
    else:
        raw = [chosen(enc_kind, *parts) for parts in [nears] + fars]
        hidden = natural(raw, 1).astype(F32)
        inv_rms = lax.rsqrt(jnp.sum(hidden * hidden, axis=-1, keepdims=True) / D + EPS)
        encoded = (hidden * inv_rms * gain_all).astype(BF16)
        encoded = encoded.reshape(length, -1, rows)[:, block_order].reshape(length, 2, -1)
        enc_own, enc_other = encoded[:, 0], encoded[:, 1]
    enc_mate = lax.ppermute(enc_other, "phase", SWAP)

    decs, gkvs, weight_sums = [], [], []
    for k in range(CHUNKS):
        if k in DIRECT:
            pieces = [blocks[k]] + slots(after(blocks[k], w_own[0]))
            pieces = lax.optimization_barrier((*pieces, grad))[:-1]
            gathered = jnp.zeros((groups * 2 * rows, cols), BF16)
            for turn, piece in enumerate(pieces):
                start = (z + turn) % groups * 2 * rows
                gathered = lax.dynamic_update_slice_in_dim(gathered, piece, start, 0)
            w_own.append(gathered)
        else:
            block = blocks[k]
            w_own.append(lax.all_gather(block, "z", axis=0, tiled=True))
            if k > 0:
                w_own[k] = after(w_own[k], grad)
        w_other.append(lax.ppermute(w_own[k], "phase", SWAP))
        part = dot(enc_own, w_own[k])
        if k > 0:
            part = after(part, decs[0][0], decs[0][2])
        dec, gkv = attend(at, part, enc_other, w_other[k], qgs, k)
        gkvs.append(gkv)
        decs.append(
            (
                lax.ppermute(dec, PLANE, [(0, 1)]),
                dec,
                lax.ppermute(dec, PLANE, [(2, 1), (1, 3)]),
            )
        )
        gkv_sent = gkv
        if tiled and k == CHUNKS - 1:
            terms = [enc_grad(at, gkvs, w_own, w_other, groups, rows, s) for s in (1, 0)][::-1]
            gkv_sent = after(gkv, *terms)
        parts = jnp.split(gkv_sent, 2, axis=1)
        gkv_mate = jnp.concatenate([lax.ppermute(p, "phase", SWAP) for p in parts], 1)
        if tiled:
            grad = weight_grad(at, enc_own, enc_mate, gkv, gkv_mate, groups, pair_scale)
        else:
            grad = pair_scale * (dot(enc_own, gkv, TN) + dot(enc_mate, gkv_mate, TN))
            grad = grad.astype(BF16)
        weight_sums.append(lax.psum_scatter(grad, "z", scatter_dimension=0, tiled=True))

    if not tiled:
        gkv_all = jnp.concatenate(gkvs, 1)
        full = dot(gkv_all, jnp.concatenate([jnp.concatenate(w, 0) for w in zip(w_own, w_other)], 1), NT)
        back = jnp.zeros_like(block_order).at[block_order].set(jnp.arange(block_order.shape[0]))
        full = full.astype(BF16).reshape(length, -1, rows)[:, back].reshape(length, D)
        terms = [cut(full, 1, (x + s) % shards, width) for s in range(shards)]
    far_terms = terms[0].astype(F32)
    for turn in range(1, shards):
        far_terms = far_terms + across(terms[turn], turn, [(1, 1), (2, 2)]).astype(F32)
    far_terms = after(far_terms.astype(BF16), decs[-1][2])
    moved = [across(terms[turn], turn, [(0, 0), (3, 3)]) for turn in range(1, shards)]
    moved.append(lax.ppermute(far_terms, PLANE, [(2, 0), (1, 3)]))

    dec_here = jnp.concatenate([jnp.where(y == 0, d[0], d[1]) for d in decs], 1)
    dec_there = jnp.concatenate([d[2] for d in decs], 1)
    dec_grads = ordered(y == 0, dec_here, dec_there, 1)
    kept = jnp.concatenate([w[:rows] for w in weight_sums], 1)
    got = [lax.ppermute(w[rows:], "y", SWAP) for w in weight_sums]
    if tiled:
        moved[0], dec_grads = lax.optimization_barrier((moved[0], dec_grads))
        grad_normed, gain_term = collect(
            at, [terms[0]] + moved, packed, here, inv_rms, gain.astype(F32)[None], pair_scale
        )
        gain_term = jnp.sum(gain_term, axis=(0, 1))
    else:
        grad_enc = terms[0].astype(F32)
        for part in moved:
            grad_enc = grad_enc + part.astype(F32)
        grad_normed = (grad_enc * gain.astype(F32)).astype(BF16)
        normed = raw[0].astype(F32) * inv_rms
        gain_term = pair_scale * jnp.sum(grad_enc * normed, axis=0)
    enc_grads = jnp.where(y == 0, grad_normed, lax.ppermute(grad_normed, PLANE, [(3, 2)]))

    gain_term = jnp.where(straight, gain_term, 0.0)
    gain_term = gain_term + lax.ppermute(gain_term, PLANE, [(0, 3), (3, 0), (1, 2), (2, 1)])
    turn = 1
    while turn < groups:
        gain_term = gain_term + lax.ppermute(gain_term, "z", [(i, i ^ turn) for i in range(groups)])
        turn *= 2
    d_gain = jnp.where(straight, gain_term, lax.ppermute(gain_term, "phase", SWAP))

    got = jnp.concatenate(got, 1)
    d_wkv = ordered(y == 0, kept, got, 1).astype(F32)
    sec_grads = jnp.where(core == 0, enc_grads, dec_grads)[None, None]
    return (sec_grads, d_wkv, d_gain)


def solution(mesh):
    size = mesh.shape
    split = (size["dp"] // 2, 2, size["phase"], size["mp"])
    fine = Mesh(mesh.devices.reshape(split), ("z", "y", "phase", "mp"))
    pairs = ("z", "y")
    acts = P("phase", pairs, None, "mp")
    weights = P(("z", "y", "phase"), "mp")
    return jax.shard_map(
        on_device,
        mesh=fine,
        in_specs=(acts, P("mp"), weights, P(pairs), P(pairs)),
        out_specs=(acts, weights, P("mp")),
        check_vma=False,
    )
```

```python
import jax
import jax.numpy as jnp
from jax import lax
from jax.experimental import pallas as pl
from jax.experimental.pallas import tpu as pltpu
from jax.sharding import Mesh, PartitionSpec as P

D = 4096
HEAD = 64
EPS = 1e-06
CHUNKS = 2
PARTS = 2
DIRECT = ()
F32 = jnp.float32
BF16 = jnp.bfloat16
NN = (((1,), (0,)), ((), ()))
NT = (((1,), (1,)), ((), ()))
TN = (((0,), (0,)), ((), ()))

PLANE = ("y", "phase")
SWAP = [(0, 1), (1, 0)]


def dot(a, b, dims=NN):
    return lax.dot_general(a, b, dims, preferred_element_type=F32)


def cost(flops, mib, exps=0):
    return pl.CostEstimate(flops=flops, bytes_accessed=mib << 20, transcendentals=exps)


def in_hbm(*arrays):
    return [pltpu.with_memory_space_constraint(a, pltpu.HBM) for a in arrays]


def params(mib):
    return pltpu.CompilerParams(vmem_limit_bytes=mib << 20)


def chosen(kind, *values):
    return jnp.where(kind == 0, values[0], jnp.where(kind == 1, values[1], values[2]))


def norm_kernel(groups, rows, at, *refs):
    nears, fars, (gain, own, other, inv_out, natural) = refs[:3], refs[3:6], refs[6:]
    x, y, core = at[1], at[2], at[3]
    width = nears[0].shape[1]
    near = chosen(at[0], *[r[...] for r in nears]).astype(F32)
    far = chosen(at[0], *[r[...] for r in fars]).astype(F32)
    total = jnp.sum(near * near, axis=-1, keepdims=True) + jnp.sum(far * far, axis=-1, keepdims=True)
    inv_rms = lax.rsqrt(total / D + EPS)
    inv_out[...] = jnp.broadcast_to(inv_rms, inv_out.shape)
    near_at = pl.ds(pl.multiple_of(x * width, width), width)
    far_at = pl.ds(pl.multiple_of((1 - x) * width, width), width)
    natural[:, near_at] = (near * inv_rms * gain[:, near_at]).astype(BF16)
    natural[:, far_at] = (far * inv_rms * gain[:, far_at]).astype(BF16)
    for group in range(groups):
        for k in range(2):
            row = 2 * group + (y if k == 0 else 1 - y)
            put = slice((2 * group + k) * rows, (2 * group + k + 1) * rows)
            for out, half in ((own, core), (other, 1 - core)):
                got = pl.multiple_of((2 * row + half) * rows, rows)
                out[:, put] = natural[:, pl.ds(got, rows)]


def norm(at, nears, fars, gain, groups, rows):
    length, width = nears[0].shape
    step = 128

    def pick(want):
        return pl.BlockSpec((step, width), lambda i, s: (jnp.where(s[0] == want, i, 0), 0))

    out = pl.BlockSpec((step, D // 2), lambda i, s: (i, 0))
    return pl.pallas_call(
        lambda *refs: norm_kernel(groups, rows, *refs),
        grid_spec=pltpu.PrefetchScalarGridSpec(
            num_scalar_prefetch=1,
            grid=(length // step,),
            in_specs=[pick(i % 3) for i in range(6)] + [pl.BlockSpec((1, D), lambda i, s: (0, 0))],
            out_specs=[out, out, pl.BlockSpec((step, 128), lambda i, s: (i, 0))],
            scratch_shapes=[pltpu.VMEM((step, D), BF16)],
        ),
        out_shape=[pltpu.HBM((length, D // 2), BF16)] * 2
        + [jax.ShapeDtypeStruct((length, 128), F32)],
        compiler_params=params(14),
        cost_estimate=cost(8 * length * D, 8),
        name="norm",
    )(at, *nears, *fars, gain)


def attend_head(bias, qg, kv):
    low_lane = lax.broadcasted_iota(jnp.int32, qg.shape, 1) < HEAD
    zero = jnp.zeros((), BF16)
    scaled = qg * jnp.asarray(1.0 / HEAD**0.5, BF16)
    queries = jnp.where(low_lane, scaled, zero)
    grads = jnp.where(low_lane, zero, scaled)
    scores = dot(queries, kv, NT) + bias
    grad_prob = dot(grads, kv, NT)
    weights = jnp.exp(scores - jnp.max(scores, axis=-1, keepdims=True))
    probs = weights * (1.0 / jnp.sum(weights, axis=-1, keepdims=True))
    prob_low = probs.astype(BF16)
    row_delta = jnp.sum(prob_low.astype(F32) * grad_prob, axis=-1, keepdims=True)
    grad_score = (probs * (grad_prob - row_delta)).astype(BF16)
    grad_query = dot(grad_score, kv)
    qg_t = qg.T
    key_t = dot(qg_t[:HEAD], grad_score)
    value_t = dot(qg_t[HEAD:], prob_low)
    gkv = jnp.concatenate([key_t, value_t], axis=0).T
    dec = jnp.where(low_lane, grad_query, pltpu.roll(gkv, HEAD, 1))
    return dec.astype(BF16), gkv.astype(BF16)


def attend_kernel(at, part, enc_other, w_other, *refs):
    qgs, (dec, gkv) = refs[:3], refs[3:]
    kv = (part[...] + dot(enc_other[...], w_other[...])).astype(BF16)
    keys = lax.broadcasted_iota(jnp.int32, (1, kv.shape[0]), 1)
    bias = jnp.where(keys < at[4], 0.0, -1e30).astype(F32)
    for head in range(kv.shape[1] // (2 * HEAD)):
        lanes = slice(head * 2 * HEAD, (head + 1) * 2 * HEAD)
        qg = chosen(at[5], *[r[:, lanes] for r in qgs])
        dec[:, lanes], gkv[:, lanes] = attend_head(bias, qg, kv[:, lanes])


def attend(at, part, enc_other, w_other, qgs, chunk):
    length = part.shape[0]
    half, cols = w_other.shape
    step = min(256, cols)
    first = chunk * (cols // step)
    enc = pl.BlockSpec((length, half), lambda i, s: (0, 0))
    weight = pl.BlockSpec((half, step), lambda i, s: (0, i))
    out = pl.BlockSpec((length, step), lambda i, s: (0, i))

    def pick(want):
        return pl.BlockSpec((length, step), lambda i, s: (0, jnp.where(s[5] == want, first + i, first)))

    return pl.pallas_call(
        attend_kernel,
        grid_spec=pltpu.PrefetchScalarGridSpec(
            num_scalar_prefetch=1,
            grid=(cols // step,),
            in_specs=[out, enc, weight, pick(0), pick(1), pick(2)],
            out_specs=[out, out],
        ),
        out_shape=[jax.ShapeDtypeStruct((length, cols), BF16)] * 2,
        compiler_params=params(26),
        cost_estimate=cost(
            length * cols * (4 * half + 14 * length), 8, length * length * cols // (2 * HEAD)
        ),
        name="attend",
    )(at, part, *in_hbm(enc_other, w_other, *qgs))


def weight_grad_kernel(scale, at, enc_a, enc_b, gkv_a, gkv_b, out):
    grad = scale * (dot(enc_a[...], gkv_a[...], TN) + dot(enc_b[...], gkv_b[...], TN))
    out[...] = grad.astype(BF16)


def weight_grad(at, enc_a, enc_b, gkv_a, gkv_b, groups, scale):
    length, half = enc_a.shape
    cols = gkv_a.shape[1]
    step = half // groups
    enc = pl.BlockSpec((length, step), lambda i, s: (0, i))
    gkv = pl.BlockSpec((length, cols), lambda i, s: (0, 0))
    return pl.pallas_call(
        lambda *refs: weight_grad_kernel(scale, *refs),
        grid_spec=pltpu.PrefetchScalarGridSpec(
            num_scalar_prefetch=1,
            grid=(groups,),
            in_specs=[enc, enc, gkv, gkv],
            out_specs=pl.BlockSpec((step, cols), lambda i, s: (i, 0)),
        ),
        out_shape=pltpu.HBM((half, cols), BF16),
        cost_estimate=cost(4 * length * half * cols // 64, 0),
        compiler_params=params(12),
        name="weight_grad",
    )(at, *in_hbm(enc_a, enc_b), gkv_a, gkv_b)


def collect_kernel(scale, at, *refs):
    terms, (local, here, inv, gain, out, gain_term) = refs[: 3 * PARTS], refs[3 * PARTS :]
    late = pl.program_id(0) >= pl.num_programs(0) // PARTS
    total = jnp.zeros(local.shape, F32)
    for i in range(0, 3 * PARTS, PARTS):
        total = total + jnp.where(late, terms[i + 1][...], terms[i][...]).astype(F32)
    out[...] = (total * gain[...]).astype(BF16)
    raw = jnp.where(at[0] == 0, local[...], here[...]).astype(F32)
    product = total * (raw * inv[:, :1])
    gain_term[0] = scale * jnp.sum(product, axis=0, keepdims=True)


def collect(at, terms, local, here, inv_rms, gain, scale):
    length, width = local.shape
    step = 128
    each = length // step // PARTS
    block = pl.BlockSpec((step, width), lambda i, s: (i, 0))

    def pick(want):
        return pl.BlockSpec((step, width), lambda i, s: (jnp.where(s[0] == want, i, 0), 0))

    def piece(part):
        return pl.BlockSpec((step, width), lambda i, s: (jnp.clip(i - part * each, 0, each - 1), 0))

    return pl.pallas_call(
        lambda *refs: collect_kernel(scale, *refs),
        grid_spec=pltpu.PrefetchScalarGridSpec(
            num_scalar_prefetch=1,
            grid=(length // step,),
            in_specs=[piece(0), piece(1)] * 3
            + [pick(0), pick(1)]
            + [
                pl.BlockSpec((step, 128), lambda i, s: (i, 0)),
                pl.BlockSpec((1, width), lambda i, s: (0, 0)),
            ],
            out_specs=[block, pl.BlockSpec((1, 1, width), lambda i, s: (i, 0, 0))],
        ),
        out_shape=[
            jax.ShapeDtypeStruct((length, width), BF16),
            jax.ShapeDtypeStruct((length // step, 1, width), F32),
        ],
        cost_estimate=cost(8 * length * width, 12),
        compiler_params=params(20),
        name="collect",
    )(at, *[p for term in terms for p in term], local, here, inv_rms, gain)


def enc_grad_kernel(at, gkv_0, gkv_1, own_0, own_1, other_0, other_1, *outs):
    rows = own_0.shape[0]
    own = dot(gkv_0[...], own_0[...], NT) + dot(gkv_1[...], own_1[...], NT)
    other = dot(gkv_0[...], other_0[...], NT) + dot(gkv_1[...], other_1[...], NT)
    first = at[3] == 0
    left = jnp.where(first, own, other).astype(BF16)
    right = jnp.where(first, other, own).astype(BF16)
    for i, out in enumerate(outs):
        part = slice(i * out.shape[0], (i + 1) * out.shape[0])
        out[:, :rows] = left[part]
        out[:, rows:] = right[part]


def enc_grad(at, gkvs, owns, others, groups, rows, shard):
    length, cols = gkvs[0].shape
    per_shard = groups // 2

    def block(i, s):
        target = lax.rem(s[1] + shard, 2)
        group = target * per_shard + i // 2
        return (2 * group + lax.rem(i + s[2], 2), 0)

    gkv = pl.BlockSpec((length, cols), lambda i, s: (0, 0))
    weight = pl.BlockSpec((rows, cols), block)
    return pl.pallas_call(
        enc_grad_kernel,
        grid_spec=pltpu.PrefetchScalarGridSpec(
            num_scalar_prefetch=1,
            grid=(groups,),
            in_specs=[gkv, gkv, weight, weight, weight, weight],
            out_specs=[pl.BlockSpec((length // PARTS, 2 * rows), lambda i, s: (0, i))] * PARTS,
        ),
        out_shape=[pltpu.HBM((length // PARTS, D // 2), BF16)] * PARTS,
        compiler_params=params(12),
        cost_estimate=cost(4 * length * D * cols, 8),
        name="enc_grad",
    )(at, *in_hbm(*gkvs, *owns, *others))


def cut(array, axis, index, size):
    return lax.dynamic_slice_in_dim(array, index * size, size, axis)


def ordered(first, own, other, axis):
    return jnp.where(
        first, jnp.concatenate([own, other], axis), jnp.concatenate([other, own], axis)
    )


def after(value, *others):
    return lax.optimization_barrier((value,) + others)[0]


def on_device(sec_acts, gain, w_kv, src_len, tgt_len):
    groups = lax.axis_size("z")
    shards = lax.axis_size("mp")
    z, y = lax.axis_index("z"), lax.axis_index("y")
    core, x = lax.axis_index("phase"), lax.axis_index("mp")
    straight = y == core
    packed = sec_acts[0, 0]
    length, width = packed.shape
    rows = w_kv.shape[0]
    half = width // 2
    cols = half // CHUNKS
    pair_scale = 1.0 / (2 * groups)
    tiled = shards == 2 and rows % 128 == 0

    def turned(count, by):
        return [(i, (i + by) % count) for i in range(count)]

    def across(value, turn, moves):
        return lax.ppermute(
            value,
            ("y", "phase", "mp"),
            [(a * shards + s, b * shards + (s + turn) % shards) for a, b in moves for s in range(shards)],
        )

    def chunk_of(side, k):
        return lax.dynamic_slice_in_dim(w_kv, side * half + k * cols, cols, 1)

    def slots(block):
        return [lax.ppermute(block, "z", turned(groups, -s)) for s in range(1, groups)]

    swapped = [lax.ppermute(chunk_of(1 - y, 0), "y", SWAP)]
    here = lax.ppermute(packed, PLANE, [(2, 3)])
    gain_sent, len_sent = lax.optimization_barrier((gain, src_len, here))[:2]
    gains = [gain] + [lax.ppermute(gain_sent, "mp", turned(shards, t)) for t in range(1, shards)]
    key_count = jnp.where(straight, src_len, lax.ppermute(len_sent, "y", SWAP))
    there = lax.ppermute(after(packed, swapped[0], key_count, *gains), PLANE, [(0, 2), (2, 1)])
    nears = [packed, here, there]
    fars = []
    for turn in range(1, shards):
        fars.append(
            [
                across(packed, turn, [(0, 0)]),
                across(here, turn, [(3, 3)]),
                across(there, turn, [(1, 1), (2, 2)]),
            ]
        )
    for k in range(1, CHUNKS):
        swapped.append(lax.ppermute(after(chunk_of(1 - y, k), there, fars[0][1]), "y", SWAP))
    blocks = [jnp.concatenate([chunk_of(y, k), swapped[k]], 0) for k in range(CHUNKS)]
    w_own, w_other = [], []

    position = lax.broadcasted_iota(jnp.int32, (length, width), 0)
    is_grad = lax.broadcasted_iota(jnp.int32, (length, width), 1) % (2 * HEAD) >= HEAD
    masked = jnp.where(is_grad & (position >= tgt_len[0]), jnp.zeros((), BF16), packed)
    qg_near, qg_far = cut(masked, 1, y, half), cut(masked, 1, 1 - y, half)
    qg_near, qg_far = lax.optimization_barrier((qg_near, qg_far, swapped[-1]))[:2]
    qgs = [
        qg_near,
        lax.ppermute(qg_near, PLANE, [(1, 0)]),
        lax.ppermute(qg_far, PLANE, [(1, 2), (3, 1)]),
    ]
    enc_kind = jnp.where(straight, y, 2)
    qg_kind = jnp.where(straight, 1 - y, 2)
    at = jnp.concatenate(
        [jnp.stack([enc_kind, x, y, core]).astype(jnp.int32), key_count, qg_kind[None]]
    )

    def natural(parts, axis):
        if shards == 2:
            return ordered(x == 0, parts[0], parts[1], axis)
        stacked = jnp.stack(parts)
        return jnp.concatenate(
            [
                lax.dynamic_index_in_dim(stacked, (x - i) % shards, 0, keepdims=False)
                for i in range(shards)
            ],
            axis,
        )

    block_group = jnp.arange(groups)
    block_pair = 2 * block_group[:, None] + jnp.stack([y, 1 - y])[None, :]
    block_order = (2 * block_pair[None] + jnp.stack([core, 1 - core])[:, None, None]).reshape(-1)
    gain_all = natural(gains, 0).astype(F32)

    if tiled:
        enc_own, enc_other, inv_rms = norm(
            at, nears, fars[0], after(gain_all[None], *qgs, *blocks), groups, rows
        )
    else:
        raw = [chosen(enc_kind, *parts) for parts in [nears] + fars]
        hidden = natural(raw, 1).astype(F32)
        inv_rms = lax.rsqrt(jnp.sum(hidden * hidden, axis=-1, keepdims=True) / D + EPS)
        encoded = (hidden * inv_rms * gain_all).astype(BF16)
        encoded = encoded.reshape(length, -1, rows)[:, block_order].reshape(length, 2, -1)
        enc_own, enc_other = encoded[:, 0], encoded[:, 1]
    enc_mate = lax.ppermute(enc_other, "phase", SWAP)

    decs, gkvs, weight_sums = [], [], []
    for k in range(CHUNKS):
        if k in DIRECT:
            pieces = [blocks[k]] + slots(after(blocks[k], w_own[0]))
            pieces = lax.optimization_barrier((*pieces, grad))[:-1]
            gathered = jnp.zeros((groups * 2 * rows, cols), BF16)
            for turn, piece in enumerate(pieces):
                start = (z + turn) % groups * 2 * rows
                gathered = lax.dynamic_update_slice_in_dim(gathered, piece, start, 0)
            w_own.append(gathered)
        else:
            block = blocks[k]
            w_own.append(lax.all_gather(block, "z", axis=0, tiled=True))
            if k > 0:
                w_own[k] = after(w_own[k], grad)
        w_other.append(lax.ppermute(w_own[k], "phase", SWAP))
        part = dot(enc_own, w_own[k])
        if k > 0:
            part = after(part, decs[0][0], decs[0][2])
        dec, gkv = attend(at, part, enc_other, w_other[k], qgs, k)
        gkvs.append(gkv)
        decs.append(
            (
                lax.ppermute(dec, PLANE, [(0, 1)]),
                dec,
                lax.ppermute(dec, PLANE, [(2, 1), (1, 3)]),
            )
        )
        gkv_sent = gkv
        if tiled and k == CHUNKS - 1:
            terms = [enc_grad(at, gkvs, w_own, w_other, groups, rows, s) for s in (1, 0)][::-1]
            gkv_sent = after(gkv, *terms[0], *terms[1])
        parts = jnp.split(gkv_sent, 2, axis=1)
        gkv_mate = jnp.concatenate([lax.ppermute(p, "phase", SWAP) for p in parts], 1)
        if tiled:
            grad = weight_grad(at, enc_own, enc_mate, gkv, gkv_mate, groups, pair_scale)
        else:
            grad = pair_scale * (dot(enc_own, gkv, TN) + dot(enc_mate, gkv_mate, TN))
            grad = grad.astype(BF16)
        weight_sums.append(lax.psum_scatter(grad, "z", scatter_dimension=0, tiled=True))

    if not tiled:
        gkv_all = jnp.concatenate(gkvs, 1)
        full = dot(gkv_all, jnp.concatenate([jnp.concatenate(w, 0) for w in zip(w_own, w_other)], 1), NT)
        back = jnp.zeros_like(block_order).at[block_order].set(jnp.arange(block_order.shape[0]))
        full = full.astype(BF16).reshape(length, -1, rows)[:, back].reshape(length, D)
        terms = [jnp.split(cut(full, 1, (x + s) % shards, width), PARTS) for s in range(shards)]
    far = []
    for part in range(PARTS):
        total = terms[0][part].astype(F32)
        for turn in range(1, shards):
            total = total + across(terms[turn][part], turn, [(1, 1), (2, 2)]).astype(F32)
        far.append(after(total.astype(BF16), decs[-1][2]))
    moved = [
        [across(part, turn, [(0, 0), (3, 3)]) for part in terms[turn]] for turn in range(1, shards)
    ]
    moved.append([lax.ppermute(part, PLANE, [(2, 0), (1, 3)]) for part in far])

    dec_here = jnp.concatenate([jnp.where(y == 0, d[0], d[1]) for d in decs], 1)
    dec_there = jnp.concatenate([d[2] for d in decs], 1)
    dec_grads = ordered(y == 0, dec_here, dec_there, 1)
    kept = jnp.concatenate([w[:rows] for w in weight_sums], 1)
    got = [lax.ppermute(w[rows:], "y", SWAP) for w in weight_sums]
    if tiled:
        moved[0][0], dec_grads, got[0] = lax.optimization_barrier((moved[0][0], dec_grads, got[0]))
        grad_normed, gain_term = collect(
            at, [terms[0]] + moved, packed, here, inv_rms, gain.astype(F32)[None], pair_scale
        )
        gain_term = jnp.sum(gain_term, axis=(0, 1))
    else:
        grad_enc = sum(jnp.concatenate(t, 0).astype(F32) for t in [terms[0]] + moved)
        grad_normed = (grad_enc * gain.astype(F32)).astype(BF16)
        normed = chosen(enc_kind, *nears).astype(F32) * inv_rms
        gain_term = pair_scale * jnp.sum(grad_enc * normed, axis=0)
    enc_grads = jnp.where(y == 0, grad_normed, lax.ppermute(grad_normed, PLANE, [(3, 2)]))
    sec_grads = jnp.where(core == 0, enc_grads, dec_grads)[None, None]

    gain_term = jnp.where(straight, gain_term, 0.0)
    gain_term = gain_term + lax.ppermute(gain_term, PLANE, [(0, 3), (3, 0), (1, 2), (2, 1)])
    turn = 1
    while turn < groups:
        if 2 * turn == groups:
            gain_term, sec_grads = lax.optimization_barrier((gain_term, sec_grads))
        gain_term = gain_term + lax.ppermute(gain_term, "z", [(i, i ^ turn) for i in range(groups)])
        turn *= 2
    d_gain = jnp.where(straight, gain_term, lax.ppermute(gain_term, "phase", SWAP))
    got = jnp.concatenate(got, 1)
    d_wkv = ordered(y == 0, kept, got, 1).astype(F32)
    return (sec_grads, d_wkv, d_gain)


def solution(mesh):
    size = mesh.shape
    split = (size["dp"] // 2, 2, size["phase"], size["mp"])
    fine = Mesh(mesh.devices.reshape(split), ("z", "y", "phase", "mp"))
    pairs = ("z", "y")
    acts = P("phase", pairs, None, "mp")
    weights = P(("z", "y", "phase"), "mp")
    return jax.shard_map(
        on_device,
        mesh=fine,
        in_specs=(acts, P("mp"), weights, P(pairs), P(pairs)),
        out_specs=(acts, weights, P("mp")),
        check_vma=False,
    )
```

```python
import jax
import jax.numpy as jnp
from jax import lax
from jax.experimental import pallas as pl
from jax.experimental.pallas import tpu as pltpu
from jax.sharding import Mesh, PartitionSpec as P

D = 4096
HEAD = 64
EPS = 1e-06
CHUNKS = 2
PARTS = 2
DIRECT = ()
F32 = jnp.float32
BF16 = jnp.bfloat16
NN = (((1,), (0,)), ((), ()))
NT = (((1,), (1,)), ((), ()))
TN = (((0,), (0,)), ((), ()))

PLANE = ("y", "phase")
SWAP = [(0, 1), (1, 0)]


def dot(a, b, dims=NN):
    return lax.dot_general(a, b, dims, preferred_element_type=F32)


def cost(flops, mib, exps=0):
    return pl.CostEstimate(flops=flops, bytes_accessed=mib << 20, transcendentals=exps)


def in_hbm(*arrays):
    return [pltpu.with_memory_space_constraint(a, pltpu.HBM) for a in arrays]


def params(mib):
    return pltpu.CompilerParams(vmem_limit_bytes=mib << 20)


def chosen(kind, *values):
    return jnp.where(kind == 0, values[0], jnp.where(kind == 1, values[1], values[2]))


def norm_kernel(groups, rows, at, *refs):
    nears, fars, (gain, own, other, inv_out, natural) = refs[:3], refs[3:6], refs[6:]
    x, y, core = at[1], at[2], at[3]
    width = nears[0].shape[1]
    near = chosen(at[0], *[r[...] for r in nears]).astype(F32)
    far = chosen(at[0], *[r[...] for r in fars]).astype(F32)
    total = jnp.sum(near * near, axis=-1, keepdims=True) + jnp.sum(far * far, axis=-1, keepdims=True)
    inv_rms = lax.rsqrt(total / D + EPS)
    inv_out[...] = jnp.broadcast_to(inv_rms, inv_out.shape)
    near_at = pl.ds(pl.multiple_of(x * width, width), width)
    far_at = pl.ds(pl.multiple_of((1 - x) * width, width), width)
    natural[:, near_at] = (near * inv_rms * gain[:, near_at]).astype(BF16)
    natural[:, far_at] = (far * inv_rms * gain[:, far_at]).astype(BF16)
    for group in range(groups):
        for k in range(2):
            row = 2 * group + (y if k == 0 else 1 - y)
            put = slice((2 * group + k) * rows, (2 * group + k + 1) * rows)
            for out, half in ((own, core), (other, 1 - core)):
                got = pl.multiple_of((2 * row + half) * rows, rows)
                out[:, put] = natural[:, pl.ds(got, rows)]


def norm(at, nears, fars, gain, groups, rows):
    length, width = nears[0].shape
    step = 128

    def pick(want):
        return pl.BlockSpec((step, width), lambda i, s: (jnp.where(s[0] == want, i, 0), 0))

    out = pl.BlockSpec((step, D // 2), lambda i, s: (i, 0))
    return pl.pallas_call(
        lambda *refs: norm_kernel(groups, rows, *refs),
        grid_spec=pltpu.PrefetchScalarGridSpec(
            num_scalar_prefetch=1,
            grid=(length // step,),
            in_specs=[pick(i % 3) for i in range(6)] + [pl.BlockSpec((1, D), lambda i, s: (0, 0))],
            out_specs=[out, out, pl.BlockSpec((step, 128), lambda i, s: (i, 0))],
            scratch_shapes=[pltpu.VMEM((step, D), BF16)],
        ),
        out_shape=[pltpu.HBM((length, D // 2), BF16)] * 2
        + [jax.ShapeDtypeStruct((length, 128), F32)],
        compiler_params=params(14),
        cost_estimate=cost(8 * length * D, 8),
        name="norm",
    )(at, *nears, *fars, gain)


def attend_head(bias, qg, kv):
    low_lane = lax.broadcasted_iota(jnp.int32, qg.shape, 1) < HEAD
    zero = jnp.zeros((), BF16)
    scaled = qg * jnp.asarray(1.0 / HEAD**0.5, BF16)
    queries = jnp.where(low_lane, scaled, zero)
    grads = jnp.where(low_lane, zero, scaled)
    scores = dot(queries, kv, NT) + bias
    grad_prob = dot(grads, kv, NT)
    weights = jnp.exp(scores - jnp.max(scores, axis=-1, keepdims=True))
    probs = weights * (1.0 / jnp.sum(weights, axis=-1, keepdims=True))
    prob_low = probs.astype(BF16)
    row_delta = jnp.sum(prob_low.astype(F32) * grad_prob, axis=-1, keepdims=True)
    grad_score = (probs * (grad_prob - row_delta)).astype(BF16)
    grad_query = dot(grad_score, kv)
    qg_t = qg.T
    key_t = dot(qg_t[:HEAD], grad_score)
    value_t = dot(qg_t[HEAD:], prob_low)
    gkv = jnp.concatenate([key_t, value_t], axis=0).T
    dec = jnp.where(low_lane, grad_query, pltpu.roll(gkv, HEAD, 1))
    return dec.astype(BF16), gkv.astype(BF16)


def attend_kernel(at, part, enc_other, w_other, *refs):
    qgs, (dec, gkv) = refs[:3], refs[3:]
    kv = (part[...] + dot(enc_other[...], w_other[...])).astype(BF16)
    keys = lax.broadcasted_iota(jnp.int32, (1, kv.shape[0]), 1)
    bias = jnp.where(keys < at[4], 0.0, -1e30).astype(F32)
    for head in range(kv.shape[1] // (2 * HEAD)):
        lanes = slice(head * 2 * HEAD, (head + 1) * 2 * HEAD)
        qg = chosen(at[5], *[r[:, lanes] for r in qgs])
        dec[:, lanes], gkv[:, lanes] = attend_head(bias, qg, kv[:, lanes])


def attend(at, part, enc_other, w_other, qgs, chunk):
    length = part.shape[0]
    half, cols = w_other.shape
    step = min(256, cols)
    first = chunk * (cols // step)
    enc = pl.BlockSpec((length, half), lambda i, s: (0, 0))
    weight = pl.BlockSpec((half, step), lambda i, s: (0, i))
    out = pl.BlockSpec((length, step), lambda i, s: (0, i))

    def pick(want):
        return pl.BlockSpec((length, step), lambda i, s: (0, jnp.where(s[5] == want, first + i, first)))

    return pl.pallas_call(
        attend_kernel,
        grid_spec=pltpu.PrefetchScalarGridSpec(
            num_scalar_prefetch=1,
            grid=(cols // step,),
            in_specs=[out, enc, weight, pick(0), pick(1), pick(2)],
            out_specs=[out, out],
        ),
        out_shape=[jax.ShapeDtypeStruct((length, cols), BF16)] * 2,
        compiler_params=params(26),
        cost_estimate=cost(
            length * cols * (4 * half + 14 * length), 8, length * length * cols // (2 * HEAD)
        ),
        name="attend",
    )(at, part, *in_hbm(enc_other, w_other, *qgs))


def weight_grad_kernel(scale, at, enc_a, enc_b, gkv_a, gkv_b, out):
    grad = scale * (dot(enc_a[...], gkv_a[...], TN) + dot(enc_b[...], gkv_b[...], TN))
    out[...] = grad.astype(BF16)


def weight_grad(at, enc_a, enc_b, gkv_a, gkv_b, groups, scale):
    length, half = enc_a.shape
    cols = gkv_a.shape[1]
    step = half // groups
    enc = pl.BlockSpec((length, step), lambda i, s: (0, i))
    gkv = pl.BlockSpec((length, cols), lambda i, s: (0, 0))
    return pl.pallas_call(
        lambda *refs: weight_grad_kernel(scale, *refs),
        grid_spec=pltpu.PrefetchScalarGridSpec(
            num_scalar_prefetch=1,
            grid=(groups,),
            in_specs=[enc, enc, gkv, gkv],
            out_specs=pl.BlockSpec((step, cols), lambda i, s: (i, 0)),
        ),
        out_shape=pltpu.HBM((half, cols), BF16),
        cost_estimate=cost(4 * length * half * cols // 64, 0),
        compiler_params=params(12),
        name="weight_grad",
    )(at, *in_hbm(enc_a, enc_b), gkv_a, gkv_b)


def collect_kernel(scale, at, *refs):
    terms, (local, here, inv, gain, out, gain_term) = refs[: 3 * PARTS], refs[3 * PARTS :]
    late = pl.program_id(0) >= pl.num_programs(0) // PARTS
    total = jnp.zeros(local.shape, F32)
    for i in range(0, 3 * PARTS, PARTS):
        total = total + jnp.where(late, terms[i + 1][...], terms[i][...]).astype(F32)
    out[...] = (total * gain[...]).astype(BF16)
    raw = jnp.where(at[0] == 0, local[...], here[...]).astype(F32)
    product = total * (raw * inv[:, :1])
    gain_term[0] = scale * jnp.sum(product, axis=0, keepdims=True)


def collect(at, terms, local, here, inv_rms, gain, scale):
    length, width = local.shape
    step = 128
    each = length // step // PARTS
    block = pl.BlockSpec((step, width), lambda i, s: (i, 0))

    def pick(want):
        return pl.BlockSpec((step, width), lambda i, s: (jnp.where(s[0] == want, i, 0), 0))

    def piece(part):
        return pl.BlockSpec((step, width), lambda i, s: (jnp.clip(i - part * each, 0, each - 1), 0))

    return pl.pallas_call(
        lambda *refs: collect_kernel(scale, *refs),
        grid_spec=pltpu.PrefetchScalarGridSpec(
            num_scalar_prefetch=1,
            grid=(length // step,),
            in_specs=[piece(0), piece(1)] * 3
            + [pick(0), pick(1)]
            + [
                pl.BlockSpec((step, 128), lambda i, s: (i, 0)),
                pl.BlockSpec((1, width), lambda i, s: (0, 0)),
            ],
            out_specs=[block, pl.BlockSpec((1, 1, width), lambda i, s: (i, 0, 0))],
        ),
        out_shape=[
            jax.ShapeDtypeStruct((length, width), BF16),
            jax.ShapeDtypeStruct((length // step, 1, width), F32),
        ],
        cost_estimate=cost(8 * length * width, 12),
        compiler_params=params(20),
        name="collect",
    )(at, *[p for term in terms for p in term], local, here, inv_rms, gain)


def enc_grad_kernel(at, gkv_0, gkv_1, own_0, own_1, other_0, other_1, *outs):
    rows = own_0.shape[0]
    own = dot(gkv_0[...], own_0[...], NT) + dot(gkv_1[...], own_1[...], NT)
    other = dot(gkv_0[...], other_0[...], NT) + dot(gkv_1[...], other_1[...], NT)
    first = at[3] == 0
    left = jnp.where(first, own, other).astype(BF16)
    right = jnp.where(first, other, own).astype(BF16)
    for i, out in enumerate(outs):
        part = slice(i * out.shape[0], (i + 1) * out.shape[0])
        out[:, :rows] = left[part]
        out[:, rows:] = right[part]


def enc_grad(at, gkvs, owns, others, groups, rows, shard):
    length, cols = gkvs[0].shape
    per_shard = groups // 2

    def block(i, s):
        target = lax.rem(s[1] + shard, 2)
        group = target * per_shard + i // 2
        return (2 * group + lax.rem(i + s[2], 2), 0)

    gkv = pl.BlockSpec((length, cols), lambda i, s: (0, 0))
    weight = pl.BlockSpec((rows, cols), block)
    return pl.pallas_call(
        enc_grad_kernel,
        grid_spec=pltpu.PrefetchScalarGridSpec(
            num_scalar_prefetch=1,
            grid=(groups,),
            in_specs=[gkv, gkv, weight, weight, weight, weight],
            out_specs=[pl.BlockSpec((length // PARTS, 2 * rows), lambda i, s: (0, i))] * PARTS,
        ),
        out_shape=[pltpu.HBM((length // PARTS, D // 2), BF16)] * PARTS,
        compiler_params=params(12),
        cost_estimate=cost(4 * length * D * cols, 8),
        name="enc_grad",
    )(at, *in_hbm(*gkvs, *owns, *others))


def cut(array, axis, index, size):
    return lax.dynamic_slice_in_dim(array, index * size, size, axis)


def ordered(first, own, other, axis):
    return jnp.where(
        first, jnp.concatenate([own, other], axis), jnp.concatenate([other, own], axis)
    )


def after(value, *others):
    return lax.optimization_barrier((value,) + others)[0]


def on_device(sec_acts, gain, w_kv, src_len, tgt_len):
    groups = lax.axis_size("z")
    shards = lax.axis_size("mp")
    z, y = lax.axis_index("z"), lax.axis_index("y")
    core, x = lax.axis_index("phase"), lax.axis_index("mp")
    straight = y == core
    packed = sec_acts[0, 0]
    length, width = packed.shape
    rows = w_kv.shape[0]
    half = width // 2
    cols = half // CHUNKS
    pair_scale = 1.0 / (2 * groups)
    tiled = shards == 2 and rows % 128 == 0

    def turned(count, by):
        return [(i, (i + by) % count) for i in range(count)]

    def across(value, turn, moves):
        return lax.ppermute(
            value,
            ("y", "phase", "mp"),
            [(a * shards + s, b * shards + (s + turn) % shards) for a, b in moves for s in range(shards)],
        )

    def chunk_of(side, k):
        return lax.dynamic_slice_in_dim(w_kv, side * half + k * cols, cols, 1)

    def slots(block):
        return [lax.ppermute(block, "z", turned(groups, -s)) for s in range(1, groups)]

    swapped = [lax.ppermute(chunk_of(1 - y, 0), "y", SWAP)]
    here = lax.ppermute(packed, PLANE, [(2, 3)])
    gains = [gain] + [
        lax.ppermute(after(gain, here), "mp", turned(shards, t)) for t in range(1, shards)
    ]
    blocks = [jnp.concatenate([chunk_of(y, 0), swapped[0]], 0)]
    there = lax.ppermute(after(packed, blocks[0]), PLANE, [(0, 2), (2, 1)])
    key_count = jnp.where(straight, src_len, lax.ppermute(after(src_len, there), "y", SWAP))
    nears = [packed, here, there]
    fars = []
    for turn in range(1, shards):
        fars.append(
            [
                across(after(packed, *gains), turn, [(0, 0)]),
                across(here, turn, [(3, 3)]),
                across(there, turn, [(1, 1), (2, 2)]),
            ]
        )
    for k in range(1, CHUNKS):
        swapped.append(lax.ppermute(after(chunk_of(1 - y, k), there, fars[0][1]), "y", SWAP))
    blocks += [jnp.concatenate([chunk_of(y, k), swapped[k]], 0) for k in range(1, CHUNKS)]
    w_own, w_other = [], []

    position = lax.broadcasted_iota(jnp.int32, (length, width), 0)
    is_grad = lax.broadcasted_iota(jnp.int32, (length, width), 1) % (2 * HEAD) >= HEAD
    masked = jnp.where(is_grad & (position >= tgt_len[0]), jnp.zeros((), BF16), packed)
    qg_near, qg_far = cut(masked, 1, y, half), cut(masked, 1, 1 - y, half)
    qg_near, qg_far = lax.optimization_barrier((qg_near, qg_far, swapped[-1]))[:2]
    qgs = [
        qg_near,
        lax.ppermute(qg_near, PLANE, [(1, 0)]),
        lax.ppermute(qg_far, PLANE, [(1, 2), (3, 1)]),
    ]
    enc_kind = jnp.where(straight, y, 2)
    qg_kind = jnp.where(straight, 1 - y, 2)
    at = jnp.concatenate(
        [jnp.stack([enc_kind, x, y, core]).astype(jnp.int32), key_count, qg_kind[None]]
    )

    def natural(parts, axis):
        if shards == 2:
            return ordered(x == 0, parts[0], parts[1], axis)
        stacked = jnp.stack(parts)
        return jnp.concatenate(
            [
                lax.dynamic_index_in_dim(stacked, (x - i) % shards, 0, keepdims=False)
                for i in range(shards)
            ],
            axis,
        )

    block_group = jnp.arange(groups)
    block_pair = 2 * block_group[:, None] + jnp.stack([y, 1 - y])[None, :]
    block_order = (2 * block_pair[None] + jnp.stack([core, 1 - core])[:, None, None]).reshape(-1)
    gain_all = natural(gains, 0).astype(F32)

    if tiled:
        enc_own, enc_other, inv_rms = norm(
            at, nears, fars[0], after(gain_all[None], *qgs, *blocks), groups, rows
        )
    else:
        raw = [chosen(enc_kind, *parts) for parts in [nears] + fars]
        hidden = natural(raw, 1).astype(F32)
        inv_rms = lax.rsqrt(jnp.sum(hidden * hidden, axis=-1, keepdims=True) / D + EPS)
        encoded = (hidden * inv_rms * gain_all).astype(BF16)
        encoded = encoded.reshape(length, -1, rows)[:, block_order].reshape(length, 2, -1)
        enc_own, enc_other = encoded[:, 0], encoded[:, 1]
    enc_mate = lax.ppermute(enc_other, "phase", SWAP)

    decs, gkvs, weight_sums = [], [], []
    for k in range(CHUNKS):
        if k in DIRECT:
            pieces = [blocks[k]] + slots(after(blocks[k], w_own[0]))
            pieces = lax.optimization_barrier((*pieces, grad))[:-1]
            gathered = jnp.zeros((groups * 2 * rows, cols), BF16)
            for turn, piece in enumerate(pieces):
                start = (z + turn) % groups * 2 * rows
                gathered = lax.dynamic_update_slice_in_dim(gathered, piece, start, 0)
            w_own.append(gathered)
        else:
            block = blocks[k]
            w_own.append(lax.all_gather(block, "z", axis=0, tiled=True))
            if k > 0:
                w_own[k] = after(w_own[k], grad)
        w_other.append(lax.ppermute(w_own[k], "phase", SWAP))
        dec, gkv = attend(at, dot(enc_own, w_own[k]), enc_other, w_other[k], qgs, k)
        gkvs.append(gkv)
        decs.append(
            (
                lax.ppermute(dec, PLANE, [(0, 1)]),
                dec,
                lax.ppermute(dec, PLANE, [(2, 1), (1, 3)]),
            )
        )
        last = k == CHUNKS - 1
        parts = jnp.split(gkv, 2, axis=1)
        gkv_mate = jnp.concatenate([lax.ppermute(p, "phase", SWAP) for p in parts], 1)
        if tiled:
            if last:
                away = enc_grad(at, gkvs, w_own, w_other, groups, rows, 1)
                gkv_mate = after(gkv_mate, *away)
            else:
                gkv_mate = after(gkv_mate, decs[k][0], decs[k][2])
            grad = weight_grad(at, enc_own, enc_mate, gkv, gkv_mate, groups, pair_scale)
            if last:
                kept = [after(gkvs[0], grad)] + gkvs[1:]
                terms = [enc_grad(at, kept, w_own, w_other, groups, rows, 0), away]
        else:
            grad = pair_scale * (dot(enc_own, gkv, TN) + dot(enc_mate, gkv_mate, TN))
            grad = grad.astype(BF16)
        weight_sums.append(lax.psum_scatter(grad, "z", scatter_dimension=0, tiled=True))

    if not tiled:
        gkv_all = jnp.concatenate(gkvs, 1)
        full = dot(gkv_all, jnp.concatenate([jnp.concatenate(w, 0) for w in zip(w_own, w_other)], 1), NT)
        back = jnp.zeros_like(block_order).at[block_order].set(jnp.arange(block_order.shape[0]))
        full = full.astype(BF16).reshape(length, -1, rows)[:, back].reshape(length, D)
        terms = [jnp.split(cut(full, 1, (x + s) % shards, width), PARTS) for s in range(shards)]
    kept = jnp.concatenate([w[:rows] for w in weight_sums], 1)
    got = [lax.ppermute(w[rows:], "y", SWAP) for w in weight_sums]
    far, first_far = [], None
    for part in range(PARTS):
        total = terms[0][part].astype(F32)
        for turn in range(1, shards):
            term = across(terms[turn][part], turn, [(1, 1), (2, 2)])
            first_far = term if first_far is None else first_far
            total = total + term.astype(F32)
        done = decs[-1][2] if part == 0 else got[0]
        far.append(after(total.astype(BF16), done))
    moved = [
        [across(after(part, first_far), turn, [(0, 0), (3, 3)]) for part in terms[turn]]
        for turn in range(1, shards)
    ]
    moved.append([lax.ppermute(part, PLANE, [(2, 0), (1, 3)]) for part in far])

    dec_here = jnp.concatenate([jnp.where(y == 0, d[0], d[1]) for d in decs], 1)
    dec_there = jnp.concatenate([d[2] for d in decs], 1)
    dec_grads = ordered(y == 0, dec_here, dec_there, 1)
    if tiled:
        moved[0][0], dec_grads = lax.optimization_barrier((moved[0][0], dec_grads))
        grad_normed, gain_term = collect(
            at, [terms[0]] + moved, packed, here, inv_rms, gain.astype(F32)[None], pair_scale
        )
        gain_term = jnp.sum(gain_term, axis=(0, 1))
    else:
        grad_enc = sum(jnp.concatenate(t, 0).astype(F32) for t in [terms[0]] + moved)
        grad_normed = (grad_enc * gain.astype(F32)).astype(BF16)
        normed = chosen(enc_kind, *nears).astype(F32) * inv_rms
        gain_term = pair_scale * jnp.sum(grad_enc * normed, axis=0)
    enc_grads = jnp.where(y == 0, grad_normed, lax.ppermute(grad_normed, PLANE, [(3, 2)]))
    sec_grads = jnp.where(core == 0, enc_grads, dec_grads)[None, None]

    gain_term = jnp.where(straight, gain_term, 0.0)
    gain_term = gain_term + lax.ppermute(gain_term, PLANE, [(0, 3), (3, 0), (1, 2), (2, 1)])
    turn = 1
    while turn < groups:
        if 2 * turn == groups:
            gain_term, sec_grads = lax.optimization_barrier((gain_term, sec_grads))
        gain_term = gain_term + lax.ppermute(gain_term, "z", [(i, i ^ turn) for i in range(groups)])
        turn *= 2
    d_gain = jnp.where(straight, gain_term, lax.ppermute(gain_term, "phase", SWAP))
    got = jnp.concatenate(got, 1)
    d_wkv = ordered(y == 0, kept, got, 1).astype(F32)
    return (sec_grads, d_wkv, d_gain)


def solution(mesh):
    size = mesh.shape
    split = (size["dp"] // 2, 2, size["phase"], size["mp"])
    fine = Mesh(mesh.devices.reshape(split), ("z", "y", "phase", "mp"))
    pairs = ("z", "y")
    acts = P("phase", pairs, None, "mp")
    weights = P(("z", "y", "phase"), "mp")
    return jax.shard_map(
        on_device,
        mesh=fine,
        in_specs=(acts, P("mp"), weights, P(pairs), P(pairs)),
        out_specs=(acts, weights, P("mp")),
        check_vma=False,
    )
```

```python
import jax
import jax.numpy as jnp
from jax import lax
from jax.experimental import pallas as pl
from jax.experimental.pallas import tpu as pltpu
from jax.sharding import Mesh, PartitionSpec as P

D = 4096
HEAD = 64
EPS = 1e-06
CHUNKS = 2
PARTS = 2
DIRECT = ()
F32 = jnp.float32
BF16 = jnp.bfloat16
NN = (((1,), (0,)), ((), ()))
NT = (((1,), (1,)), ((), ()))
TN = (((0,), (0,)), ((), ()))

PLANE = ("y", "phase")
SWAP = [(0, 1), (1, 0)]


def dot(a, b, dims=NN):
    return lax.dot_general(a, b, dims, preferred_element_type=F32)


def cost(flops, mib, exps=0):
    return pl.CostEstimate(flops=flops, bytes_accessed=mib << 20, transcendentals=exps)


def in_hbm(*arrays):
    return [pltpu.with_memory_space_constraint(a, pltpu.HBM) for a in arrays]


def params(mib):
    return pltpu.CompilerParams(vmem_limit_bytes=mib << 20)


def chosen(kind, *values):
    return jnp.where(kind == 0, values[0], jnp.where(kind == 1, values[1], values[2]))


def norm_kernel(groups, rows, at, *refs):
    nears, fars, (gain, own, other, inv_out, natural) = refs[:3], refs[3:6], refs[6:]
    x, y, core = at[1], at[2], at[3]
    width = nears[0].shape[1]
    near = chosen(at[0], *[r[...] for r in nears]).astype(F32)
    far = chosen(at[0], *[r[...] for r in fars]).astype(F32)
    total = jnp.sum(near * near, axis=-1, keepdims=True) + jnp.sum(far * far, axis=-1, keepdims=True)
    inv_rms = lax.rsqrt(total / D + EPS)
    inv_out[...] = jnp.broadcast_to(inv_rms, inv_out.shape)
    near_at = pl.ds(pl.multiple_of(x * width, width), width)
    far_at = pl.ds(pl.multiple_of((1 - x) * width, width), width)
    natural[:, near_at] = (near * inv_rms * gain[:, near_at]).astype(BF16)
    natural[:, far_at] = (far * inv_rms * gain[:, far_at]).astype(BF16)
    for group in range(groups):
        for k in range(2):
            row = 2 * group + (y if k == 0 else 1 - y)
            put = slice((2 * group + k) * rows, (2 * group + k + 1) * rows)
            for out, half in ((own, core), (other, 1 - core)):
                got = pl.multiple_of((2 * row + half) * rows, rows)
                out[:, put] = natural[:, pl.ds(got, rows)]


def norm(at, nears, fars, gain, groups, rows):
    length, width = nears[0].shape
    step = 128

    def pick(want):
        return pl.BlockSpec((step, width), lambda i, s: (jnp.where(s[0] == want, i, 0), 0))

    out = pl.BlockSpec((step, D // 2), lambda i, s: (i, 0))
    return pl.pallas_call(
        lambda *refs: norm_kernel(groups, rows, *refs),
        grid_spec=pltpu.PrefetchScalarGridSpec(
            num_scalar_prefetch=1,
            grid=(length // step,),
            in_specs=[pick(i % 3) for i in range(6)] + [pl.BlockSpec((1, D), lambda i, s: (0, 0))],
            out_specs=[out, out, pl.BlockSpec((step, 128), lambda i, s: (i, 0))],
            scratch_shapes=[pltpu.VMEM((step, D), BF16)],
        ),
        out_shape=[pltpu.HBM((length, D // 2), BF16)] * 2
        + [jax.ShapeDtypeStruct((length, 128), F32)],
        compiler_params=params(14),
        cost_estimate=cost(8 * length * D, 8),
        name="norm",
    )(at, *nears, *fars, gain)


def attend_head(bias, qg, kv):
    low_lane = lax.broadcasted_iota(jnp.int32, qg.shape, 1) < HEAD
    zero = jnp.zeros((), BF16)
    scaled = qg * jnp.asarray(1.0 / HEAD**0.5, BF16)
    queries = jnp.where(low_lane, scaled, zero)
    grads = jnp.where(low_lane, zero, scaled)
    scores = dot(queries, kv, NT) + bias
    grad_prob = dot(grads, kv, NT)
    weights = jnp.exp(scores - jnp.max(scores, axis=-1, keepdims=True))
    probs = weights * (1.0 / jnp.sum(weights, axis=-1, keepdims=True))
    prob_low = probs.astype(BF16)
    row_delta = jnp.sum(prob_low.astype(F32) * grad_prob, axis=-1, keepdims=True)
    grad_score = (probs * (grad_prob - row_delta)).astype(BF16)
    grad_query = dot(grad_score, kv)
    qg_t = qg.T
    key_t = dot(qg_t[:HEAD], grad_score)
    value_t = dot(qg_t[HEAD:], prob_low)
    gkv = jnp.concatenate([key_t, value_t], axis=0).T
    dec = jnp.where(low_lane, grad_query, pltpu.roll(gkv, HEAD, 1))
    return dec.astype(BF16), gkv.astype(BF16)


def attend_kernel(at, part, enc_other, w_other, *refs):
    qgs, (dec, gkv) = refs[:3], refs[-2:]
    kv = (part[...] + dot(enc_other[...], w_other[...])).astype(BF16)
    keys = lax.broadcasted_iota(jnp.int32, (1, kv.shape[0]), 1)
    bias = jnp.where(keys < at[4], 0.0, -1e30).astype(F32)
    for head in range(kv.shape[1] // (2 * HEAD)):
        lanes = slice(head * 2 * HEAD, (head + 1) * 2 * HEAD)
        qg = chosen(at[5], *[r[:, lanes] for r in qgs])
        dec[:, lanes], gkv[:, lanes] = attend_head(bias, qg, kv[:, lanes])


def attend(at, part, enc_other, w_other, qgs, chunk, dec_before):
    length = part.shape[0]
    half, cols = w_other.shape
    step = min(256, cols)
    first = chunk * (cols // step)
    before = [] if dec_before is None else [dec_before]
    enc = pl.BlockSpec((length, half), lambda i, s: (0, 0))
    weight = pl.BlockSpec((half, step), lambda i, s: (0, i))
    out = pl.BlockSpec((length, step), lambda i, s: (0, i))

    def pick(want):
        return pl.BlockSpec((length, step), lambda i, s: (0, jnp.where(s[5] == want, first + i, first)))

    return pl.pallas_call(
        attend_kernel,
        grid_spec=pltpu.PrefetchScalarGridSpec(
            num_scalar_prefetch=1,
            grid=(cols // step,),
            in_specs=[out, enc, weight, pick(0), pick(1), pick(2)] + [pl.BlockSpec(memory_space=pl.ANY)] * len(before),
            out_specs=[pl.BlockSpec((length, step), lambda i, s: (0, first + i)), out],
        ),
        out_shape=[pltpu.HBM(qgs[0].shape, BF16), jax.ShapeDtypeStruct((length, cols), BF16)],
        input_output_aliases={7: 0} if before else {},
        compiler_params=params(26),
        cost_estimate=cost(
            length * cols * (4 * half + 14 * length), 8, length * length * cols // (2 * HEAD)
        ),
        name="attend",
    )(at, part, *in_hbm(enc_other, w_other, *qgs), *before)


def weight_grad_kernel(scale, at, enc_a, enc_b, gkv_a, gkv_b, out):
    grad = scale * (dot(enc_a[...], gkv_a[...], TN) + dot(enc_b[...], gkv_b[...], TN))
    out[...] = grad.astype(BF16)


def weight_grad(at, enc_a, enc_b, gkv_a, gkv_b, groups, scale):
    length, half = enc_a.shape
    cols = gkv_a.shape[1]
    step = half // groups
    enc = pl.BlockSpec((length, step), lambda i, s: (0, i))
    gkv = pl.BlockSpec((length, cols), lambda i, s: (0, 0))
    return pl.pallas_call(
        lambda *refs: weight_grad_kernel(scale, *refs),
        grid_spec=pltpu.PrefetchScalarGridSpec(
            num_scalar_prefetch=1,
            grid=(groups,),
            in_specs=[enc, enc, gkv, gkv],
            out_specs=pl.BlockSpec((step, cols), lambda i, s: (i, 0)),
        ),
        out_shape=pltpu.HBM((half, cols), BF16),
        cost_estimate=cost(4 * length * half * cols // 64, 0),
        compiler_params=params(12),
        name="weight_grad",
    )(at, *in_hbm(enc_a, enc_b), gkv_a, gkv_b)


def collect_kernel(scale, at, *refs):
    terms, (local, here, inv, gain, out, gain_term) = refs[: 3 * PARTS], refs[3 * PARTS :]
    late = pl.program_id(0) >= pl.num_programs(0) // PARTS
    total = jnp.zeros(local.shape, F32)
    for i in range(0, 3 * PARTS, PARTS):
        total = total + jnp.where(late, terms[i + 1][...], terms[i][...]).astype(F32)
    out[...] = (total * gain[...]).astype(BF16)
    raw = jnp.where(at[0] == 0, local[...], here[...]).astype(F32)
    product = total * (raw * inv[:, :1])
    gain_term[0] = scale * jnp.sum(product, axis=0, keepdims=True)


def collect(at, terms, local, here, inv_rms, gain, scale):
    length, width = local.shape
    step = 128
    each = length // step // PARTS
    block = pl.BlockSpec((step, width), lambda i, s: (i, 0))

    def pick(want):
        return pl.BlockSpec((step, width), lambda i, s: (jnp.where(s[0] == want, i, 0), 0))

    def piece(part):
        return pl.BlockSpec((step, width), lambda i, s: (jnp.clip(i - part * each, 0, each - 1), 0))

    return pl.pallas_call(
        lambda *refs: collect_kernel(scale, *refs),
        grid_spec=pltpu.PrefetchScalarGridSpec(
            num_scalar_prefetch=1,
            grid=(length // step,),
            in_specs=[piece(0), piece(1)] * 3
            + [pick(0), pick(1)]
            + [
                pl.BlockSpec((step, 128), lambda i, s: (i, 0)),
                pl.BlockSpec((1, width), lambda i, s: (0, 0)),
            ],
            out_specs=[block, pl.BlockSpec((1, 1, width), lambda i, s: (i, 0, 0))],
        ),
        out_shape=[
            jax.ShapeDtypeStruct((length, width), BF16),
            jax.ShapeDtypeStruct((length // step, 1, width), F32),
        ],
        cost_estimate=cost(8 * length * width, 12),
        compiler_params=params(20),
        name="collect",
    )(at, *[p for term in terms for p in term], local, here, inv_rms, gain)


def enc_grad_kernel(at, gkv_0, gkv_1, own_0, own_1, other_0, other_1, *outs):
    rows = own_0.shape[0]
    own = dot(gkv_0[...], own_0[...], NT) + dot(gkv_1[...], own_1[...], NT)
    other = dot(gkv_0[...], other_0[...], NT) + dot(gkv_1[...], other_1[...], NT)
    first = at[3] == 0
    left = jnp.where(first, own, other).astype(BF16)
    right = jnp.where(first, other, own).astype(BF16)
    for i, out in enumerate(outs):
        part = slice(i * out.shape[0], (i + 1) * out.shape[0])
        out[:, :rows] = left[part]
        out[:, rows:] = right[part]


def enc_grad(at, gkvs, owns, others, groups, rows, shard):
    length, cols = gkvs[0].shape
    per_shard = groups // 2

    def block(i, s):
        target = lax.rem(s[1] + shard, 2)
        group = target * per_shard + i // 2
        return (2 * group + lax.rem(i + s[2], 2), 0)

    gkv = pl.BlockSpec((length, cols), lambda i, s: (0, 0))
    weight = pl.BlockSpec((rows, cols), block)
    return pl.pallas_call(
        enc_grad_kernel,
        grid_spec=pltpu.PrefetchScalarGridSpec(
            num_scalar_prefetch=1,
            grid=(groups,),
            in_specs=[gkv, gkv, weight, weight, weight, weight],
            out_specs=[pl.BlockSpec((length // PARTS, 2 * rows), lambda i, s: (0, i))] * PARTS,
        ),
        out_shape=[pltpu.HBM((length // PARTS, D // 2), BF16)] * PARTS,
        compiler_params=params(12),
        cost_estimate=cost(4 * length * D * cols, 8),
        name="enc_grad",
    )(at, *in_hbm(*gkvs, *owns, *others))


def cut(array, axis, index, size):
    return lax.dynamic_slice_in_dim(array, index * size, size, axis)


def ordered(first, own, other, axis):
    return jnp.where(
        first, jnp.concatenate([own, other], axis), jnp.concatenate([other, own], axis)
    )


def after(value, *others):
    return lax.optimization_barrier((value,) + others)[0]


def on_device(sec_acts, gain, w_kv, src_len, tgt_len):
    groups = lax.axis_size("z")
    shards = lax.axis_size("mp")
    z, y = lax.axis_index("z"), lax.axis_index("y")
    core, x = lax.axis_index("phase"), lax.axis_index("mp")
    straight = y == core
    packed = sec_acts[0, 0]
    length, width = packed.shape
    rows = w_kv.shape[0]
    half = width // 2
    cols = half // CHUNKS
    pair_scale = 1.0 / (2 * groups)
    tiled = shards == 2 and rows % 128 == 0

    def turned(count, by):
        return [(i, (i + by) % count) for i in range(count)]

    def across(value, turn, moves):
        return lax.ppermute(
            value,
            ("y", "phase", "mp"),
            [(a * shards + s, b * shards + (s + turn) % shards) for a, b in moves for s in range(shards)],
        )

    def chunk_of(side, k):
        return lax.dynamic_slice_in_dim(w_kv, side * half + k * cols, cols, 1)

    def slots(block):
        return [lax.ppermute(block, "z", turned(groups, -s)) for s in range(1, groups)]

    swapped = [lax.ppermute(chunk_of(1 - y, 0), "y", SWAP)]
    here = lax.ppermute(packed, PLANE, [(2, 3)])
    gains = [gain] + [
        lax.ppermute(after(gain, here), "mp", turned(shards, t)) for t in range(1, shards)
    ]
    blocks = [jnp.concatenate([chunk_of(y, 0), swapped[0]], 0)]
    there = lax.ppermute(after(packed, blocks[0]), PLANE, [(0, 2), (2, 1)])
    key_count = jnp.where(straight, src_len, lax.ppermute(after(src_len, there), "y", SWAP))
    nears = [packed, here, there]
    fars = []
    for turn in range(1, shards):
        fars.append(
            [
                across(after(packed, *gains), turn, [(0, 0)]),
                across(here, turn, [(3, 3)]),
                across(there, turn, [(1, 1), (2, 2)]),
            ]
        )
    for k in range(1, CHUNKS):
        swapped.append(lax.ppermute(after(chunk_of(1 - y, k), there, fars[0][1]), "y", SWAP))
    blocks += [jnp.concatenate([chunk_of(y, k), swapped[k]], 0) for k in range(1, CHUNKS)]
    w_own, w_other = [], []

    position = lax.broadcasted_iota(jnp.int32, (length, width), 0)
    is_grad = lax.broadcasted_iota(jnp.int32, (length, width), 1) % (2 * HEAD) >= HEAD
    masked = jnp.where(is_grad & (position >= tgt_len[0]), jnp.zeros((), BF16), packed)
    qg_near, qg_far = cut(masked, 1, y, half), cut(masked, 1, 1 - y, half)
    qg_near, qg_far = lax.optimization_barrier((qg_near, qg_far, swapped[-1], key_count))[:2]
    qgs = [
        qg_near,
        lax.ppermute(qg_near, PLANE, [(1, 0)]),
        lax.ppermute(qg_far, PLANE, [(1, 2), (3, 1)]),
    ]
    enc_kind = jnp.where(straight, y, 2)
    qg_kind = jnp.where(straight, 1 - y, 2)
    at = jnp.concatenate(
        [jnp.stack([enc_kind, x, y, core]).astype(jnp.int32), key_count, qg_kind[None]]
    )

    def natural(parts, axis):
        if shards == 2:
            return ordered(x == 0, parts[0], parts[1], axis)
        stacked = jnp.stack(parts)
        return jnp.concatenate(
            [
                lax.dynamic_index_in_dim(stacked, (x - i) % shards, 0, keepdims=False)
                for i in range(shards)
            ],
            axis,
        )

    block_group = jnp.arange(groups)
    block_pair = 2 * block_group[:, None] + jnp.stack([y, 1 - y])[None, :]
    block_order = (2 * block_pair[None] + jnp.stack([core, 1 - core])[:, None, None]).reshape(-1)
    gain_all = natural(gains, 0).astype(F32)

    if tiled:
        enc_own, enc_other, inv_rms = norm(
            at, nears, fars[0], after(gain_all[None], *qgs, *blocks), groups, rows
        )
    else:
        raw = [chosen(enc_kind, *parts) for parts in [nears] + fars]
        hidden = natural(raw, 1).astype(F32)
        inv_rms = lax.rsqrt(jnp.sum(hidden * hidden, axis=-1, keepdims=True) / D + EPS)
        encoded = (hidden * inv_rms * gain_all).astype(BF16)
        encoded = encoded.reshape(length, -1, rows)[:, block_order].reshape(length, 2, -1)
        enc_own, enc_other = encoded[:, 0], encoded[:, 1]
    enc_mate = lax.ppermute(enc_other, "phase", SWAP)

    dec, gkvs, weight_sums = None, [], []
    for k in range(CHUNKS):
        if k in DIRECT:
            pieces = [blocks[k]] + slots(after(blocks[k], w_own[0]))
            pieces = lax.optimization_barrier((*pieces, grad))[:-1]
            gathered = jnp.zeros((groups * 2 * rows, cols), BF16)
            for turn, piece in enumerate(pieces):
                start = (z + turn) % groups * 2 * rows
                gathered = lax.dynamic_update_slice_in_dim(gathered, piece, start, 0)
            w_own.append(gathered)
        else:
            block = blocks[k]
            w_own.append(lax.all_gather(block, "z", axis=0, tiled=True))
            if k > 0:
                w_own[k] = after(w_own[k], grad)
        w_other.append(lax.ppermute(w_own[k], "phase", SWAP))
        dec, gkv = attend(at, dot(enc_own, w_own[k]), enc_other, w_other[k], qgs, k, dec)
        gkvs.append(gkv)
        last = k == CHUNKS - 1
        gkv_mate = lax.ppermute(gkv, "phase", SWAP)
        if tiled:
            if last:
                away = enc_grad(at, gkvs, w_own, w_other, groups, rows, 1)
                gkv_mate = after(gkv_mate, *away)
            grad = weight_grad(at, enc_own, enc_mate, gkv, gkv_mate, groups, pair_scale)
            if last:
                kept = [after(gkvs[0], grad)] + gkvs[1:]
                terms = [enc_grad(at, kept, w_own, w_other, groups, rows, 0), away]
        else:
            grad = pair_scale * (dot(enc_own, gkv, TN) + dot(enc_mate, gkv_mate, TN))
            grad = grad.astype(BF16)
        weight_sums.append(lax.psum_scatter(grad, "z", scatter_dimension=0, tiled=True))

    if not tiled:
        gkv_all = jnp.concatenate(gkvs, 1)
        full = dot(gkv_all, jnp.concatenate([jnp.concatenate(w, 0) for w in zip(w_own, w_other)], 1), NT)
        back = jnp.zeros_like(block_order).at[block_order].set(jnp.arange(block_order.shape[0]))
        full = full.astype(BF16).reshape(length, -1, rows)[:, back].reshape(length, D)
        terms = [jnp.split(cut(full, 1, (x + s) % shards, width), PARTS) for s in range(shards)]
    kept = jnp.concatenate([w[:rows] for w in weight_sums], 1)
    got = [lax.ppermute(w[rows:], "y", SWAP) for w in weight_sums]
    dec_here = jnp.where(y == 0, lax.ppermute(dec, PLANE, [(0, 1)]), dec)
    dec_there = lax.ppermute(dec, PLANE, [(2, 1), (1, 3)])
    dec_grads = ordered(y == 0, dec_here, dec_there, 1)

    far, first_far = [], None
    for part in range(PARTS):
        total = terms[0][part].astype(F32)
        for turn in range(1, shards):
            term = across(terms[turn][part], turn, [(1, 1), (2, 2)])
            first_far = term if first_far is None else first_far
            total = total + term.astype(F32)
        far.append(after(total.astype(BF16), dec_there, got[0]))
    moved = [
        [across(after(part, first_far), turn, [(0, 0), (3, 3)]) for part in terms[turn]]
        for turn in range(1, shards)
    ]
    moved.append([lax.ppermute(part, PLANE, [(2, 0), (1, 3)]) for part in far])

    if tiled:
        moved[0][0], dec_grads = lax.optimization_barrier((moved[0][0], dec_grads))
        grad_normed, gain_term = collect(
            at, [terms[0]] + moved, packed, here, inv_rms, gain.astype(F32)[None], pair_scale
        )
        gain_term = jnp.sum(gain_term, axis=(0, 1))
    else:
        grad_enc = sum(jnp.concatenate(t, 0).astype(F32) for t in [terms[0]] + moved)
        grad_normed = (grad_enc * gain.astype(F32)).astype(BF16)
        normed = chosen(enc_kind, *nears).astype(F32) * inv_rms
        gain_term = pair_scale * jnp.sum(grad_enc * normed, axis=0)
    enc_grads = jnp.where(y == 0, grad_normed, lax.ppermute(grad_normed, PLANE, [(3, 2)]))
    sec_grads = jnp.where(core == 0, enc_grads, dec_grads)[None, None]

    gain_term = jnp.where(straight, gain_term, 0.0)
    gain_term = gain_term + lax.ppermute(gain_term, PLANE, [(0, 3), (3, 0), (1, 2), (2, 1)])
    turn = 1
    while turn < groups:
        if 2 * turn == groups:
            gain_term, sec_grads = lax.optimization_barrier((gain_term, sec_grads))
        gain_term = gain_term + lax.ppermute(gain_term, "z", [(i, i ^ turn) for i in range(groups)])
        turn *= 2
    d_gain = jnp.where(straight, gain_term, lax.ppermute(gain_term, "phase", SWAP))
    got = jnp.concatenate(got, 1)
    d_wkv = ordered(y == 0, kept, got, 1).astype(F32)
    return (sec_grads, d_wkv, d_gain)


def solution(mesh):
    size = mesh.shape
    split = (size["dp"] // 2, 2, size["phase"], size["mp"])
    fine = Mesh(mesh.devices.reshape(split), ("z", "y", "phase", "mp"))
    pairs = ("z", "y")
    acts = P("phase", pairs, None, "mp")
    weights = P(("z", "y", "phase"), "mp")
    return jax.shard_map(
        on_device,
        mesh=fine,
        in_specs=(acts, P("mp"), weights, P(pairs), P(pairs)),
        out_specs=(acts, weights, P("mp")),
        check_vma=False,
    )
```

```python
import jax
import jax.numpy as jnp
from jax import lax
from jax.experimental import pallas as pl
from jax.experimental.pallas import tpu as pltpu
from jax.sharding import Mesh, PartitionSpec as P

D = 4096
HEAD = 64
EPS = 1e-06
CHUNKS = 2
PARTS = 2
DIRECT = ()
F32 = jnp.float32
BF16 = jnp.bfloat16
NN = (((1,), (0,)), ((), ()))
NT = (((1,), (1,)), ((), ()))
TN = (((0,), (0,)), ((), ()))

PLANE = ("y", "phase")
SWAP = [(0, 1), (1, 0)]


def dot(a, b, dims=NN):
    return lax.dot_general(a, b, dims, preferred_element_type=F32)


def cost(flops, mib, exps=0):
    return pl.CostEstimate(flops=flops, bytes_accessed=mib << 20, transcendentals=exps)


def in_hbm(*arrays):
    return [pltpu.with_memory_space_constraint(a, pltpu.HBM) for a in arrays]


def params(mib):
    return pltpu.CompilerParams(vmem_limit_bytes=mib << 20)


def chosen(kind, *values):
    return jnp.where(kind == 0, values[0], jnp.where(kind == 1, values[1], values[2]))


def norm_kernel(groups, rows, at, *refs):
    nears, fars, (gain, own, other, inv_out, natural) = refs[:3], refs[3:6], refs[6:]
    x, y, core = at[1], at[2], at[3]
    width = nears[0].shape[1]
    near = chosen(at[0], *[r[...] for r in nears]).astype(F32)
    far = chosen(at[0], *[r[...] for r in fars]).astype(F32)
    total = jnp.sum(near * near, axis=-1, keepdims=True) + jnp.sum(far * far, axis=-1, keepdims=True)
    inv_rms = lax.rsqrt(total / D + EPS)
    inv_out[...] = jnp.broadcast_to(inv_rms, inv_out.shape)
    near_at = pl.ds(pl.multiple_of(x * width, width), width)
    far_at = pl.ds(pl.multiple_of((1 - x) * width, width), width)
    natural[:, near_at] = (near * inv_rms * gain[:, near_at]).astype(BF16)
    natural[:, far_at] = (far * inv_rms * gain[:, far_at]).astype(BF16)
    for group in range(groups):
        for k in range(2):
            row = 2 * group + (y if k == 0 else 1 - y)
            put = slice((2 * group + k) * rows, (2 * group + k + 1) * rows)
            for out, half in ((own, core), (other, 1 - core)):
                got = pl.multiple_of((2 * row + half) * rows, rows)
                out[:, put] = natural[:, pl.ds(got, rows)]


def norm(at, nears, fars, gain, groups, rows):
    length, width = nears[0].shape
    step = 128

    def pick(want):
        return pl.BlockSpec((step, width), lambda i, s: (jnp.where(s[0] == want, i, 0), 0))

    out = pl.BlockSpec((step, D // 2), lambda i, s: (i, 0))
    return pl.pallas_call(
        lambda *refs: norm_kernel(groups, rows, *refs),
        grid_spec=pltpu.PrefetchScalarGridSpec(
            num_scalar_prefetch=1,
            grid=(length // step,),
            in_specs=[pick(i % 3) for i in range(6)] + [pl.BlockSpec((1, D), lambda i, s: (0, 0))],
            out_specs=[out, out, pl.BlockSpec((step, 128), lambda i, s: (i, 0))],
            scratch_shapes=[pltpu.VMEM((step, D), BF16)],
        ),
        out_shape=[pltpu.HBM((length, D // 2), BF16)] * 2
        + [jax.ShapeDtypeStruct((length, 128), F32)],
        compiler_params=params(14),
        cost_estimate=cost(8 * length * D, 8),
        name="norm",
    )(at, *nears, *fars, gain)


def attend_head(bias, qg, kv):
    low_lane = lax.broadcasted_iota(jnp.int32, qg.shape, 1) < HEAD
    zero = jnp.zeros((), BF16)
    scaled = qg * jnp.asarray(1.0 / HEAD**0.5, BF16)
    queries = jnp.where(low_lane, scaled, zero)
    grads = jnp.where(low_lane, zero, scaled)
    scores = dot(queries, kv, NT) + bias
    grad_prob = dot(grads, kv, NT)
    weights = jnp.exp(scores - jnp.max(scores, axis=-1, keepdims=True))
    probs = weights * (1.0 / jnp.sum(weights, axis=-1, keepdims=True))
    prob_low = probs.astype(BF16)
    row_delta = jnp.sum(prob_low.astype(F32) * grad_prob, axis=-1, keepdims=True)
    grad_score = (probs * (grad_prob - row_delta)).astype(BF16)
    grad_query = dot(grad_score, kv)
    qg_t = qg.T
    key_t = dot(qg_t[:HEAD], grad_score)
    value_t = dot(qg_t[HEAD:], prob_low)
    gkv = jnp.concatenate([key_t, value_t], axis=0).T
    dec = jnp.where(low_lane, grad_query, pltpu.roll(gkv, HEAD, 1))
    return dec.astype(BF16), gkv.astype(BF16)


def attend_kernel(at, part, enc_other, w_other, *refs):
    qgs, (dec, gkv) = refs[:3], refs[-2:]
    kv = (part[...] + dot(enc_other[...], w_other[...])).astype(BF16)
    keys = lax.broadcasted_iota(jnp.int32, (1, kv.shape[0]), 1)
    bias = jnp.where(keys < at[4], 0.0, -1e30).astype(F32)
    for head in range(kv.shape[1] // (2 * HEAD)):
        lanes = slice(head * 2 * HEAD, (head + 1) * 2 * HEAD)
        qg = chosen(at[5], *[r[:, lanes] for r in qgs])
        dec[:, lanes], gkv[:, lanes] = attend_head(bias, qg, kv[:, lanes])


def attend(at, part, enc_other, w_other, qgs, chunk, dec_before):
    length = part.shape[0]
    half, cols = w_other.shape
    step = min(256, cols)
    first = chunk * (cols // step)
    before = [] if dec_before is None else [dec_before]
    enc = pl.BlockSpec((length, half), lambda i, s: (0, 0))
    weight = pl.BlockSpec((half, step), lambda i, s: (0, i))
    out = pl.BlockSpec((length, step), lambda i, s: (0, i))

    def pick(want):
        return pl.BlockSpec((length, step), lambda i, s: (0, jnp.where(s[5] == want, first + i, first)))

    return pl.pallas_call(
        attend_kernel,
        grid_spec=pltpu.PrefetchScalarGridSpec(
            num_scalar_prefetch=1,
            grid=(cols // step,),
            in_specs=[out, enc, weight, pick(0), pick(1), pick(2)] + [pl.BlockSpec(memory_space=pl.ANY)] * len(before),
            out_specs=[pl.BlockSpec((length, step), lambda i, s: (0, first + i)), out],
        ),
        out_shape=[pltpu.HBM(qgs[0].shape, BF16), jax.ShapeDtypeStruct((length, cols), BF16)],
        input_output_aliases={7: 0} if before else {},
        compiler_params=params(26),
        cost_estimate=cost(
            length * cols * (4 * half + 14 * length), 8, length * length * cols // (2 * HEAD)
        ),
        name="attend",
    )(at, part, *in_hbm(enc_other, w_other, *qgs), *before)


def weight_grad_kernel(scale, at, enc_a, enc_b, gkv_a, gkv_b, out):
    grad = scale * (dot(enc_a[...], gkv_a[...], TN) + dot(enc_b[...], gkv_b[...], TN))
    out[...] = grad.astype(BF16)


def weight_grad(at, enc_a, enc_b, gkv_a, gkv_b, groups, scale):
    length, half = enc_a.shape
    cols = gkv_a.shape[1]
    step = half // groups
    enc = pl.BlockSpec((length, step), lambda i, s: (0, i))
    gkv = pl.BlockSpec((length, cols), lambda i, s: (0, 0))
    return pl.pallas_call(
        lambda *refs: weight_grad_kernel(scale, *refs),
        grid_spec=pltpu.PrefetchScalarGridSpec(
            num_scalar_prefetch=1,
            grid=(groups,),
            in_specs=[enc, enc, gkv, gkv],
            out_specs=pl.BlockSpec((step, cols), lambda i, s: (i, 0)),
        ),
        out_shape=pltpu.HBM((half, cols), BF16),
        cost_estimate=cost(4 * length * half * cols // 64, 0),
        compiler_params=params(12),
        name="weight_grad",
    )(at, *in_hbm(enc_a, enc_b), gkv_a, gkv_b)


def collect_kernel(scale, at, own, near, far, local, here, inv, gain, out, gain_term):
    total = own[...].astype(F32) + near[...].astype(F32) + far[...].astype(F32)
    out[...] = (total * gain[...]).astype(BF16)
    raw = jnp.where(at[0] == 0, local[...], here[...]).astype(F32)
    product = total * (raw * inv[:, :1])
    gain_term[0] = scale * jnp.sum(product, axis=0, keepdims=True)


def collect(at, terms, part, local, here, inv_rms, gain, scale):
    length, width = terms[0].shape
    step = 128
    first = part * (length // step)
    block = pl.BlockSpec((step, width), lambda i, s: (i, 0))

    def pick(want):
        return pl.BlockSpec((step, width), lambda i, s: (jnp.where(s[0] == want, first + i, 0), 0))

    return pl.pallas_call(
        lambda *refs: collect_kernel(scale, *refs),
        grid_spec=pltpu.PrefetchScalarGridSpec(
            num_scalar_prefetch=1,
            grid=(length // step,),
            in_specs=[block] * 3
            + [pick(0), pick(1)]
            + [
                pl.BlockSpec((step, 128), lambda i, s: (first + i, 0)),
                pl.BlockSpec((1, width), lambda i, s: (0, 0)),
            ],
            out_specs=[block, pl.BlockSpec((1, 1, width), lambda i, s: (i, 0, 0))],
        ),
        out_shape=[
            jax.ShapeDtypeStruct((length, width), BF16),
            jax.ShapeDtypeStruct((length // step, 1, width), F32),
        ],
        cost_estimate=cost(8 * length * width, 6),
        compiler_params=params(16),
        name="collect",
    )(at, *terms, local, here, inv_rms, gain)


def assemble_kernel(at, *refs):
    sums, moved, (dec, out) = refs[:PARTS], refs[PARTS:-2], refs[-2:]
    late = pl.program_id(0) >= pl.num_programs(0) // PARTS
    enc = [jnp.where(late, r[1][...], r[0][...]) for r in (sums, moved)]
    out[...] = jnp.where(at[3] == 1, dec[...], jnp.where(at[2] == 1, enc[1], enc[0]))


def assemble(at, sums, moved, dec):
    length, width = dec.shape
    step = 128
    each = length // step // PARTS

    def piece(part, row):
        def block(i, s):
            wanted = (s[3] == 0) & (s[2] == row)
            return (jnp.where(wanted, jnp.clip(i - part * each, 0, each - 1), 0), 0)

        return pl.BlockSpec((step, width), block)

    return pl.pallas_call(
        assemble_kernel,
        grid_spec=pltpu.PrefetchScalarGridSpec(
            num_scalar_prefetch=1,
            grid=(length // step,),
            in_specs=[piece(p, row) for row in range(2) for p in range(PARTS)]
            + [pl.BlockSpec((step, width), lambda i, s: (jnp.where(s[3] == 1, i, 0), 0))],
            out_specs=pl.BlockSpec((step, width), lambda i, s: (i, 0)),
        ),
        out_shape=jax.ShapeDtypeStruct((length, width), BF16),
        cost_estimate=cost(length * width, 4),
        compiler_params=params(14),
        name="assemble",
    )(at, *sums, *moved, dec)


def enc_grad_kernel(at, gkv_0, gkv_1, own_0, own_1, other_0, other_1, *outs):
    rows = own_0.shape[0]
    own = dot(gkv_0[...], own_0[...], NT) + dot(gkv_1[...], own_1[...], NT)
    other = dot(gkv_0[...], other_0[...], NT) + dot(gkv_1[...], other_1[...], NT)
    first = at[3] == 0
    left = jnp.where(first, own, other).astype(BF16)
    right = jnp.where(first, other, own).astype(BF16)
    for i, out in enumerate(outs):
        part = slice(i * out.shape[0], (i + 1) * out.shape[0])
        out[:, :rows] = left[part]
        out[:, rows:] = right[part]


def enc_grad(at, gkvs, owns, others, groups, rows, shard):
    length, cols = gkvs[0].shape
    per_shard = groups // 2

    def block(i, s):
        target = lax.rem(s[1] + shard, 2)
        group = target * per_shard + i // 2
        return (2 * group + lax.rem(i + s[2], 2), 0)

    gkv = pl.BlockSpec((length, cols), lambda i, s: (0, 0))
    weight = pl.BlockSpec((rows, cols), block)
    return pl.pallas_call(
        enc_grad_kernel,
        grid_spec=pltpu.PrefetchScalarGridSpec(
            num_scalar_prefetch=1,
            grid=(groups,),
            in_specs=[gkv, gkv, weight, weight, weight, weight],
            out_specs=[pl.BlockSpec((length // PARTS, 2 * rows), lambda i, s: (0, i))] * PARTS,
        ),
        out_shape=[pltpu.HBM((length // PARTS, D // 2), BF16)] * PARTS,
        compiler_params=params(12),
        cost_estimate=cost(4 * length * D * cols, 8),
        name="enc_grad",
    )(at, *in_hbm(*gkvs, *owns, *others))


def cut(array, axis, index, size):
    return lax.dynamic_slice_in_dim(array, index * size, size, axis)


def ordered(first, own, other, axis):
    return jnp.where(
        first, jnp.concatenate([own, other], axis), jnp.concatenate([other, own], axis)
    )


def after(value, *others):
    return lax.optimization_barrier((value,) + others)[0]


def on_device(sec_acts, gain, w_kv, src_len, tgt_len):
    groups = lax.axis_size("z")
    shards = lax.axis_size("mp")
    z, y = lax.axis_index("z"), lax.axis_index("y")
    core, x = lax.axis_index("phase"), lax.axis_index("mp")
    straight = y == core
    packed = sec_acts[0, 0]
    length, width = packed.shape
    rows = w_kv.shape[0]
    half = width // 2
    cols = half // CHUNKS
    pair_scale = 1.0 / (2 * groups)
    tiled = shards == 2 and rows % 128 == 0

    def turned(count, by):
        return [(i, (i + by) % count) for i in range(count)]

    def across(value, turn, moves):
        return lax.ppermute(
            value,
            ("y", "phase", "mp"),
            [(a * shards + s, b * shards + (s + turn) % shards) for a, b in moves for s in range(shards)],
        )

    def chunk_of(side, k):
        return lax.dynamic_slice_in_dim(w_kv, side * half + k * cols, cols, 1)

    def slots(block):
        return [lax.ppermute(block, "z", turned(groups, -s)) for s in range(1, groups)]

    swapped = [lax.ppermute(chunk_of(1 - y, 0), "y", SWAP)]
    here = lax.ppermute(packed, PLANE, [(2, 3)])
    gains = [gain] + [
        lax.ppermute(after(gain, here), "mp", turned(shards, t)) for t in range(1, shards)
    ]
    blocks = [jnp.concatenate([chunk_of(y, 0), swapped[0]], 0)]
    there = lax.ppermute(after(packed, blocks[0]), PLANE, [(0, 2), (2, 1)])
    key_count = jnp.where(straight, src_len, lax.ppermute(after(src_len, there), "y", SWAP))
    nears = [packed, here, there]
    fars = []
    for turn in range(1, shards):
        fars.append(
            [
                across(after(packed, *gains), turn, [(0, 0)]),
                across(here, turn, [(3, 3)]),
                across(there, turn, [(1, 1), (2, 2)]),
            ]
        )
    for k in range(1, CHUNKS):
        swapped.append(lax.ppermute(after(chunk_of(1 - y, k), there, fars[0][1]), "y", SWAP))
    blocks += [jnp.concatenate([chunk_of(y, k), swapped[k]], 0) for k in range(1, CHUNKS)]
    w_own, w_other = [], []

    position = lax.broadcasted_iota(jnp.int32, (length, width), 0)
    is_grad = lax.broadcasted_iota(jnp.int32, (length, width), 1) % (2 * HEAD) >= HEAD
    masked = jnp.where(is_grad & (position >= tgt_len[0]), jnp.zeros((), BF16), packed)
    qg_near, qg_far = cut(masked, 1, y, half), cut(masked, 1, 1 - y, half)
    qg_near, qg_far = lax.optimization_barrier((qg_near, qg_far, swapped[-1], key_count))[:2]
    qgs = [
        qg_near,
        lax.ppermute(qg_near, PLANE, [(1, 0)]),
        lax.ppermute(qg_far, PLANE, [(1, 2), (3, 1)]),
    ]
    enc_kind = jnp.where(straight, y, 2)
    qg_kind = jnp.where(straight, 1 - y, 2)
    at = jnp.concatenate(
        [jnp.stack([enc_kind, x, y, core]).astype(jnp.int32), key_count, qg_kind[None]]
    )

    def natural(parts, axis):
        if shards == 2:
            return ordered(x == 0, parts[0], parts[1], axis)
        stacked = jnp.stack(parts)
        return jnp.concatenate(
            [
                lax.dynamic_index_in_dim(stacked, (x - i) % shards, 0, keepdims=False)
                for i in range(shards)
            ],
            axis,
        )

    block_group = jnp.arange(groups)
    block_pair = 2 * block_group[:, None] + jnp.stack([y, 1 - y])[None, :]
    block_order = (2 * block_pair[None] + jnp.stack([core, 1 - core])[:, None, None]).reshape(-1)
    gain_all = natural(gains, 0).astype(F32)

    if tiled:
        enc_own, enc_other, inv_rms = norm(
            at, nears, fars[0], after(gain_all[None], *qgs, *blocks), groups, rows
        )
    else:
        raw = [chosen(enc_kind, *parts) for parts in [nears] + fars]
        hidden = natural(raw, 1).astype(F32)
        inv_rms = lax.rsqrt(jnp.sum(hidden * hidden, axis=-1, keepdims=True) / D + EPS)
        encoded = (hidden * inv_rms * gain_all).astype(BF16)
        encoded = encoded.reshape(length, -1, rows)[:, block_order].reshape(length, 2, -1)
        enc_own, enc_other = encoded[:, 0], encoded[:, 1]
    enc_mate = lax.ppermute(enc_other, "phase", SWAP)

    dec, gkvs, weight_sums = None, [], []
    for k in range(CHUNKS):
        if k in DIRECT:
            pieces = [blocks[k]] + slots(after(blocks[k], w_own[0]))
            pieces = lax.optimization_barrier((*pieces, grad))[:-1]
            gathered = jnp.zeros((groups * 2 * rows, cols), BF16)
            for turn, piece in enumerate(pieces):
                start = (z + turn) % groups * 2 * rows
                gathered = lax.dynamic_update_slice_in_dim(gathered, piece, start, 0)
            w_own.append(gathered)
        else:
            block = blocks[k]
            w_own.append(lax.all_gather(block, "z", axis=0, tiled=True))
            if k > 0:
                w_own[k] = after(w_own[k], grad)
        w_other.append(lax.ppermute(w_own[k], "phase", SWAP))
        dec, gkv = attend(at, dot(enc_own, w_own[k]), enc_other, w_other[k], qgs, k, dec)
        gkvs.append(gkv)
        last = k == CHUNKS - 1
        gkv_mate = lax.ppermute(gkv, "phase", SWAP)
        if tiled:
            if last:
                away = enc_grad(at, gkvs, w_own, w_other, groups, rows, 1)
                gkv_mate = after(gkv_mate, *away)
            grad = weight_grad(at, enc_own, enc_mate, gkv, gkv_mate, groups, pair_scale)
            if last:
                kept = [after(gkvs[0], grad)] + gkvs[1:]
                terms = [enc_grad(at, kept, w_own, w_other, groups, rows, 0), away]
        else:
            grad = pair_scale * (dot(enc_own, gkv, TN) + dot(enc_mate, gkv_mate, TN))
            grad = grad.astype(BF16)
        weight_sums.append(lax.psum_scatter(grad, "z", scatter_dimension=0, tiled=True))

    if not tiled:
        gkv_all = jnp.concatenate(gkvs, 1)
        full = dot(gkv_all, jnp.concatenate([jnp.concatenate(w, 0) for w in zip(w_own, w_other)], 1), NT)
        back = jnp.zeros_like(block_order).at[block_order].set(jnp.arange(block_order.shape[0]))
        full = full.astype(BF16).reshape(length, -1, rows)[:, back].reshape(length, D)
        terms = [jnp.split(cut(full, 1, (x + s) % shards, width), PARTS) for s in range(shards)]
    kept = jnp.concatenate([w[:rows] for w in weight_sums], 1)
    got = [lax.ppermute(w[rows:], "y", SWAP) for w in weight_sums]
    dec_here = jnp.where(y == 0, lax.ppermute(dec, PLANE, [(0, 1)]), dec)
    dec_there = lax.ppermute(dec, PLANE, [(2, 1), (1, 3)])
    dec_grads = ordered(y == 0, dec_here, dec_there, 1)

    far, first_far = [], None
    for part in range(PARTS):
        total = terms[0][part].astype(F32)
        for turn in range(1, shards):
            term = across(terms[turn][part], turn, [(1, 1), (2, 2)])
            first_far = term if first_far is None else first_far
            total = total + term.astype(F32)
        far.append(after(total.astype(BF16), dec_there))
    moved = [
        [across(after(part, first_far), turn, [(0, 0), (3, 3)]) for part in terms[turn]]
        for turn in range(1, shards)
    ]
    moved.append([lax.ppermute(part, PLANE, [(2, 0), (1, 3)]) for part in far])

    if tiled:
        grad_normed, gain_term = [], 0.0
        for part in range(PARTS):
            pieces = [t[part] for t in [terms[0]] + moved]
            if part > 0:
                pieces[1], grad_normed[-1], dec_grads, got[0] = lax.optimization_barrier(
                    (pieces[1], grad_normed[-1], dec_grads, got[0])
                )
            summed, term = collect(
                at, pieces, part, packed, here, inv_rms, gain.astype(F32)[None], pair_scale
            )
            grad_normed.append(summed)
            gain_term = gain_term + jnp.sum(term, axis=(0, 1))
    else:
        grad_enc = sum(jnp.concatenate(t, 0).astype(F32) for t in [terms[0]] + moved)
        grad_normed = jnp.split((grad_enc * gain.astype(F32)).astype(BF16), PARTS)
        normed = chosen(enc_kind, *nears).astype(F32) * inv_rms
        gain_term = pair_scale * jnp.sum(grad_enc * normed, axis=0)
    sent = [lax.ppermute(g, PLANE, [(3, 2)]) for g in grad_normed]
    if tiled:
        sec_grads = assemble(at, grad_normed, sent, dec_grads)[None, None]
    else:
        enc_grads = jnp.where(y == 0, jnp.concatenate(grad_normed, 0), jnp.concatenate(sent, 0))
        sec_grads = jnp.where(core == 0, enc_grads, dec_grads)[None, None]

    gain_term = jnp.where(straight, gain_term, 0.0)
    gain_term = gain_term + lax.ppermute(gain_term, PLANE, [(0, 3), (3, 0), (1, 2), (2, 1)])
    turn = 1
    while turn < groups:
        if 2 * turn == groups:
            gain_term, sec_grads = lax.optimization_barrier((gain_term, sec_grads))
        gain_term = gain_term + lax.ppermute(gain_term, "z", [(i, i ^ turn) for i in range(groups)])
        turn *= 2
    d_gain = jnp.where(straight, gain_term, lax.ppermute(gain_term, "phase", SWAP))
    got = jnp.concatenate(got, 1)
    d_wkv = ordered(y == 0, kept, got, 1).astype(F32)
    return (sec_grads, d_wkv, d_gain)


def solution(mesh):
    size = mesh.shape
    split = (size["dp"] // 2, 2, size["phase"], size["mp"])
    fine = Mesh(mesh.devices.reshape(split), ("z", "y", "phase", "mp"))
    pairs = ("z", "y")
    acts = P("phase", pairs, None, "mp")
    weights = P(("z", "y", "phase"), "mp")
    return jax.shard_map(
        on_device,
        mesh=fine,
        in_specs=(acts, P("mp"), weights, P(pairs), P(pairs)),
        out_specs=(acts, weights, P("mp")),
        check_vma=False,
    )
```

```python
import jax
import jax.numpy as jnp
from jax import lax
from jax.experimental import pallas as pl
from jax.experimental.pallas import tpu as pltpu
from jax.sharding import Mesh, PartitionSpec as P

D = 4096
HEAD = 64
EPS = 1e-06
CHUNKS = 2
PARTS = 2
DIRECT = ()
F32 = jnp.float32
BF16 = jnp.bfloat16
NN = (((1,), (0,)), ((), ()))
NT = (((1,), (1,)), ((), ()))
TN = (((0,), (0,)), ((), ()))

PLANE = ("y", "phase")
SWAP = [(0, 1), (1, 0)]


def dot(a, b, dims=NN):
    return lax.dot_general(a, b, dims, preferred_element_type=F32)


def cost(flops, mib, exps=0):
    return pl.CostEstimate(flops=flops, bytes_accessed=mib << 20, transcendentals=exps)


def in_hbm(*arrays):
    return [pltpu.with_memory_space_constraint(a, pltpu.HBM) for a in arrays]


def params(mib):
    return pltpu.CompilerParams(vmem_limit_bytes=mib << 20)


def chosen(kind, *values):
    return jnp.where(kind == 0, values[0], jnp.where(kind == 1, values[1], values[2]))


def norm_kernel(groups, rows, at, *refs):
    nears, fars, (gain, own, other, inv_out, natural) = refs[:3], refs[3:6], refs[6:]
    x, y, core = at[1], at[2], at[3]
    width = nears[0].shape[1]
    near = chosen(at[0], *[r[...] for r in nears]).astype(F32)
    far = chosen(at[0], *[r[...] for r in fars]).astype(F32)
    total = jnp.sum(near * near, axis=-1, keepdims=True) + jnp.sum(far * far, axis=-1, keepdims=True)
    inv_rms = lax.rsqrt(total / D + EPS)
    inv_out[...] = jnp.broadcast_to(inv_rms, inv_out.shape)
    near_at = pl.ds(pl.multiple_of(x * width, width), width)
    far_at = pl.ds(pl.multiple_of((1 - x) * width, width), width)
    natural[:, near_at] = (near * inv_rms * gain[:, near_at]).astype(BF16)
    natural[:, far_at] = (far * inv_rms * gain[:, far_at]).astype(BF16)
    for group in range(groups):
        for k in range(2):
            row = 2 * group + (y if k == 0 else 1 - y)
            put = slice((2 * group + k) * rows, (2 * group + k + 1) * rows)
            for out, half in ((own, core), (other, 1 - core)):
                got = pl.multiple_of((2 * row + half) * rows, rows)
                out[:, put] = natural[:, pl.ds(got, rows)]


def norm(at, nears, fars, gain, groups, rows):
    length, width = nears[0].shape
    step = 128

    def pick(want):
        return pl.BlockSpec((step, width), lambda i, s: (jnp.where(s[0] == want, i, 0), 0))

    out = pl.BlockSpec((step, D // 2), lambda i, s: (i, 0))
    return pl.pallas_call(
        lambda *refs: norm_kernel(groups, rows, *refs),
        grid_spec=pltpu.PrefetchScalarGridSpec(
            num_scalar_prefetch=1,
            grid=(length // step,),
            in_specs=[pick(i % 3) for i in range(6)] + [pl.BlockSpec((1, D), lambda i, s: (0, 0))],
            out_specs=[out, out, pl.BlockSpec((step, 128), lambda i, s: (i, 0))],
            scratch_shapes=[pltpu.VMEM((step, D), BF16)],
        ),
        out_shape=[pltpu.HBM((length, D // 2), BF16)] * 2
        + [jax.ShapeDtypeStruct((length, 128), F32)],
        compiler_params=params(14),
        cost_estimate=cost(8 * length * D, 8),
        name="norm",
    )(at, *nears, *fars, gain)


def attend_head(bias, qg, kv):
    low_lane = lax.broadcasted_iota(jnp.int32, qg.shape, 1) < HEAD
    zero = jnp.zeros((), BF16)
    scaled = qg * jnp.asarray(1.0 / HEAD**0.5, BF16)
    queries = jnp.where(low_lane, scaled, zero)
    grads = jnp.where(low_lane, zero, scaled)
    scores = dot(queries, kv, NT) + bias
    grad_prob = dot(grads, kv, NT)
    weights = jnp.exp(scores - jnp.max(scores, axis=-1, keepdims=True))
    probs = weights * (1.0 / jnp.sum(weights, axis=-1, keepdims=True))
    prob_low = probs.astype(BF16)
    row_delta = jnp.sum(prob_low.astype(F32) * grad_prob, axis=-1, keepdims=True)
    grad_score = (probs * (grad_prob - row_delta)).astype(BF16)
    grad_query = dot(grad_score, kv)
    qg_t = qg.T
    key_t = dot(qg_t[:HEAD], grad_score)
    value_t = dot(qg_t[HEAD:], prob_low)
    gkv = jnp.concatenate([key_t, value_t], axis=0).T
    dec = jnp.where(low_lane, grad_query, pltpu.roll(gkv, HEAD, 1))
    return dec.astype(BF16), gkv.astype(BF16)


def attend_kernel(at, part, enc_other, w_other, *refs):
    qgs, (dec, gkv) = refs[:3], refs[-2:]
    kv = (part[...] + dot(enc_other[...], w_other[...])).astype(BF16)
    keys = lax.broadcasted_iota(jnp.int32, (1, kv.shape[0]), 1)
    bias = jnp.where(keys < at[4], 0.0, -1e30).astype(F32)
    for head in range(kv.shape[1] // (2 * HEAD)):
        lanes = slice(head * 2 * HEAD, (head + 1) * 2 * HEAD)
        qg = chosen(at[5], *[r[:, lanes] for r in qgs])
        dec[:, lanes], gkv[:, lanes] = attend_head(bias, qg, kv[:, lanes])


def attend(at, part, enc_other, w_other, qgs, chunk, dec_before):
    length = part.shape[0]
    half, cols = w_other.shape
    step = min(256, cols)
    first = chunk * (cols // step)
    before = [] if dec_before is None else [dec_before]
    enc = pl.BlockSpec((length, half), lambda i, s: (0, 0))
    weight = pl.BlockSpec((half, step), lambda i, s: (0, i))
    out = pl.BlockSpec((length, step), lambda i, s: (0, i))

    def pick(want):
        return pl.BlockSpec((length, step), lambda i, s: (0, jnp.where(s[5] == want, first + i, first)))

    return pl.pallas_call(
        attend_kernel,
        grid_spec=pltpu.PrefetchScalarGridSpec(
            num_scalar_prefetch=1,
            grid=(cols // step,),
            in_specs=[out, enc, weight, pick(0), pick(1), pick(2)] + [pl.BlockSpec(memory_space=pl.ANY)] * len(before),
            out_specs=[pl.BlockSpec((length, step), lambda i, s: (0, first + i)), out],
        ),
        out_shape=[pltpu.HBM(qgs[0].shape, BF16), jax.ShapeDtypeStruct((length, cols), BF16)],
        input_output_aliases={7: 0} if before else {},
        compiler_params=params(26),
        cost_estimate=cost(
            length * cols * (4 * half + 14 * length), 8, length * length * cols // (2 * HEAD)
        ),
        name="attend",
    )(at, part, *in_hbm(enc_other, w_other, *qgs), *before)


def weight_grad_kernel(scale, at, enc_a, enc_b, gkv_a, gkv_b, out):
    grad = scale * (dot(enc_a[...], gkv_a[...], TN) + dot(enc_b[...], gkv_b[...], TN))
    out[...] = grad.astype(BF16)


def weight_grad(at, enc_a, enc_b, gkv_a, gkv_b, groups, scale):
    length, half = enc_a.shape
    cols = gkv_a.shape[1]
    step = half // groups
    enc = pl.BlockSpec((length, step), lambda i, s: (0, i))
    gkv = pl.BlockSpec((length, cols), lambda i, s: (0, 0))
    return pl.pallas_call(
        lambda *refs: weight_grad_kernel(scale, *refs),
        grid_spec=pltpu.PrefetchScalarGridSpec(
            num_scalar_prefetch=1,
            grid=(groups,),
            in_specs=[enc, enc, gkv, gkv],
            out_specs=pl.BlockSpec((step, cols), lambda i, s: (i, 0)),
        ),
        out_shape=pltpu.HBM((half, cols), BF16),
        cost_estimate=cost(4 * length * half * cols // 64, 0),
        compiler_params=params(12),
        name="weight_grad",
    )(at, *in_hbm(enc_a, enc_b), gkv_a, gkv_b)


def collect_kernel(scale, at, own, near, far, local, here, inv, gain, out, gain_term):
    total = own[...].astype(F32) + near[...].astype(F32) + far[...].astype(F32)
    out[...] = (total * gain[...]).astype(BF16)
    raw = jnp.where(at[0] == 0, local[...], here[...]).astype(F32)
    product = total * (raw * inv[:, :1])
    gain_term[0] = scale * jnp.sum(product, axis=0, keepdims=True)


def collect(at, terms, part, local, here, inv_rms, gain, scale):
    length, width = terms[0].shape
    step = 128
    first = part * (length // step)
    block = pl.BlockSpec((step, width), lambda i, s: (i, 0))

    def pick(want):
        return pl.BlockSpec((step, width), lambda i, s: (jnp.where(s[0] == want, first + i, 0), 0))

    return pl.pallas_call(
        lambda *refs: collect_kernel(scale, *refs),
        grid_spec=pltpu.PrefetchScalarGridSpec(
            num_scalar_prefetch=1,
            grid=(length // step,),
            in_specs=[block] * 3
            + [pick(0), pick(1)]
            + [
                pl.BlockSpec((step, 128), lambda i, s: (first + i, 0)),
                pl.BlockSpec((1, width), lambda i, s: (0, 0)),
            ],
            out_specs=[block, pl.BlockSpec((1, 1, width), lambda i, s: (i, 0, 0))],
        ),
        out_shape=[
            jax.ShapeDtypeStruct((length, width), BF16),
            jax.ShapeDtypeStruct((length // step, 1, width), F32),
        ],
        cost_estimate=cost(8 * length * width, 6),
        compiler_params=params(16),
        name="collect",
    )(at, *terms, local, here, inv_rms, gain)


def assemble_kernel(at, *refs):
    sums, moved, (dec, out) = refs[:PARTS], refs[PARTS:-2], refs[-2:]
    late = pl.program_id(0) >= pl.num_programs(0) // PARTS
    enc = [jnp.where(late, r[1][...], r[0][...]) for r in (sums, moved)]
    out[...] = jnp.where(at[3] == 1, dec[...], jnp.where(at[2] == 1, enc[1], enc[0]))


def assemble(at, sums, moved, dec):
    length, width = dec.shape
    step = 128
    each = length // step // PARTS

    def piece(part, row):
        def block(i, s):
            wanted = (s[3] == 0) & (s[2] == row)
            return (jnp.where(wanted, jnp.clip(i - part * each, 0, each - 1), 0), 0)

        return pl.BlockSpec((step, width), block)

    return pl.pallas_call(
        assemble_kernel,
        grid_spec=pltpu.PrefetchScalarGridSpec(
            num_scalar_prefetch=1,
            grid=(length // step,),
            in_specs=[piece(p, row) for row in range(2) for p in range(PARTS)]
            + [pl.BlockSpec((step, width), lambda i, s: (jnp.where(s[3] == 1, i, 0), 0))],
            out_specs=pl.BlockSpec((step, width), lambda i, s: (i, 0)),
        ),
        out_shape=jax.ShapeDtypeStruct((length, width), BF16),
        cost_estimate=cost(length * width, 4),
        compiler_params=params(14),
        name="assemble",
    )(at, *sums, *moved, *in_hbm(dec))


def enc_grad_kernel(at, gkv_0, gkv_1, own_0, own_1, other_0, other_1, *outs):
    rows = own_0.shape[0]
    own = dot(gkv_0[...], own_0[...], NT) + dot(gkv_1[...], own_1[...], NT)
    other = dot(gkv_0[...], other_0[...], NT) + dot(gkv_1[...], other_1[...], NT)
    first = at[3] == 0
    left = jnp.where(first, own, other).astype(BF16)
    right = jnp.where(first, other, own).astype(BF16)
    for i, out in enumerate(outs):
        part = slice(i * out.shape[0], (i + 1) * out.shape[0])
        out[:, :rows] = left[part]
        out[:, rows:] = right[part]


def enc_grad(at, gkvs, owns, others, groups, rows, shard):
    length, cols = gkvs[0].shape
    per_shard = groups // 2

    def block(i, s):
        target = lax.rem(s[1] + shard, 2)
        group = target * per_shard + i // 2
        return (2 * group + lax.rem(i + s[2], 2), 0)

    gkv = pl.BlockSpec((length, cols), lambda i, s: (0, 0))
    weight = pl.BlockSpec((rows, cols), block)
    return pl.pallas_call(
        enc_grad_kernel,
        grid_spec=pltpu.PrefetchScalarGridSpec(
            num_scalar_prefetch=1,
            grid=(groups,),
            in_specs=[gkv, gkv, weight, weight, weight, weight],
            out_specs=[pl.BlockSpec((length // PARTS, 2 * rows), lambda i, s: (0, i))] * PARTS,
        ),
        out_shape=[pltpu.HBM((length // PARTS, D // 2), BF16)] * PARTS,
        compiler_params=params(12),
        cost_estimate=cost(4 * length * D * cols, 8),
        name="enc_grad",
    )(at, *in_hbm(*gkvs, *owns, *others))


def cut(array, axis, index, size):
    return lax.dynamic_slice_in_dim(array, index * size, size, axis)


def ordered(first, own, other, axis):
    return jnp.where(
        first, jnp.concatenate([own, other], axis), jnp.concatenate([other, own], axis)
    )


def after(value, *others):
    return lax.optimization_barrier((value,) + others)[0]


def on_device(sec_acts, gain, w_kv, src_len, tgt_len):
    groups = lax.axis_size("z")
    shards = lax.axis_size("mp")
    z, y = lax.axis_index("z"), lax.axis_index("y")
    core, x = lax.axis_index("phase"), lax.axis_index("mp")
    straight = y == core
    packed = sec_acts[0, 0]
    length, width = packed.shape
    rows = w_kv.shape[0]
    half = width // 2
    cols = half // CHUNKS
    pair_scale = 1.0 / (2 * groups)
    tiled = shards == 2 and rows % 128 == 0

    def turned(count, by):
        return [(i, (i + by) % count) for i in range(count)]

    def across(value, turn, moves):
        return lax.ppermute(
            value,
            ("y", "phase", "mp"),
            [(a * shards + s, b * shards + (s + turn) % shards) for a, b in moves for s in range(shards)],
        )

    def chunk_of(side, k):
        return lax.dynamic_slice_in_dim(w_kv, side * half + k * cols, cols, 1)

    def slots(block):
        return [lax.ppermute(block, "z", turned(groups, -s)) for s in range(1, groups)]

    swapped = [lax.ppermute(chunk_of(1 - y, 0), "y", SWAP)]
    here = lax.ppermute(packed, PLANE, [(2, 3)])
    gains = [gain] + [
        lax.ppermute(after(gain, here), "mp", turned(shards, t)) for t in range(1, shards)
    ]
    blocks = [jnp.concatenate([chunk_of(y, 0), swapped[0]], 0)]
    there = lax.ppermute(after(packed, blocks[0]), PLANE, [(0, 2), (2, 1)])
    key_count = jnp.where(straight, src_len, lax.ppermute(after(src_len, there), "y", SWAP))
    nears = [packed, here, there]
    fars = []
    for turn in range(1, shards):
        fars.append(
            [
                across(after(packed, *gains), turn, [(0, 0)]),
                across(here, turn, [(3, 3)]),
                across(there, turn, [(1, 1), (2, 2)]),
            ]
        )
    for k in range(1, CHUNKS):
        swapped.append(lax.ppermute(after(chunk_of(1 - y, k), there, fars[0][1]), "y", SWAP))
    blocks += [jnp.concatenate([chunk_of(y, k), swapped[k]], 0) for k in range(1, CHUNKS)]
    w_own, w_other = [], []

    position = lax.broadcasted_iota(jnp.int32, (length, width), 0)
    is_grad = lax.broadcasted_iota(jnp.int32, (length, width), 1) % (2 * HEAD) >= HEAD
    masked = jnp.where(is_grad & (position >= tgt_len[0]), jnp.zeros((), BF16), packed)
    qg_near, qg_far = cut(masked, 1, y, half), cut(masked, 1, 1 - y, half)
    qg_near, qg_far = lax.optimization_barrier((qg_near, qg_far, swapped[-1], key_count))[:2]
    qgs = [
        qg_near,
        lax.ppermute(qg_near, PLANE, [(1, 0)]),
        lax.ppermute(qg_far, PLANE, [(1, 2), (3, 1)]),
    ]
    enc_kind = jnp.where(straight, y, 2)
    qg_kind = jnp.where(straight, 1 - y, 2)
    at = jnp.concatenate(
        [jnp.stack([enc_kind, x, y, core]).astype(jnp.int32), key_count, qg_kind[None]]
    )

    def natural(parts, axis):
        if shards == 2:
            return ordered(x == 0, parts[0], parts[1], axis)
        stacked = jnp.stack(parts)
        return jnp.concatenate(
            [
                lax.dynamic_index_in_dim(stacked, (x - i) % shards, 0, keepdims=False)
                for i in range(shards)
            ],
            axis,
        )

    block_group = jnp.arange(groups)
    block_pair = 2 * block_group[:, None] + jnp.stack([y, 1 - y])[None, :]
    block_order = (2 * block_pair[None] + jnp.stack([core, 1 - core])[:, None, None]).reshape(-1)
    gain_all = natural(gains, 0).astype(F32)

    if tiled:
        enc_own, enc_other, inv_rms = norm(
            at, nears, fars[0], after(gain_all[None], *qgs, *blocks), groups, rows
        )
    else:
        raw = [chosen(enc_kind, *parts) for parts in [nears] + fars]
        hidden = natural(raw, 1).astype(F32)
        inv_rms = lax.rsqrt(jnp.sum(hidden * hidden, axis=-1, keepdims=True) / D + EPS)
        encoded = (hidden * inv_rms * gain_all).astype(BF16)
        encoded = encoded.reshape(length, -1, rows)[:, block_order].reshape(length, 2, -1)
        enc_own, enc_other = encoded[:, 0], encoded[:, 1]
    enc_mate = lax.ppermute(enc_other, "phase", SWAP)

    dec, gkvs, weight_sums = None, [], []
    for k in range(CHUNKS):
        if k in DIRECT:
            pieces = [blocks[k]] + slots(after(blocks[k], w_own[0]))
            pieces = lax.optimization_barrier((*pieces, grad))[:-1]
            gathered = jnp.zeros((groups * 2 * rows, cols), BF16)
            for turn, piece in enumerate(pieces):
                start = (z + turn) % groups * 2 * rows
                gathered = lax.dynamic_update_slice_in_dim(gathered, piece, start, 0)
            w_own.append(gathered)
        else:
            block = blocks[k]
            w_own.append(lax.all_gather(block, "z", axis=0, tiled=True))
            if k > 0:
                w_own[k] = after(w_own[k], grad)
        w_other.append(lax.ppermute(w_own[k], "phase", SWAP))
        dec, gkv = attend(at, dot(enc_own, w_own[k]), enc_other, w_other[k], qgs, k, dec)
        gkvs.append(gkv)
        last = k == CHUNKS - 1
        gkv_mate = lax.ppermute(gkv, "phase", SWAP)
        if tiled:
            if last:
                away = enc_grad(at, gkvs, w_own, w_other, groups, rows, 1)
                gkv_mate = after(gkv_mate, *away)
            grad = weight_grad(at, enc_own, enc_mate, gkv, gkv_mate, groups, pair_scale)
            if last:
                kept = [after(gkvs[0], grad)] + gkvs[1:]
                terms = [enc_grad(at, kept, w_own, w_other, groups, rows, 0), away]
        else:
            grad = pair_scale * (dot(enc_own, gkv, TN) + dot(enc_mate, gkv_mate, TN))
            grad = grad.astype(BF16)
        weight_sums.append(lax.psum_scatter(grad, "z", scatter_dimension=0, tiled=True))

    if not tiled:
        gkv_all = jnp.concatenate(gkvs, 1)
        full = dot(gkv_all, jnp.concatenate([jnp.concatenate(w, 0) for w in zip(w_own, w_other)], 1), NT)
        back = jnp.zeros_like(block_order).at[block_order].set(jnp.arange(block_order.shape[0]))
        full = full.astype(BF16).reshape(length, -1, rows)[:, back].reshape(length, D)
        terms = [jnp.split(cut(full, 1, (x + s) % shards, width), PARTS) for s in range(shards)]
    kept = jnp.concatenate([w[:rows] for w in weight_sums], 1)
    got = [lax.ppermute(w[rows:], "y", SWAP) for w in weight_sums]
    dec_here = jnp.where(y == 0, lax.ppermute(dec, PLANE, [(0, 1)]), dec)
    dec_there = lax.ppermute(dec, PLANE, [(2, 1), (1, 3)])
    dec_grads = ordered(y == 0, dec_here, dec_there, 1)

    far, first_far = [], None
    for part in range(PARTS):
        total = terms[0][part].astype(F32)
        for turn in range(1, shards):
            term = across(terms[turn][part], turn, [(1, 1), (2, 2)])
            first_far = term if first_far is None else first_far
            total = total + term.astype(F32)
        done = dec_there if part == 0 else got[0]
        far.append(after(total.astype(BF16), done))
    moved = [
        [across(after(part, first_far), turn, [(0, 0), (3, 3)]) for part in terms[turn]]
        for turn in range(1, shards)
    ]
    moved.append([lax.ppermute(part, PLANE, [(2, 0), (1, 3)]) for part in far])

    if tiled:
        grad_normed, gain_term = [], 0.0
        for part in range(PARTS):
            pieces = [t[part] for t in [terms[0]] + moved]
            if part > 0:
                pieces[1], grad_normed[-1], dec_grads = lax.optimization_barrier(
                    (pieces[1], grad_normed[-1], dec_grads)
                )
            summed, term = collect(
                at, pieces, part, packed, here, inv_rms, gain.astype(F32)[None], pair_scale
            )
            grad_normed.append(summed)
            gain_term = gain_term + jnp.sum(term, axis=(0, 1))
    else:
        grad_enc = sum(jnp.concatenate(t, 0).astype(F32) for t in [terms[0]] + moved)
        grad_normed = jnp.split((grad_enc * gain.astype(F32)).astype(BF16), PARTS)
        normed = chosen(enc_kind, *nears).astype(F32) * inv_rms
        gain_term = pair_scale * jnp.sum(grad_enc * normed, axis=0)
    sent = [lax.ppermute(g, PLANE, [(3, 2)]) for g in grad_normed]
    if tiled:
        sec_grads = assemble(at, grad_normed, sent, dec_grads)[None, None]
    else:
        enc_grads = jnp.where(y == 0, jnp.concatenate(grad_normed, 0), jnp.concatenate(sent, 0))
        sec_grads = jnp.where(core == 0, enc_grads, dec_grads)[None, None]

    gain_term = jnp.where(straight, gain_term, 0.0)
    gain_term = gain_term + lax.ppermute(gain_term, PLANE, [(0, 3), (3, 0), (1, 2), (2, 1)])
    turn = 1
    while turn < groups:
        if 2 * turn == groups:
            gain_term, sec_grads = lax.optimization_barrier((gain_term, sec_grads))
        gain_term = gain_term + lax.ppermute(gain_term, "z", [(i, i ^ turn) for i in range(groups)])
        turn *= 2
    d_gain = jnp.where(straight, gain_term, lax.ppermute(gain_term, "phase", SWAP))
    got = jnp.concatenate(got, 1)
    d_wkv = ordered(y == 0, kept, got, 1).astype(F32)
    return (sec_grads, d_wkv, d_gain)


def solution(mesh):
    size = mesh.shape
    split = (size["dp"] // 2, 2, size["phase"], size["mp"])
    fine = Mesh(mesh.devices.reshape(split), ("z", "y", "phase", "mp"))
    pairs = ("z", "y")
    acts = P("phase", pairs, None, "mp")
    weights = P(("z", "y", "phase"), "mp")
    return jax.shard_map(
        on_device,
        mesh=fine,
        in_specs=(acts, P("mp"), weights, P(pairs), P(pairs)),
        out_specs=(acts, weights, P("mp")),
        check_vma=False,
    )
```

```python
import jax
import jax.numpy as jnp
from jax import lax
from jax.experimental import pallas as pl
from jax.experimental.pallas import tpu as pltpu
from jax.sharding import Mesh, PartitionSpec as P

D = 4096
HEAD = 64
EPS = 1e-06
CHUNKS = 2
PARTS = 2
DIRECT = ()
F32 = jnp.float32
BF16 = jnp.bfloat16
NN = (((1,), (0,)), ((), ()))
NT = (((1,), (1,)), ((), ()))
TN = (((0,), (0,)), ((), ()))

PLANE = ("y", "phase")
SWAP = [(0, 1), (1, 0)]


def dot(a, b, dims=NN):
    return lax.dot_general(a, b, dims, preferred_element_type=F32)


def cost(flops, mib, exps=0):
    return pl.CostEstimate(flops=flops, bytes_accessed=mib << 20, transcendentals=exps)


def in_hbm(*arrays):
    return [pltpu.with_memory_space_constraint(a, pltpu.HBM) for a in arrays]


def params(mib):
    return pltpu.CompilerParams(vmem_limit_bytes=mib << 20)


def chosen(kind, *values):
    return jnp.where(kind == 0, values[0], jnp.where(kind == 1, values[1], values[2]))


def norm_kernel(groups, rows, at, *refs):
    nears, fars, (gain, own, other, inv_out, natural) = refs[:3], refs[3:6], refs[6:]
    x, y, core = at[1], at[2], at[3]
    width = nears[0].shape[1]
    near = chosen(at[0], *[r[...] for r in nears]).astype(F32)
    far = chosen(at[0], *[r[...] for r in fars]).astype(F32)
    total = jnp.sum(near * near, axis=-1, keepdims=True) + jnp.sum(far * far, axis=-1, keepdims=True)
    inv_rms = lax.rsqrt(total / D + EPS)
    inv_out[...] = jnp.broadcast_to(inv_rms, inv_out.shape)
    near_at = pl.ds(pl.multiple_of(x * width, width), width)
    far_at = pl.ds(pl.multiple_of((1 - x) * width, width), width)
    natural[:, near_at] = (near * inv_rms * gain[:, near_at]).astype(BF16)
    natural[:, far_at] = (far * inv_rms * gain[:, far_at]).astype(BF16)
    for group in range(groups):
        for k in range(2):
            row = 2 * group + (y if k == 0 else 1 - y)
            put = slice((2 * group + k) * rows, (2 * group + k + 1) * rows)
            for out, half in ((own, core), (other, 1 - core)):
                got = pl.multiple_of((2 * row + half) * rows, rows)
                out[:, put] = natural[:, pl.ds(got, rows)]


def norm(at, nears, fars, gain, groups, rows):
    length, width = nears[0].shape
    step = 128

    def pick(want):
        return pl.BlockSpec((step, width), lambda i, s: (jnp.where(s[0] == want, i, 0), 0))

    out = pl.BlockSpec((step, D // 2), lambda i, s: (i, 0))
    return pl.pallas_call(
        lambda *refs: norm_kernel(groups, rows, *refs),
        grid_spec=pltpu.PrefetchScalarGridSpec(
            num_scalar_prefetch=1,
            grid=(length // step,),
            in_specs=[pick(i % 3) for i in range(6)] + [pl.BlockSpec((1, D), lambda i, s: (0, 0))],
            out_specs=[out, out, pl.BlockSpec((step, 128), lambda i, s: (i, 0))],
            scratch_shapes=[pltpu.VMEM((step, D), BF16)],
        ),
        out_shape=[pltpu.HBM((length, D // 2), BF16)] * 2
        + [jax.ShapeDtypeStruct((length, 128), F32)],
        compiler_params=params(14),
        cost_estimate=cost(8 * length * D, 8),
        name="norm",
    )(at, *nears, *fars, gain)


def attend_head(bias, qg, kv):
    low_lane = lax.broadcasted_iota(jnp.int32, qg.shape, 1) < HEAD
    zero = jnp.zeros((), BF16)
    scaled = qg * jnp.asarray(1.0 / HEAD**0.5, BF16)
    queries = jnp.where(low_lane, scaled, zero)
    grads = jnp.where(low_lane, zero, scaled)
    scores = dot(queries, kv, NT) + bias
    grad_prob = dot(grads, kv, NT)
    weights = jnp.exp(scores - jnp.max(scores, axis=-1, keepdims=True))
    probs = weights * (1.0 / jnp.sum(weights, axis=-1, keepdims=True))
    prob_low = probs.astype(BF16)
    row_delta = jnp.sum(prob_low.astype(F32) * grad_prob, axis=-1, keepdims=True)
    grad_score = (probs * (grad_prob - row_delta)).astype(BF16)
    grad_query = dot(grad_score, kv)
    qg_t = qg.T
    key_t = dot(qg_t[:HEAD], grad_score)
    value_t = dot(qg_t[HEAD:], prob_low)
    gkv = jnp.concatenate([key_t, value_t], axis=0).T
    dec = jnp.where(low_lane, grad_query, pltpu.roll(gkv, HEAD, 1))
    return dec.astype(BF16), gkv.astype(BF16)


def attend_kernel(at, part, enc_other, w_other, *refs):
    qgs, (dec, gkv) = refs[:3], refs[-2:]
    kv = (part[...] + dot(enc_other[...], w_other[...])).astype(BF16)
    keys = lax.broadcasted_iota(jnp.int32, (1, kv.shape[0]), 1)
    bias = jnp.where(keys < at[4], 0.0, -1e30).astype(F32)
    for head in range(kv.shape[1] // (2 * HEAD)):
        lanes = slice(head * 2 * HEAD, (head + 1) * 2 * HEAD)
        qg = chosen(at[5], *[r[:, lanes] for r in qgs])
        dec[:, lanes], gkv[:, lanes] = attend_head(bias, qg, kv[:, lanes])


def attend(at, part, enc_other, w_other, qgs, chunk, dec_before):
    length = part.shape[0]
    half, cols = w_other.shape
    step = min(256, cols)
    first = chunk * (cols // step)
    before = [] if dec_before is None else [dec_before]
    enc = pl.BlockSpec((length, half), lambda i, s: (0, 0))
    weight = pl.BlockSpec((half, step), lambda i, s: (0, i))
    out = pl.BlockSpec((length, step), lambda i, s: (0, i))

    def pick(want):
        return pl.BlockSpec((length, step), lambda i, s: (0, jnp.where(s[5] == want, first + i, first)))

    return pl.pallas_call(
        attend_kernel,
        grid_spec=pltpu.PrefetchScalarGridSpec(
            num_scalar_prefetch=1,
            grid=(cols // step,),
            in_specs=[out, enc, weight, pick(0), pick(1), pick(2)] + [pl.BlockSpec(memory_space=pl.ANY)] * len(before),
            out_specs=[pl.BlockSpec((length, step), lambda i, s: (0, first + i)), out],
        ),
        out_shape=[pltpu.HBM(qgs[0].shape, BF16), jax.ShapeDtypeStruct((length, cols), BF16)],
        input_output_aliases={7: 0} if before else {},
        compiler_params=params(26),
        cost_estimate=cost(
            length * cols * (4 * half + 14 * length), 8, length * length * cols // (2 * HEAD)
        ),
        name="attend",
    )(at, part, *in_hbm(enc_other, w_other, *qgs), *before)


def weight_grad_kernel(scale, at, enc_a, enc_b, gkv_a, gkv_b, out):
    grad = scale * (dot(enc_a[...], gkv_a[...], TN) + dot(enc_b[...], gkv_b[...], TN))
    out[...] = grad.astype(BF16)


def weight_grad(at, enc_a, enc_b, gkv_a, gkv_b, groups, scale):
    length, half = enc_a.shape
    cols = gkv_a.shape[1]
    step = half // groups
    enc = pl.BlockSpec((length, step), lambda i, s: (0, i))
    gkv = pl.BlockSpec((length, cols), lambda i, s: (0, 0))
    return pl.pallas_call(
        lambda *refs: weight_grad_kernel(scale, *refs),
        grid_spec=pltpu.PrefetchScalarGridSpec(
            num_scalar_prefetch=1,
            grid=(groups,),
            in_specs=[enc, enc, gkv, gkv],
            out_specs=pl.BlockSpec((step, cols), lambda i, s: (i, 0)),
        ),
        out_shape=pltpu.HBM((half, cols), BF16),
        cost_estimate=cost(4 * length * half * cols // 64, 0),
        compiler_params=params(12),
        name="weight_grad",
    )(at, *in_hbm(enc_a, enc_b), gkv_a, gkv_b)


def collect_kernel(scale, at, own, near, far, local, here, inv, gain, out, gain_term):
    total = own[...].astype(F32) + near[...].astype(F32) + far[...].astype(F32)
    out[...] = (total * gain[...]).astype(BF16)
    raw = jnp.where(at[0] == 0, local[...], here[...]).astype(F32)
    product = total * (raw * inv[:, :1])
    gain_term[0] = scale * jnp.sum(product, axis=0, keepdims=True)


def collect(at, terms, part, local, here, inv_rms, gain, scale):
    length, width = terms[0].shape
    step = 128
    first = part * (length // step)
    block = pl.BlockSpec((step, width), lambda i, s: (i, 0))

    def pick(want):
        return pl.BlockSpec((step, width), lambda i, s: (jnp.where(s[0] == want, first + i, 0), 0))

    return pl.pallas_call(
        lambda *refs: collect_kernel(scale, *refs),
        grid_spec=pltpu.PrefetchScalarGridSpec(
            num_scalar_prefetch=1,
            grid=(length // step,),
            in_specs=[block] * 3
            + [pick(0), pick(1)]
            + [
                pl.BlockSpec((step, 128), lambda i, s: (first + i, 0)),
                pl.BlockSpec((1, width), lambda i, s: (0, 0)),
            ],
            out_specs=[block, pl.BlockSpec((1, 1, width), lambda i, s: (i, 0, 0))],
        ),
        out_shape=[
            jax.ShapeDtypeStruct((length, width), BF16),
            jax.ShapeDtypeStruct((length // step, 1, width), F32),
        ],
        cost_estimate=cost(8 * length * width, 6),
        compiler_params=params(16),
        name="collect",
    )(at, *terms, local, here, inv_rms, gain)


def assemble_kernel(at, *refs):
    sums, moved, (dec, out) = refs[:PARTS], refs[PARTS:-2], refs[-2:]
    late = pl.program_id(0) >= pl.num_programs(0) // PARTS
    enc = [jnp.where(late, r[1][...], r[0][...]) for r in (sums, moved)]
    out[...] = jnp.where(at[3] == 1, dec[...], jnp.where(at[2] == 1, enc[1], enc[0]))


def assemble(at, sums, moved, dec):
    length, width = dec.shape
    step = 128
    each = length // step // PARTS

    def piece(part, row):
        def block(i, s):
            wanted = (s[3] == 0) & (s[2] == row)
            return (jnp.where(wanted, jnp.clip(i - part * each, 0, each - 1), 0), 0)

        return pl.BlockSpec((step, width), block)

    return pl.pallas_call(
        assemble_kernel,
        grid_spec=pltpu.PrefetchScalarGridSpec(
            num_scalar_prefetch=1,
            grid=(length // step,),
            in_specs=[piece(p, row) for row in range(2) for p in range(PARTS)]
            + [pl.BlockSpec((step, width), lambda i, s: (jnp.where(s[3] == 1, i, 0), 0))],
            out_specs=pl.BlockSpec((step, width), lambda i, s: (i, 0)),
        ),
        out_shape=jax.ShapeDtypeStruct((length, width), BF16),
        cost_estimate=cost(length * width, 4),
        compiler_params=params(14),
        name="assemble",
    )(at, *sums, *moved, *in_hbm(dec))


def enc_grad_kernel(at, gkv_0, gkv_1, own_0, own_1, other_0, other_1, *outs):
    rows = own_0.shape[0]
    own = dot(gkv_0[...], own_0[...], NT) + dot(gkv_1[...], own_1[...], NT)
    other = dot(gkv_0[...], other_0[...], NT) + dot(gkv_1[...], other_1[...], NT)
    first = at[3] == 0
    left = jnp.where(first, own, other).astype(BF16)
    right = jnp.where(first, other, own).astype(BF16)
    for i, out in enumerate(outs):
        part = slice(i * out.shape[0], (i + 1) * out.shape[0])
        out[:, :rows] = left[part]
        out[:, rows:] = right[part]


def enc_grad(at, gkvs, owns, others, groups, rows, shard):
    length, cols = gkvs[0].shape
    per_shard = groups // 2

    def block(i, s):
        target = lax.rem(s[1] + shard, 2)
        group = target * per_shard + i // 2
        return (2 * group + lax.rem(i + s[2], 2), 0)

    gkv = pl.BlockSpec((length, cols), lambda i, s: (0, 0))
    weight = pl.BlockSpec((rows, cols), block)
    return pl.pallas_call(
        enc_grad_kernel,
        grid_spec=pltpu.PrefetchScalarGridSpec(
            num_scalar_prefetch=1,
            grid=(groups,),
            in_specs=[gkv, gkv, weight, weight, weight, weight],
            out_specs=[pl.BlockSpec((length // PARTS, 2 * rows), lambda i, s: (0, i))] * PARTS,
        ),
        out_shape=[pltpu.HBM((length // PARTS, D // 2), BF16)] * PARTS,
        compiler_params=params(12),
        cost_estimate=cost(4 * length * D * cols, 8),
        name="enc_grad",
    )(at, *in_hbm(*gkvs, *owns, *others))


def cut(array, axis, index, size):
    return lax.dynamic_slice_in_dim(array, index * size, size, axis)


def ordered(first, own, other, axis):
    return jnp.where(
        first, jnp.concatenate([own, other], axis), jnp.concatenate([other, own], axis)
    )


def after(value, *others):
    return lax.optimization_barrier((value,) + others)[0]


def on_device(sec_acts, gain, w_kv, src_len, tgt_len):
    groups = lax.axis_size("z")
    shards = lax.axis_size("mp")
    z, y = lax.axis_index("z"), lax.axis_index("y")
    core, x = lax.axis_index("phase"), lax.axis_index("mp")
    straight = y == core
    packed = sec_acts[0, 0]
    length, width = packed.shape
    rows = w_kv.shape[0]
    half = width // 2
    cols = half // CHUNKS
    pair_scale = 1.0 / (2 * groups)
    tiled = shards == 2 and rows % 128 == 0

    def turned(count, by):
        return [(i, (i + by) % count) for i in range(count)]

    def across(value, turn, moves):
        return lax.ppermute(
            value,
            ("y", "phase", "mp"),
            [(a * shards + s, b * shards + (s + turn) % shards) for a, b in moves for s in range(shards)],
        )

    def chunk_of(side, k):
        return lax.dynamic_slice_in_dim(w_kv, side * half + k * cols, cols, 1)

    def slots(block):
        return [lax.ppermute(block, "z", turned(groups, -s)) for s in range(1, groups)]

    swapped = [lax.ppermute(chunk_of(1 - y, 0), "y", SWAP)]
    here = lax.ppermute(packed, PLANE, [(2, 3)])
    gains = [gain] + [
        lax.ppermute(after(gain, here), "mp", turned(shards, t)) for t in range(1, shards)
    ]
    blocks = [jnp.concatenate([chunk_of(y, 0), swapped[0]], 0)]
    there = lax.ppermute(after(packed, blocks[0]), PLANE, [(0, 2), (2, 1)])
    key_count = jnp.where(straight, src_len, lax.ppermute(after(src_len, there), "y", SWAP))
    nears = [packed, here, there]
    fars = []
    for turn in range(1, shards):
        fars.append(
            [
                across(after(packed, *gains), turn, [(0, 0)]),
                across(here, turn, [(3, 3)]),
                across(there, turn, [(1, 1), (2, 2)]),
            ]
        )
    for k in range(1, CHUNKS):
        swapped.append(lax.ppermute(after(chunk_of(1 - y, k), there, fars[0][1]), "y", SWAP))
    blocks += [jnp.concatenate([chunk_of(y, k), swapped[k]], 0) for k in range(1, CHUNKS)]
    w_own, w_other = [], []

    position = lax.broadcasted_iota(jnp.int32, (length, width), 0)
    is_grad = lax.broadcasted_iota(jnp.int32, (length, width), 1) % (2 * HEAD) >= HEAD
    masked = jnp.where(is_grad & (position >= tgt_len[0]), jnp.zeros((), BF16), packed)
    qg_near, qg_far = cut(masked, 1, y, half), cut(masked, 1, 1 - y, half)
    qg_near, qg_far = lax.optimization_barrier((qg_near, qg_far, swapped[-1], key_count))[:2]
    qgs = [
        qg_near,
        lax.ppermute(qg_near, PLANE, [(1, 0)]),
        lax.ppermute(qg_far, PLANE, [(1, 2), (3, 1)]),
    ]
    enc_kind = jnp.where(straight, y, 2)
    qg_kind = jnp.where(straight, 1 - y, 2)
    at = jnp.concatenate(
        [jnp.stack([enc_kind, x, y, core]).astype(jnp.int32), key_count, qg_kind[None]]
    )

    def natural(parts, axis):
        if shards == 2:
            return ordered(x == 0, parts[0], parts[1], axis)
        stacked = jnp.stack(parts)
        return jnp.concatenate(
            [
                lax.dynamic_index_in_dim(stacked, (x - i) % shards, 0, keepdims=False)
                for i in range(shards)
            ],
            axis,
        )

    block_group = jnp.arange(groups)
    block_pair = 2 * block_group[:, None] + jnp.stack([y, 1 - y])[None, :]
    block_order = (2 * block_pair[None] + jnp.stack([core, 1 - core])[:, None, None]).reshape(-1)
    gain_all = natural(gains, 0).astype(F32)

    if tiled:
        enc_own, enc_other, inv_rms = norm(
            at, nears, fars[0], after(gain_all[None], *qgs, *blocks), groups, rows
        )
    else:
        raw = [chosen(enc_kind, *parts) for parts in [nears] + fars]
        hidden = natural(raw, 1).astype(F32)
        inv_rms = lax.rsqrt(jnp.sum(hidden * hidden, axis=-1, keepdims=True) / D + EPS)
        encoded = (hidden * inv_rms * gain_all).astype(BF16)
        encoded = encoded.reshape(length, -1, rows)[:, block_order].reshape(length, 2, -1)
        enc_own, enc_other = encoded[:, 0], encoded[:, 1]
    enc_mate = lax.ppermute(enc_other, "phase", SWAP)

    dec, gkvs, weight_sums = None, [], []
    for k in range(CHUNKS):
        if k in DIRECT:
            pieces = [blocks[k]] + slots(after(blocks[k], w_own[0]))
            pieces = lax.optimization_barrier((*pieces, grad))[:-1]
            gathered = jnp.zeros((groups * 2 * rows, cols), BF16)
            for turn, piece in enumerate(pieces):
                start = (z + turn) % groups * 2 * rows
                gathered = lax.dynamic_update_slice_in_dim(gathered, piece, start, 0)
            w_own.append(gathered)
        else:
            block = blocks[k]
            w_own.append(lax.all_gather(block, "z", axis=0, tiled=True))
            if k > 0:
                w_own[k] = after(w_own[k], grad)
        w_other.append(lax.ppermute(w_own[k], "phase", SWAP))
        dec, gkv = attend(at, dot(enc_own, w_own[k]), enc_other, w_other[k], qgs, k, dec)
        gkvs.append(gkv)
        last = k == CHUNKS - 1
        gkv_mate = lax.ppermute(gkv, "phase", SWAP)
        if tiled:
            if last:
                away = enc_grad(at, gkvs, w_own, w_other, groups, rows, 1)
                gkv_mate = after(gkv_mate, *away)
            grad = weight_grad(at, enc_own, enc_mate, gkv, gkv_mate, groups, pair_scale)
            if last:
                kept = [after(gkvs[0], grad)] + gkvs[1:]
                terms = [enc_grad(at, kept, w_own, w_other, groups, rows, 0), away]
        else:
            grad = pair_scale * (dot(enc_own, gkv, TN) + dot(enc_mate, gkv_mate, TN))
            grad = grad.astype(BF16)
        weight_sums.append(lax.psum_scatter(grad, "z", scatter_dimension=0, tiled=True))

    if not tiled:
        gkv_all = jnp.concatenate(gkvs, 1)
        full = dot(gkv_all, jnp.concatenate([jnp.concatenate(w, 0) for w in zip(w_own, w_other)], 1), NT)
        back = jnp.zeros_like(block_order).at[block_order].set(jnp.arange(block_order.shape[0]))
        full = full.astype(BF16).reshape(length, -1, rows)[:, back].reshape(length, D)
        terms = [jnp.split(cut(full, 1, (x + s) % shards, width), PARTS) for s in range(shards)]
    kept = jnp.concatenate([w[:rows] for w in weight_sums], 1)
    got = lax.ppermute(jnp.concatenate([w[rows:] for w in weight_sums], 1), "y", SWAP)
    dec_here = jnp.where(y == 0, lax.ppermute(dec, PLANE, [(0, 1)]), dec)
    dec_there = lax.ppermute(dec, PLANE, [(2, 1), (1, 3)])
    dec_grads = ordered(y == 0, dec_here, dec_there, 1)

    far, first_far = [], None
    for part in range(PARTS):
        total = terms[0][part].astype(F32)
        for turn in range(1, shards):
            term = across(terms[turn][part], turn, [(1, 1), (2, 2)])
            first_far = term if first_far is None else first_far
            total = total + term.astype(F32)
        far.append(after(total.astype(BF16), dec_there))
    moved = [
        [across(after(part, first_far), turn, [(0, 0), (3, 3)]) for part in terms[turn]]
        for turn in range(1, shards)
    ]
    moved.append([lax.ppermute(part, PLANE, [(2, 0), (1, 3)]) for part in far])

    if tiled:
        grad_normed, gain_term = [], 0.0
        for part in range(PARTS):
            pieces = [t[part] for t in [terms[0]] + moved]
            if part > 0:
                pieces[1], grad_normed[-1], dec_grads = lax.optimization_barrier(
                    (pieces[1], grad_normed[-1], dec_grads)
                )
            summed, term = collect(
                at, pieces, part, packed, here, inv_rms, gain.astype(F32)[None], pair_scale
            )
            grad_normed.append(summed)
            gain_term = gain_term + jnp.sum(term, axis=(0, 1))
    else:
        grad_enc = sum(jnp.concatenate(t, 0).astype(F32) for t in [terms[0]] + moved)
        grad_normed = jnp.split((grad_enc * gain.astype(F32)).astype(BF16), PARTS)
        normed = chosen(enc_kind, *nears).astype(F32) * inv_rms
        gain_term = pair_scale * jnp.sum(grad_enc * normed, axis=0)
    sent = [lax.ppermute(g, PLANE, [(3, 2)]) for g in grad_normed]
    gain_term = jnp.where(straight, gain_term, 0.0)
    gain_term = gain_term + lax.ppermute(gain_term, PLANE, [(0, 3), (3, 0), (1, 2), (2, 1)])
    turn = 1
    while turn < groups:
        gain_term = gain_term + lax.ppermute(gain_term, "z", [(i, i ^ turn) for i in range(groups)])
        turn *= 2
    if tiled:
        sent[0] = after(sent[0], gain_term)
        sec_grads = assemble(at, grad_normed, sent, dec_grads)[None, None]
    else:
        enc_grads = jnp.where(y == 0, jnp.concatenate(grad_normed, 0), jnp.concatenate(sent, 0))
        sec_grads = jnp.where(core == 0, enc_grads, dec_grads)[None, None]

    d_gain = jnp.where(straight, gain_term, lax.ppermute(gain_term, "phase", SWAP))
    d_wkv = ordered(y == 0, kept, got, 1).astype(F32)
    return (sec_grads, d_wkv, d_gain)


def solution(mesh):
    size = mesh.shape
    split = (size["dp"] // 2, 2, size["phase"], size["mp"])
    fine = Mesh(mesh.devices.reshape(split), ("z", "y", "phase", "mp"))
    pairs = ("z", "y")
    acts = P("phase", pairs, None, "mp")
    weights = P(("z", "y", "phase"), "mp")
    return jax.shard_map(
        on_device,
        mesh=fine,
        in_specs=(acts, P("mp"), weights, P(pairs), P(pairs)),
        out_specs=(acts, weights, P("mp")),
        check_vma=False,
    )
```

```python
import jax
import jax.numpy as jnp
from jax import lax
from jax.experimental import pallas as pl
from jax.experimental.pallas import tpu as pltpu
from jax.sharding import Mesh, PartitionSpec as P

D = 4096
HEAD = 64
EPS = 1e-06
CHUNKS = 2
PARTS = 2
DIRECT = ()
F32 = jnp.float32
BF16 = jnp.bfloat16
NN = (((1,), (0,)), ((), ()))
NT = (((1,), (1,)), ((), ()))
TN = (((0,), (0,)), ((), ()))

PLANE = ("y", "phase")
SWAP = [(0, 1), (1, 0)]


def dot(a, b, dims=NN):
    return lax.dot_general(a, b, dims, preferred_element_type=F32)


def cost(flops, mib, exps=0):
    return pl.CostEstimate(flops=flops, bytes_accessed=mib << 20, transcendentals=exps)


def in_hbm(*arrays):
    return [pltpu.with_memory_space_constraint(a, pltpu.HBM) for a in arrays]


def params(mib):
    return pltpu.CompilerParams(vmem_limit_bytes=mib << 20)


def chosen(kind, *values):
    return jnp.where(kind == 0, values[0], jnp.where(kind == 1, values[1], values[2]))


def norm_kernel(groups, rows, at, *refs):
    nears, fars, (gain, own, other, inv_out, natural) = refs[:3], refs[3:6], refs[6:]
    x, y, core = at[1], at[2], at[3]
    width = nears[0].shape[1]
    near = chosen(at[0], *[r[...] for r in nears]).astype(F32)
    far = chosen(at[0], *[r[...] for r in fars]).astype(F32)
    total = jnp.sum(near * near, axis=-1, keepdims=True) + jnp.sum(far * far, axis=-1, keepdims=True)
    inv_rms = lax.rsqrt(total / D + EPS)
    inv_out[...] = jnp.broadcast_to(inv_rms, inv_out.shape)
    near_at = pl.ds(pl.multiple_of(x * width, width), width)
    far_at = pl.ds(pl.multiple_of((1 - x) * width, width), width)
    natural[:, near_at] = (near * inv_rms * gain[:, near_at]).astype(BF16)
    natural[:, far_at] = (far * inv_rms * gain[:, far_at]).astype(BF16)
    for group in range(groups):
        for k in range(2):
            row = 2 * group + (y if k == 0 else 1 - y)
            put = slice((2 * group + k) * rows, (2 * group + k + 1) * rows)
            for out, half in ((own, core), (other, 1 - core)):
                got = pl.multiple_of((2 * row + half) * rows, rows)
                out[:, put] = natural[:, pl.ds(got, rows)]


def norm(at, nears, fars, gain, groups, rows):
    length, width = nears[0].shape
    step = 128

    def pick(want):
        return pl.BlockSpec((step, width), lambda i, s: (jnp.where(s[0] == want, i, 0), 0))

    out = pl.BlockSpec((step, D // 2), lambda i, s: (i, 0))
    return pl.pallas_call(
        lambda *refs: norm_kernel(groups, rows, *refs),
        grid_spec=pltpu.PrefetchScalarGridSpec(
            num_scalar_prefetch=1,
            grid=(length // step,),
            in_specs=[pick(i % 3) for i in range(6)] + [pl.BlockSpec((1, D), lambda i, s: (0, 0))],
            out_specs=[out, out, pl.BlockSpec((step, 128), lambda i, s: (i, 0))],
            scratch_shapes=[pltpu.VMEM((step, D), BF16)],
        ),
        out_shape=[pltpu.HBM((length, D // 2), BF16)] * 2
        + [jax.ShapeDtypeStruct((length, 128), F32)],
        compiler_params=params(14),
        cost_estimate=cost(8 * length * D, 8),
        name="norm",
    )(at, *nears, *fars, gain)


def attend_head(bias, qg, kv):
    low_lane = lax.broadcasted_iota(jnp.int32, qg.shape, 1) < HEAD
    zero = jnp.zeros((), BF16)
    scaled = qg * jnp.asarray(1.0 / HEAD**0.5, BF16)
    queries = jnp.where(low_lane, scaled, zero)
    grads = jnp.where(low_lane, zero, scaled)
    scores = dot(queries, kv, NT) + bias
    grad_prob = dot(grads, kv, NT)
    weights = jnp.exp(scores - jnp.max(scores, axis=-1, keepdims=True))
    probs = weights * (1.0 / jnp.sum(weights, axis=-1, keepdims=True))
    prob_low = probs.astype(BF16)
    row_delta = jnp.sum(prob_low.astype(F32) * grad_prob, axis=-1, keepdims=True)
    grad_score = (probs * (grad_prob - row_delta)).astype(BF16)
    grad_query = dot(grad_score, kv)
    qg_t = qg.T
    key_t = dot(qg_t[:HEAD], grad_score)
    value_t = dot(qg_t[HEAD:], prob_low)
    gkv = jnp.concatenate([key_t, value_t], axis=0).T
    dec = jnp.where(low_lane, grad_query, pltpu.roll(gkv, HEAD, 1))
    return dec.astype(BF16), gkv.astype(BF16)


def attend_kernel(at, part, enc_other, w_other, *refs):
    qgs, (dec, gkv) = refs[:3], refs[-2:]
    kv = (part[...] + dot(enc_other[...], w_other[...])).astype(BF16)
    keys = lax.broadcasted_iota(jnp.int32, (1, kv.shape[0]), 1)
    bias = jnp.where(keys < at[4], 0.0, -1e30).astype(F32)
    for head in range(kv.shape[1] // (2 * HEAD)):
        lanes = slice(head * 2 * HEAD, (head + 1) * 2 * HEAD)
        qg = chosen(at[5], *[r[:, lanes] for r in qgs])
        dec[:, lanes], gkv[:, lanes] = attend_head(bias, qg, kv[:, lanes])


def attend(at, part, enc_other, w_other, qgs, chunk, dec_before):
    length = part.shape[0]
    half, cols = w_other.shape
    step = min(256, cols)
    first = chunk * (cols // step)
    before = [] if dec_before is None else [dec_before]
    enc = pl.BlockSpec((length, half), lambda i, s: (0, 0))
    weight = pl.BlockSpec((half, step), lambda i, s: (0, i))
    out = pl.BlockSpec((length, step), lambda i, s: (0, i))

    def pick(want):
        return pl.BlockSpec((length, step), lambda i, s: (0, jnp.where(s[5] == want, first + i, first)))

    return pl.pallas_call(
        attend_kernel,
        grid_spec=pltpu.PrefetchScalarGridSpec(
            num_scalar_prefetch=1,
            grid=(cols // step,),
            in_specs=[out, enc, weight, pick(0), pick(1), pick(2)] + [pl.BlockSpec(memory_space=pl.ANY)] * len(before),
            out_specs=[pl.BlockSpec((length, step), lambda i, s: (0, first + i)), out],
        ),
        out_shape=[pltpu.HBM(qgs[0].shape, BF16), jax.ShapeDtypeStruct((length, cols), BF16)],
        input_output_aliases={7: 0} if before else {},
        compiler_params=params(26),
        cost_estimate=cost(
            length * cols * (4 * half + 14 * length), 8, length * length * cols // (2 * HEAD)
        ),
        name="attend",
    )(at, part, *in_hbm(enc_other, w_other, *qgs), *before)


def weight_grad_kernel(scale, at, enc_a, enc_b, gkv_a, gkv_b, out):
    grad = scale * (dot(enc_a[...], gkv_a[...], TN) + dot(enc_b[...], gkv_b[...], TN))
    out[...] = grad.astype(BF16)


def weight_grad(at, enc_a, enc_b, gkv_a, gkv_b, groups, scale):
    length, half = enc_a.shape
    cols = gkv_a.shape[1]
    step = half // groups
    enc = pl.BlockSpec((length, step), lambda i, s: (0, i))
    gkv = pl.BlockSpec((length, cols), lambda i, s: (0, 0))
    return pl.pallas_call(
        lambda *refs: weight_grad_kernel(scale, *refs),
        grid_spec=pltpu.PrefetchScalarGridSpec(
            num_scalar_prefetch=1,
            grid=(groups,),
            in_specs=[enc, enc, gkv, gkv],
            out_specs=pl.BlockSpec((step, cols), lambda i, s: (i, 0)),
        ),
        out_shape=pltpu.HBM((half, cols), BF16),
        cost_estimate=cost(4 * length * half * cols // 64, 0),
        compiler_params=params(12),
        name="weight_grad",
    )(at, *in_hbm(enc_a, enc_b), gkv_a, gkv_b)


def collect_kernel(scale, at, own, near, far, local, here, inv, gain, out, gain_term):
    total = own[...].astype(F32) + near[...].astype(F32) + far[...].astype(F32)
    out[...] = (total * gain[...]).astype(BF16)
    raw = jnp.where(at[0] == 0, local[...], here[...]).astype(F32)
    product = total * (raw * inv[:, :1])
    gain_term[0] = scale * jnp.sum(product, axis=0, keepdims=True)


def collect(at, terms, part, local, here, inv_rms, gain, scale):
    length, width = terms[0].shape
    step = 128
    first = part * (length // step)
    block = pl.BlockSpec((step, width), lambda i, s: (i, 0))

    def pick(want):
        return pl.BlockSpec((step, width), lambda i, s: (jnp.where(s[0] == want, first + i, 0), 0))

    return pl.pallas_call(
        lambda *refs: collect_kernel(scale, *refs),
        grid_spec=pltpu.PrefetchScalarGridSpec(
            num_scalar_prefetch=1,
            grid=(length // step,),
            in_specs=[block] * 3
            + [pick(0), pick(1)]
            + [
                pl.BlockSpec((step, 128), lambda i, s: (first + i, 0)),
                pl.BlockSpec((1, width), lambda i, s: (0, 0)),
            ],
            out_specs=[block, pl.BlockSpec((1, 1, width), lambda i, s: (i, 0, 0))],
        ),
        out_shape=[
            jax.ShapeDtypeStruct((length, width), BF16),
            jax.ShapeDtypeStruct((length // step, 1, width), F32),
        ],
        cost_estimate=cost(8 * length * width, 6),
        compiler_params=params(16),
        name="collect",
    )(at, *terms, local, here, inv_rms, gain)


def assemble_kernel(at, *refs):
    sums, moved, (dec, out) = refs[:PARTS], refs[PARTS:-2], refs[-2:]
    late = pl.program_id(0) >= pl.num_programs(0) // PARTS
    enc = [jnp.where(late, r[1][...], r[0][...]) for r in (sums, moved)]
    out[...] = jnp.where(at[3] == 1, dec[...], jnp.where(at[2] == 1, enc[1], enc[0]))


def assemble(at, sums, moved, dec):
    length, width = dec.shape
    step = 256
    each = length // step // PARTS

    def piece(part, row):
        def block(i, s):
            wanted = (s[3] == 0) & (s[2] == row)
            return (jnp.where(wanted, jnp.clip(i - part * each, 0, each - 1), 0), 0)

        return pl.BlockSpec((step, width), block)

    return pl.pallas_call(
        assemble_kernel,
        grid_spec=pltpu.PrefetchScalarGridSpec(
            num_scalar_prefetch=1,
            grid=(length // step,),
            in_specs=[piece(p, row) for row in range(2) for p in range(PARTS)]
            + [pl.BlockSpec((step, width), lambda i, s: (jnp.where(s[3] == 1, i, 0), 0))],
            out_specs=pl.BlockSpec((step, width), lambda i, s: (i, 0)),
        ),
        out_shape=jax.ShapeDtypeStruct((length, width), BF16),
        cost_estimate=cost(length * width, 4),
        compiler_params=params(24),
        name="assemble",
    )(at, *sums, *moved, *in_hbm(dec))


def enc_grad_kernel(at, gkv_0, gkv_1, own_0, own_1, other_0, other_1, *outs):
    rows = own_0.shape[0]
    own = dot(gkv_0[...], own_0[...], NT) + dot(gkv_1[...], own_1[...], NT)
    other = dot(gkv_0[...], other_0[...], NT) + dot(gkv_1[...], other_1[...], NT)
    first = at[3] == 0
    left = jnp.where(first, own, other).astype(BF16)
    right = jnp.where(first, other, own).astype(BF16)
    for i, out in enumerate(outs):
        part = slice(i * out.shape[0], (i + 1) * out.shape[0])
        out[:, :rows] = left[part]
        out[:, rows:] = right[part]


def enc_grad(at, gkvs, owns, others, groups, rows, shard):
    length, cols = gkvs[0].shape
    per_shard = groups // 2

    def block(i, s):
        target = lax.rem(s[1] + shard, 2)
        group = target * per_shard + i // 2
        return (2 * group + lax.rem(i + s[2], 2), 0)

    gkv = pl.BlockSpec((length, cols), lambda i, s: (0, 0))
    weight = pl.BlockSpec((rows, cols), block)
    return pl.pallas_call(
        enc_grad_kernel,
        grid_spec=pltpu.PrefetchScalarGridSpec(
            num_scalar_prefetch=1,
            grid=(groups,),
            in_specs=[gkv, gkv, weight, weight, weight, weight],
            out_specs=[pl.BlockSpec((length // PARTS, 2 * rows), lambda i, s: (0, i))] * PARTS,
        ),
        out_shape=[pltpu.HBM((length // PARTS, D // 2), BF16)] * PARTS,
        compiler_params=params(12),
        cost_estimate=cost(4 * length * D * cols, 8),
        name="enc_grad",
    )(at, *in_hbm(*gkvs, *owns, *others))


def cut(array, axis, index, size):
    return lax.dynamic_slice_in_dim(array, index * size, size, axis)


def ordered(first, own, other, axis):
    return jnp.where(
        first, jnp.concatenate([own, other], axis), jnp.concatenate([other, own], axis)
    )


def after(value, *others):
    return lax.optimization_barrier((value,) + others)[0]


def on_device(sec_acts, gain, w_kv, src_len, tgt_len):
    groups = lax.axis_size("z")
    shards = lax.axis_size("mp")
    z, y = lax.axis_index("z"), lax.axis_index("y")
    core, x = lax.axis_index("phase"), lax.axis_index("mp")
    straight = y == core
    packed = sec_acts[0, 0]
    length, width = packed.shape
    rows = w_kv.shape[0]
    half = width // 2
    cols = half // CHUNKS
    pair_scale = 1.0 / (2 * groups)
    tiled = shards == 2 and rows % 128 == 0

    def turned(count, by):
        return [(i, (i + by) % count) for i in range(count)]

    def across(value, turn, moves):
        return lax.ppermute(
            value,
            ("y", "phase", "mp"),
            [(a * shards + s, b * shards + (s + turn) % shards) for a, b in moves for s in range(shards)],
        )

    def chunk_of(side, k):
        return lax.dynamic_slice_in_dim(w_kv, side * half + k * cols, cols, 1)

    def slots(block):
        return [lax.ppermute(block, "z", turned(groups, -s)) for s in range(1, groups)]

    swapped = [lax.ppermute(chunk_of(1 - y, 0), "y", SWAP)]
    here = lax.ppermute(packed, PLANE, [(2, 3)])
    gains = [gain] + [
        lax.ppermute(after(gain, here), "mp", turned(shards, t)) for t in range(1, shards)
    ]
    blocks = [jnp.concatenate([chunk_of(y, 0), swapped[0]], 0)]
    there = lax.ppermute(after(packed, blocks[0]), PLANE, [(0, 2), (2, 1)])
    key_count = jnp.where(straight, src_len, lax.ppermute(after(src_len, there), "y", SWAP))
    nears = [packed, here, there]
    fars = []
    for turn in range(1, shards):
        fars.append(
            [
                across(after(packed, *gains), turn, [(0, 0)]),
                across(here, turn, [(3, 3)]),
                across(there, turn, [(1, 1), (2, 2)]),
            ]
        )
    for k in range(1, CHUNKS):
        swapped.append(lax.ppermute(after(chunk_of(1 - y, k), there, fars[0][1]), "y", SWAP))
    blocks += [jnp.concatenate([chunk_of(y, k), swapped[k]], 0) for k in range(1, CHUNKS)]
    w_own, w_other = [], []

    position = lax.broadcasted_iota(jnp.int32, (length, width), 0)
    is_grad = lax.broadcasted_iota(jnp.int32, (length, width), 1) % (2 * HEAD) >= HEAD
    masked = jnp.where(is_grad & (position >= tgt_len[0]), jnp.zeros((), BF16), packed)
    qg_near, qg_far = cut(masked, 1, y, half), cut(masked, 1, 1 - y, half)
    qg_near, qg_far = lax.optimization_barrier((qg_near, qg_far, swapped[-1], key_count))[:2]
    qgs = [
        qg_near,
        lax.ppermute(qg_near, PLANE, [(1, 0)]),
        lax.ppermute(qg_far, PLANE, [(1, 2), (3, 1)]),
    ]
    enc_kind = jnp.where(straight, y, 2)
    qg_kind = jnp.where(straight, 1 - y, 2)
    at = jnp.concatenate(
        [jnp.stack([enc_kind, x, y, core]).astype(jnp.int32), key_count, qg_kind[None]]
    )

    def natural(parts, axis):
        if shards == 2:
            return ordered(x == 0, parts[0], parts[1], axis)
        stacked = jnp.stack(parts)
        return jnp.concatenate(
            [
                lax.dynamic_index_in_dim(stacked, (x - i) % shards, 0, keepdims=False)
                for i in range(shards)
            ],
            axis,
        )

    block_group = jnp.arange(groups)
    block_pair = 2 * block_group[:, None] + jnp.stack([y, 1 - y])[None, :]
    block_order = (2 * block_pair[None] + jnp.stack([core, 1 - core])[:, None, None]).reshape(-1)
    gain_all = natural(gains, 0).astype(F32)

    if tiled:
        enc_own, enc_other, inv_rms = norm(
            at, nears, fars[0], after(gain_all[None], *qgs, *blocks), groups, rows
        )
    else:
        raw = [chosen(enc_kind, *parts) for parts in [nears] + fars]
        hidden = natural(raw, 1).astype(F32)
        inv_rms = lax.rsqrt(jnp.sum(hidden * hidden, axis=-1, keepdims=True) / D + EPS)
        encoded = (hidden * inv_rms * gain_all).astype(BF16)
        encoded = encoded.reshape(length, -1, rows)[:, block_order].reshape(length, 2, -1)
        enc_own, enc_other = encoded[:, 0], encoded[:, 1]
    enc_mate = lax.ppermute(enc_other, "phase", SWAP)

    dec, gkvs, weight_sums = None, [], []
    for k in range(CHUNKS):
        if k in DIRECT:
            pieces = [blocks[k]] + slots(after(blocks[k], w_own[0]))
            pieces = lax.optimization_barrier((*pieces, grad))[:-1]
            gathered = jnp.zeros((groups * 2 * rows, cols), BF16)
            for turn, piece in enumerate(pieces):
                start = (z + turn) % groups * 2 * rows
                gathered = lax.dynamic_update_slice_in_dim(gathered, piece, start, 0)
            w_own.append(gathered)
        else:
            block = blocks[k]
            w_own.append(lax.all_gather(block, "z", axis=0, tiled=True))
            if k > 0:
                w_own[k] = after(w_own[k], grad)
        w_other.append(lax.ppermute(w_own[k], "phase", SWAP))
        dec, gkv = attend(at, dot(enc_own, w_own[k]), enc_other, w_other[k], qgs, k, dec)
        gkvs.append(gkv)
        last = k == CHUNKS - 1
        gkv_mate = lax.ppermute(gkv, "phase", SWAP)
        if tiled:
            if last:
                away = enc_grad(at, gkvs, w_own, w_other, groups, rows, 1)
                gkv_mate = after(gkv_mate, *away)
            grad = weight_grad(at, enc_own, enc_mate, gkv, gkv_mate, groups, pair_scale)
            if last:
                kept = [after(gkvs[0], grad)] + gkvs[1:]
                terms = [enc_grad(at, kept, w_own, w_other, groups, rows, 0), away]
        else:
            grad = pair_scale * (dot(enc_own, gkv, TN) + dot(enc_mate, gkv_mate, TN))
            grad = grad.astype(BF16)
        weight_sums.append(lax.psum_scatter(grad, "z", scatter_dimension=0, tiled=True))

    if not tiled:
        gkv_all = jnp.concatenate(gkvs, 1)
        full = dot(gkv_all, jnp.concatenate([jnp.concatenate(w, 0) for w in zip(w_own, w_other)], 1), NT)
        back = jnp.zeros_like(block_order).at[block_order].set(jnp.arange(block_order.shape[0]))
        full = full.astype(BF16).reshape(length, -1, rows)[:, back].reshape(length, D)
        terms = [jnp.split(cut(full, 1, (x + s) % shards, width), PARTS) for s in range(shards)]
    kept = jnp.concatenate([w[:rows] for w in weight_sums], 1)
    got = [lax.ppermute(w[rows:], "y", SWAP) for w in weight_sums]
    dec_here = jnp.where(y == 0, lax.ppermute(dec, PLANE, [(0, 1)]), dec)
    dec_there = lax.ppermute(dec, PLANE, [(2, 1), (1, 3)])
    dec_grads = ordered(y == 0, dec_here, dec_there, 1)

    far, first_far = [], None
    for part in range(PARTS):
        total = terms[0][part].astype(F32)
        for turn in range(1, shards):
            term = across(terms[turn][part], turn, [(1, 1), (2, 2)])
            first_far = term if first_far is None else first_far
            total = total + term.astype(F32)
        done = dec_there if part == 0 else got[0]
        far.append(after(total.astype(BF16), done))
    moved = [
        [across(after(part, first_far), turn, [(0, 0), (3, 3)]) for part in terms[turn]]
        for turn in range(1, shards)
    ]
    moved.append([lax.ppermute(part, PLANE, [(2, 0), (1, 3)]) for part in far])

    if tiled:
        grad_normed, gain_term = [], 0.0
        for part in range(PARTS):
            pieces = [t[part] for t in [terms[0]] + moved]
            if part > 0:
                pieces[1], grad_normed[-1], dec_grads = lax.optimization_barrier(
                    (pieces[1], grad_normed[-1], dec_grads)
                )
            summed, term = collect(
                at, pieces, part, packed, here, inv_rms, gain.astype(F32)[None], pair_scale
            )
            grad_normed.append(summed)
            gain_term = gain_term + jnp.sum(term, axis=(0, 1))
    else:
        grad_enc = sum(jnp.concatenate(t, 0).astype(F32) for t in [terms[0]] + moved)
        grad_normed = jnp.split((grad_enc * gain.astype(F32)).astype(BF16), PARTS)
        normed = chosen(enc_kind, *nears).astype(F32) * inv_rms
        gain_term = pair_scale * jnp.sum(grad_enc * normed, axis=0)
    sent = [lax.ppermute(g, PLANE, [(3, 2)]) for g in grad_normed]
    if tiled:
        sec_grads = assemble(at, grad_normed, sent, dec_grads)[None, None]
    else:
        enc_grads = jnp.where(y == 0, jnp.concatenate(grad_normed, 0), jnp.concatenate(sent, 0))
        sec_grads = jnp.where(core == 0, enc_grads, dec_grads)[None, None]

    gain_term = jnp.where(straight, gain_term, 0.0)
    gain_term = gain_term + lax.ppermute(gain_term, PLANE, [(0, 3), (3, 0), (1, 2), (2, 1)])
    turn = 1
    while turn < groups:
        if 2 * turn == groups:
            gain_term, sec_grads = lax.optimization_barrier((gain_term, sec_grads))
        gain_term = gain_term + lax.ppermute(gain_term, "z", [(i, i ^ turn) for i in range(groups)])
        turn *= 2
    d_gain = jnp.where(straight, gain_term, lax.ppermute(gain_term, "phase", SWAP))
    got = jnp.concatenate(got, 1)
    d_wkv = ordered(y == 0, kept, got, 1).astype(F32)
    return (sec_grads, d_wkv, d_gain)


def solution(mesh):
    size = mesh.shape
    split = (size["dp"] // 2, 2, size["phase"], size["mp"])
    fine = Mesh(mesh.devices.reshape(split), ("z", "y", "phase", "mp"))
    pairs = ("z", "y")
    acts = P("phase", pairs, None, "mp")
    weights = P(("z", "y", "phase"), "mp")
    return jax.shard_map(
        on_device,
        mesh=fine,
        in_specs=(acts, P("mp"), weights, P(pairs), P(pairs)),
        out_specs=(acts, weights, P("mp")),
        check_vma=False,
    )
```
